128 devices in a mesh: section: 2 (over x_hi), dp: 8 (over y, core), tensor: 8 (over x_lo, z).
Axes of the slice: x: 4 (x_hi: 2, x_lo: 2; x = x_hi * 2 + x_lo), y: 4, z: 4, core: 2. Of those that a mesh axis runs over, the one named last changes fastest.
Arguments:
- inputs: float32 [2, 8, 768, 1024], P(None, 'dp', None, 'tensor'), may hold values from -6 to 6
- cotangent: float32 [2, 8, 768, 1024], P(None, 'dp', None, 'tensor'), may hold values from -6 to 6
- packed_weight: bfloat16 [2, 1024, 3, 1024], P('section', 'dp', None, 'tensor'), may hold values from -0.1875 to 0.1875
- bias_pair: bfloat16 [2, 2, 1024], P('section', None, ('tensor', 'dp')), may hold values from -3 to 3
- output_weight: bfloat16 [2, 1024, 1024], P('section', 'tensor', 'dp'), may hold values from -1 to 1
- output_bias: bfloat16 [2, 1024], P('section', ('tensor', 'dp')), may hold values from -3 to 3
- expand_weight: bfloat16 [2, 1024, 4096], P('section', 'dp', 'tensor'), may hold values from -0.1875 to 0.1875
- expand_bias: bfloat16 [2, 4096], P('section', ('tensor', 'dp')), may hold values from -3 to 3
- contract_weight: bfloat16 [2, 4096, 1024], P('section', 'tensor', 'dp'), may hold values from -0.09375 to 0.09375
- contract_bias: bfloat16 [2, 1024], P('section', ('tensor', 'dp')), may hold values from -3 to 3
- gain_first: bfloat16 [2, 1024], P('section', ('tensor', 'dp')), may hold values from 0.25 to 1.75
- shift_first: bfloat16 [2, 1024], P('section', ('tensor', 'dp')), may hold values from -3 to 3
- gain_second: bfloat16 [2, 1024], P('section', ('tensor', 'dp')), may hold values from 0.25 to 1.75
- shift_second: bfloat16 [2, 1024], P('section', ('tensor', 'dp')), may hold values from -3 to 3
Outputs:
- section_outputs: float32 [2, 2, 8, 768, 1024], P('section', None, 'dp', None, 'tensor')
- section_grads: float32 [2, 2, 8, 768, 1024], P('section', None, 'dp', None, 'tensor')
- packed_weight_grad: float32 [2, 1024, 3, 1024], P('section', 'dp', None, 'tensor')
- bias_pair_grad: float32 [2, 2, 1024], P('section', None, ('tensor', 'dp'))
- output_weight_grad: float32 [2, 1024, 1024], P('section', 'tensor', 'dp')
- output_bias_grad: float32 [2, 1024], P('section', ('tensor', 'dp'))
- expand_weight_grad: float32 [2, 1024, 4096], P('section', 'dp', 'tensor')
- expand_bias_grad: float32 [2, 4096], P('section', ('tensor', 'dp'))
- contract_weight_grad: float32 [2, 4096, 1024], P('section', 'tensor', 'dp')
- contract_bias_grad: float32 [2, 1024], P('section', ('tensor', 'dp'))
- gain_first_grad: float32 [2, 1024], P('section', ('tensor', 'dp'))
- shift_first_grad: float32 [2, 1024], P('section', ('tensor', 'dp'))
- gain_second_grad: float32 [2, 1024], P('section', ('tensor', 'dp'))
- shift_second_grad: float32 [2, 1024], P('section', ('tensor', 'dp'))
The draws below stay inside these ranges and needn't reach their ends.
All inputs are finite; a program needn't handle non-finite values.
Results may differ from the reference program's by a relative error of at most 0.025.
Values may be sent and summed in bfloat16 or wider, within the bound.
No kernel may reach another device: no remote copies, remote signals or barrier semaphores. Data moves between devices by JAX's collectives and lax.ppermute only.
A program may use at most 192 MiB of HBM per device.

```python
import math
import jax
import jax.numpy as jnp
from jax import lax

D = 1024
HEADS = 16
HEAD_DIM = 64
FF = 4096
SEQ_LEN = 768
MICRO = 2
BATCH = 8
LAYERS = 2


def level_of(own_key, shape, pieces, low, top_value):
    level = 1.0
    for axis_at, blocks in pieces:
        steps = jax.random.uniform(jax.random.fold_in(jax.random.fold_in(own_key, 6), axis_at), (blocks,), jnp.float32, low / len(pieces), top_value / len(pieces))
        level = level * jnp.repeat(jnp.exp(steps), shape[axis_at] // blocks).reshape((-1,) + (1,) * (len(shape) - 1 - axis_at))
    return level


def centred(rng, shape, spread, reach, cuts=(), kind=jnp.bfloat16):
    level = level_of(rng, shape, cuts, -0.22, 0.18) if cuts else 1.0
    drawn = jax.random.normal(rng, shape, jnp.float32) * spread * level
    return jnp.minimum(jnp.maximum(drawn, -reach), reach).astype(kind)


def setup_inputs(seed: int = 0) -> dict:
    keys = jax.random.split(jax.random.key(seed), 15)
    return {
        "inputs": centred(keys[0], (MICRO, BATCH, SEQ_LEN, D), 1.0, 6.0, ((1, 8), (3, 8)), jnp.float32),
        "cotangent": centred(keys[1], (MICRO, BATCH, SEQ_LEN, D), 1.0, 6.0, ((1, 8), (3, 8)), jnp.float32),
        "packed_weight": centred(keys[2], (LAYERS, D, 3, D), D ** -0.5, 0.1875, ((0, 2), (1, 8), (3, 8))),
        "bias_pair": centred(keys[3], (LAYERS, 2, D), 0.5, 3.0, ((0, 2), (2, 64))),
        "output_weight": centred(keys[4], (LAYERS, D, D), (D * 32 // SEQ_LEN) ** -0.5, 1.0, ((0, 2), (1, 8), (2, 8))),
        "output_bias": centred(keys[5], (LAYERS, D), 0.5, 3.0, ((0, 2), (1, 64))),
        "expand_weight": centred(keys[6], (LAYERS, D, FF), D ** -0.5, 0.1875, ((0, 2), (1, 8), (2, 8))),
        "expand_bias": centred(keys[7], (LAYERS, FF), 0.5, 3.0, ((0, 2), (1, 64))),
        "contract_weight": centred(keys[8], (LAYERS, FF, D), FF ** -0.5, 0.09375, ((0, 2), (1, 8), (2, 8))),
        "contract_bias": centred(keys[9], (LAYERS, D), 0.5, 3.0, ((0, 2), (1, 64))),
        "gain_first": jnp.clip(1.0 + 0.15 * jax.random.normal(keys[10], (LAYERS, D), jnp.float32), 0.25, 1.75).astype(jnp.bfloat16),
        "shift_first": centred(keys[11], (LAYERS, D), 0.5, 3.0, ((0, 2), (1, 64))),
        "gain_second": jnp.clip(1.0 + 0.15 * jax.random.normal(keys[12], (LAYERS, D), jnp.float32), 0.25, 1.75).astype(jnp.bfloat16),
        "shift_second": centred(keys[13], (LAYERS, D), 0.5, 3.0, ((0, 2), (1, 64))),
    }


@jax.custom_vjp
def low(v):
    return lax.optimization_barrier(v.astype(jnp.bfloat16)).astype(jnp.float32)

@jax.custom_vjp
def low_back(v):
    return v

def low_keep(v):
    return (low(v), None)

def low_pass(kept, grad):
    return (grad,)

def back_keep(v):
    return (v, None)

def back_low(kept, grad):
    return (low(grad),)
low.defvjp(low_keep, low_pass)
low_back.defvjp(back_keep, back_low)
epsilon = 1e-05
gelu_coef = math.sqrt(2.0 / math.pi)
precise = lax.Precision.HIGHEST

def gelu_tanh(values):
    return 0.5 * values * (1.0 + jnp.tanh(gelu_coef * (values + 0.044715 * values * values * values)))

def layer_norm(stream, gain, offset):
    mean_row = lax.optimization_barrier(jnp.mean(stream, axis=-1, keepdims=True))
    var_row = lax.optimization_barrier(jnp.mean(stream * stream, axis=-1, keepdims=True)) - mean_row * mean_row
    return (stream - mean_row) * lax.rsqrt(var_row + epsilon) * gain + offset

def layer(stream, params):
    packed_weight, bias_pair, output_weight, output_bias, expand_weight, expand_bias, contract_weight, contract_bias, gain_first, shift_first, gain_second, shift_second = params
    length = stream.shape[0]
    normed_one = low(layer_norm(stream, gain_first, shift_first))
    packed = jnp.einsum('nd,dcf->ncf', normed_one, packed_weight, precision=precise)
    queries = low_back(low(packed[:, 0] + bias_pair[0])).reshape(length, HEADS, HEAD_DIM)
    keys_in = low_back(low(packed[:, 1])).reshape(length, HEADS, HEAD_DIM)
    values_in = low_back(low(packed[:, 2] + bias_pair[1])).reshape(length, HEADS, HEAD_DIM)
    scores = low_back(jnp.einsum('qhe,khe->hqk', queries, keys_in, precision=precise) * HEAD_DIM ** (-0.5))
    causal = jnp.arange(length)[:, None] >= jnp.arange(length)[None, :]
    probs_full = jax.nn.softmax(jnp.where(causal[None], scores, -1e+30), axis=-1)
    mixture = low_back(low(jnp.einsum('hqk,khe->qhe', low(probs_full), values_in, precision=precise)))
    mixture = mixture.reshape(length, D)
    residual = stream + low_back(jnp.dot(mixture, output_weight, precision=precise)) + output_bias
    normed_two = low(layer_norm(residual, gain_second, shift_second))
    hidden_pre = low_back(jnp.dot(normed_two, expand_weight, precision=precise) + expand_bias)
    hidden = low(gelu_tanh(hidden_pre))
    return residual + low_back(jnp.dot(hidden, contract_weight, precision=precise)) + contract_bias

def reference(inputs, cotangent, packed_weight, bias_pair, output_weight, output_bias, expand_weight, expand_bias, contract_weight, contract_bias, gain_first, shift_first, gain_second, shift_second):
    params = (packed_weight, bias_pair, output_weight, output_bias, expand_weight, expand_bias, contract_weight, contract_bias, gain_first, shift_first, gain_second, shift_second)
    params = tuple((member.astype(jnp.float32) for member in params))
    layer_zero = tuple((member[0] for member in params))
    layer_last = tuple((member[1] for member in params))
    micro_count = inputs.shape[0]
    batch_count = inputs.shape[1]
    flat_inputs = inputs.reshape(micro_count * batch_count, SEQ_LEN, D)
    flat_grads = cotangent.reshape(micro_count * batch_count, SEQ_LEN, D)

    def one_sequence(totals, operands):
        seq_input, seq_grad = operands
        middle, back_zero = jax.vjp(layer, seq_input, layer_zero)
        final_out, back_last = jax.vjp(layer, middle, layer_last)
        middle_grad, grads_last = back_last(seq_grad)
        input_grad, grads_zero = back_zero(middle_grad)
        totals = (jax.tree.map(jnp.add, totals[0], grads_zero), jax.tree.map(jnp.add, totals[1], grads_last))
        return (totals, (middle, final_out, input_grad, middle_grad))
    zeros_init = (jax.tree.map(jnp.zeros_like, layer_zero), jax.tree.map(jnp.zeros_like, layer_last))
    (sums_zero, sums_last), (middle, final_out, input_grad, middle_grad) = lax.scan(one_sequence, zeros_init, (flat_inputs, flat_grads))
    full_shape = (2, micro_count, batch_count, SEQ_LEN, D)
    section_outputs = jnp.stack([middle, final_out]).reshape(full_shape)
    section_grads = jnp.stack([input_grad, middle_grad]).reshape(full_shape)
    stacked = tuple((jnp.stack([grad_zero, grad_last]) for grad_zero, grad_last in zip(sums_zero, sums_last)))
    return (section_outputs, section_grads, stacked[0], stacked[1], stacked[2], stacked[3], stacked[4], stacked[5], stacked[6], stacked[7], stacked[8], stacked[9], stacked[10], stacked[11])
```

```python
import math

import jax
import jax.numpy as jnp
from jax import lax
from jax.sharding import PartitionSpec as P

HEAD_DIM = 64


epsilon = 1e-05
gelu_coef = math.sqrt(2.0 / math.pi)
masked_value = -1e30


def sent_to_all(array, axis):
    copies = jnp.broadcast_to(array, (lax.axis_size(axis), *array.shape))
    return lax.all_to_all(copies, axis, split_axis=0, concat_axis=0, tiled=True)


def taken_together(array, axis):
    return sent_to_all(array, axis).sum(axis=0)


def in_one(arrays, axis):
    ends = [0]
    for a in arrays:
        ends.append(ends[-1] + a.size)
    subtotal = lax.psum(jnp.concatenate([a.ravel() for a in arrays]), axis)
    return tuple((subtotal[b:e].reshape(a.shape) for a, b, e in zip(arrays, ends, ends[1:])))


def joined_along(parts, dim):
    parts = jnp.moveaxis(parts, 0, dim)
    shape = parts.shape
    return parts.reshape(*shape[:dim], shape[dim] * shape[dim + 1], *shape[dim + 2 :])


def collect(array, axis, dim):
    return lax.all_gather(array, axis, axis=dim, tiled=True)


def in_blocks(array, dim, peers):
    before, after = (array.shape[:dim], array.shape[dim + 1 :])
    return jnp.moveaxis(array.reshape(*before, peers, -1, *after), dim, 0)


def summed_on_arrival(array, axis, dim):
    return lax.psum_scatter(array, axis, scatter_dimension=dim, tiled=True).astype(jnp.float32)


def side_by_side(arrays, axis, dim, along):
    both = jnp.concatenate(arrays, axis=along)
    result, at, gathered = (lax.psum_scatter(both, axis, scatter_dimension=dim, tiled=True), 0, [])
    for a in arrays:
        gathered.append(lax.slice_in_dim(result, at, at + a.shape[along], axis=along))
        at += a.shape[along]
    return tuple(gathered)


def in_one_piece(arrays, axis, dim, along):
    both = jnp.concatenate(arrays, axis=along)
    result, at, gathered = (lax.all_gather(both, axis, axis=dim, tiled=True), 0, [])
    for a in arrays:
        gathered.append(lax.slice_in_dim(result, at, at + a.shape[along], axis=along))
        at += a.shape[along]
    return tuple(gathered)


def from_behind(array, axis, by):
    peers = lax.axis_size(axis)
    pairs = [(i, i + by) for i in range(peers) if 0 <= i + by < peers]
    return lax.ppermute(array, axis, pairs)


def gelu_tanh(values):
    return (
        0.5 * values * (1.0 + jnp.tanh(gelu_coef * (values + 0.044715 * values * values * values)))
    )


def norm_forward(stream, gain, offset):
    width_all = stream.shape[1] * lax.axis_size("tensor")
    totals, squares = in_one((jnp.sum(stream, axis=1), jnp.sum(stream * stream, axis=1)), "tensor")
    mean_row = (totals / width_all)[:, None]
    var_row = (squares / width_all)[:, None] - mean_row * mean_row
    inv_scale = lax.rsqrt(var_row + epsilon)
    normal_part = (stream - mean_row) * inv_scale
    normed = (normal_part * gain + offset).astype(jnp.bfloat16)
    return (collect(normed, "tensor", 1), normal_part, inv_scale)


def norm_backward(partial_term, normal_part, inv_scale, gain):
    width_all = partial_term.shape[1]
    d_normed = summed_on_arrival(partial_term.astype(jnp.bfloat16), "tensor", 1)
    gain_grad = jnp.sum(d_normed * normal_part, axis=0)
    offset_grad = jnp.sum(d_normed, axis=0)
    scaled = d_normed * gain
    first_sum, second_sum = in_one(
        (jnp.sum(scaled, axis=1), jnp.sum(scaled * normal_part, axis=1)), "tensor"
    )
    stream_grad = inv_scale * (
        scaled - first_sum[:, None] / width_all - normal_part * second_sum[:, None] / width_all
    )
    return (stream_grad, gain_grad, offset_grad)


def branch_sum(partial_term):
    return summed_on_arrival(partial_term.astype(jnp.bfloat16), "tensor", 1)


def branch_grad(stream_grad):
    return collect(stream_grad.astype(jnp.bfloat16), "tensor", 1)


def causal_scores(queries, keys_in):
    length = queries.shape[0]
    scale_factor = queries.shape[2] ** (-0.5)
    scores = (
        jnp.einsum("qhe,khe->hqk", queries, keys_in, preferred_element_type=jnp.float32)
        * scale_factor
    )
    causal = lax.broadcasted_iota(jnp.int32, (length, length), 0) >= lax.broadcasted_iota(
        jnp.int32, (length, length), 1
    )
    return (jnp.where(causal[None], scores, masked_value), scale_factor)


def attend(operands):
    queries, keys_in, values_in = operands
    masked, scale_factor = causal_scores(queries, keys_in)
    highest = jnp.max(masked, axis=2, keepdims=True)
    logsum = highest + jnp.log(jnp.sum(jnp.exp(masked - highest), axis=2, keepdims=True))
    weights_low = jnp.exp(masked - logsum).astype(jnp.bfloat16)
    mixture = jnp.einsum("hqk,khe->qhe", weights_low, values_in, preferred_element_type=jnp.float32)
    return (mixture.astype(jnp.bfloat16), logsum[:, :, 0])


def attend_back(operands):
    queries, keys_in, values_in, logsum, mixed_grad = operands
    masked, scale_factor = causal_scores(queries, keys_in)
    probs_full = jnp.exp(masked - logsum[:, :, None])
    probs_grad = jnp.einsum(
        "qhe,khe->hqk", mixed_grad, values_in, preferred_element_type=jnp.float32
    )
    row_dot = jnp.sum(probs_full * probs_grad, axis=2, keepdims=True)
    score_grad = (probs_full * (probs_grad - row_dot)).astype(jnp.bfloat16)
    query_grad = (
        jnp.einsum("hqk,khe->qhe", score_grad, keys_in, preferred_element_type=jnp.float32)
        * scale_factor
    )
    key_grad = (
        jnp.einsum("hqk,qhe->khe", score_grad, queries, preferred_element_type=jnp.float32)
        * scale_factor
    )
    value_grad = jnp.einsum(
        "hqk,qhe->khe",
        probs_full.astype(jnp.bfloat16),
        mixed_grad,
        preferred_element_type=jnp.float32,
    )
    return (
        query_grad.astype(jnp.bfloat16),
        key_grad.astype(jnp.bfloat16),
        value_grad.astype(jnp.bfloat16),
    )


def attention_forward(normed_one, packed_weight, bias_pair, shape_heads, rows_count, width_part):
    packed = jnp.einsum(
        "nd,dcf->ncf", normed_one, packed_weight, preferred_element_type=jnp.float32
    )
    queries = (packed[:, 0] + bias_pair[0]).astype(jnp.bfloat16)
    keys_in = packed[:, 1].astype(jnp.bfloat16)
    values_in = (packed[:, 2] + bias_pair[1]).astype(jnp.bfloat16)
    mixture, logsum = lax.map(
        attend,
        (
            queries.reshape(shape_heads),
            keys_in.reshape(shape_heads),
            values_in.reshape(shape_heads),
        ),
    )
    return (queries, keys_in, values_in, logsum, mixture.reshape(rows_count, width_part))


def attention_backward(branch_one, kept_part, output_weight, shape_heads, rows_count, width_part):
    queries, keys_in, values_in, logsum, mixed_rows, normed_one = kept_part
    output_weight_grad = jnp.einsum(
        "nf,nd->fd", mixed_rows, branch_one, preferred_element_type=jnp.float32
    )
    mixed_grad = jnp.einsum(
        "nd,fd->nf", branch_one, output_weight, preferred_element_type=jnp.float32
    ).astype(jnp.bfloat16)
    query_grad, key_grad, value_grad = lax.map(
        attend_back,
        (
            queries.reshape(shape_heads),
            keys_in.reshape(shape_heads),
            values_in.reshape(shape_heads),
            logsum,
            mixed_grad.reshape(shape_heads),
        ),
    )
    query_rows = query_grad.reshape(rows_count, width_part)
    key_rows = key_grad.reshape(rows_count, width_part)
    value_rows = value_grad.reshape(rows_count, width_part)
    packed_grad = jnp.stack([query_rows, key_rows, value_rows], axis=1)
    bias_pair_grad = jnp.stack(
        [
            jnp.sum(query_rows.astype(jnp.float32), axis=0),
            jnp.sum(value_rows.astype(jnp.float32), axis=0),
        ]
    )
    packed_weight_grad = jnp.einsum(
        "nd,ncf->dcf", normed_one, packed_grad, preferred_element_type=jnp.float32
    )
    return (packed_grad, packed_weight_grad, bias_pair_grad, output_weight_grad)


def layer_forward(stream, weights):
    (
        packed_weight,
        bias_pair,
        output_weight,
        output_bias,
        expand_weight,
        expand_bias,
        contract_weight,
        contract_bias,
        gain_first,
        shift_first,
        gain_second,
        shift_second,
    ) = weights
    seq_count, length, width_part = stream.shape
    rows_count = seq_count * length
    shape_heads = (seq_count, length, width_part // HEAD_DIM, HEAD_DIM)
    stream_rows = stream.reshape(rows_count, width_part)
    normed_one, normal_one, inv_one = norm_forward(stream_rows, gain_first, shift_first)
    queries, keys_in, values_in, logsum, mixed_rows = attention_forward(
        normed_one, packed_weight, bias_pair, shape_heads, rows_count, width_part
    )
    residual = (
        stream_rows
        + branch_sum(jnp.dot(mixed_rows, output_weight, preferred_element_type=jnp.float32))
        + output_bias
    )
    normed_two, normal_two, inv_two = norm_forward(residual, gain_second, shift_second)
    hidden_pre = (
        jnp.dot(normed_two, expand_weight, preferred_element_type=jnp.float32) + expand_bias
    )
    hidden = gelu_tanh(hidden_pre).astype(jnp.bfloat16)
    result = (
        residual
        + branch_sum(jnp.dot(hidden, contract_weight, preferred_element_type=jnp.float32))
        + contract_bias
    )
    kept_values = (
        normed_one,
        normal_one,
        inv_one,
        queries,
        keys_in,
        values_in,
        logsum,
        mixed_rows,
        normed_two,
        normal_two,
        inv_two,
        hidden_pre,
        hidden,
    )
    return (result.reshape(stream.shape), kept_values)


def layer_backward(out_grad, kept_values, weights):
    (
        packed_weight,
        bias_pair,
        output_weight,
        output_bias,
        expand_weight,
        expand_bias,
        contract_weight,
        contract_bias,
        gain_first,
        shift_first,
        gain_second,
        shift_second,
    ) = weights
    (
        normed_one,
        normal_one,
        inv_one,
        queries,
        keys_in,
        values_in,
        logsum,
        mixed_rows,
        normed_two,
        normal_two,
        inv_two,
        hidden_pre,
        hidden,
    ) = kept_values
    seq_count, length, width_part = out_grad.shape
    rows_count = seq_count * length
    shape_heads = (seq_count, length, width_part // HEAD_DIM, HEAD_DIM)
    grad_rows = out_grad.reshape(rows_count, width_part)
    contract_bias_grad = jnp.sum(grad_rows, axis=0)
    branch_two = branch_grad(grad_rows)
    contract_weight_grad = jnp.einsum(
        "nf,nd->fd", hidden, branch_two, preferred_element_type=jnp.float32
    )
    hidden_grad = jnp.einsum(
        "nd,fd->nf", branch_two, contract_weight, preferred_element_type=jnp.float32
    )
    pre_grad = jax.vjp(gelu_tanh, hidden_pre)[1](hidden_grad)[0].astype(jnp.bfloat16)
    expand_bias_grad = jnp.sum(pre_grad.astype(jnp.float32), axis=0)
    expand_weight_grad = jnp.einsum(
        "nd,nf->df", normed_two, pre_grad, preferred_element_type=jnp.float32
    )
    second_grad, gain_second_grad, shift_second_grad = norm_backward(
        jnp.einsum("nf,df->nd", pre_grad, expand_weight, preferred_element_type=jnp.float32),
        normal_two,
        inv_two,
        gain_second,
    )
    residual_grad = grad_rows + second_grad
    output_bias_grad = jnp.sum(residual_grad, axis=0)
    branch_one = branch_grad(residual_grad)
    packed_grad, packed_weight_grad, bias_pair_grad, output_weight_grad = attention_backward(
        branch_one,
        (queries, keys_in, values_in, logsum, mixed_rows, normed_one),
        output_weight,
        shape_heads,
        rows_count,
        width_part,
    )
    first_grad, gain_first_grad, shift_first_grad = norm_backward(
        jnp.einsum("ncf,dcf->nd", packed_grad, packed_weight, preferred_element_type=jnp.float32),
        normal_one,
        inv_one,
        gain_first,
    )
    input_grad = (residual_grad + first_grad).reshape(out_grad.shape)
    return (
        input_grad,
        (
            packed_weight_grad,
            bias_pair_grad,
            output_weight_grad,
            output_bias_grad,
            expand_weight_grad,
            expand_bias_grad,
            contract_weight_grad,
            contract_bias_grad,
            gain_first_grad,
            shift_first_grad,
            gain_second_grad,
            shift_second_grad,
        ),
    )


def sum_at_end(grads):
    (
        part_packed,
        part_pair,
        part_outmat,
        part_outbias,
        part_expmat,
        part_expbias,
        part_conmat,
        part_conbias,
        part_gainone,
        part_shiftone,
        part_gaintwo,
        part_shifttwo,
    ) = grads
    return (
        lax.psum_scatter(
            part_packed[None].astype(jnp.bfloat16), "dp", scatter_dimension=1, tiled=True
        ).astype(jnp.float32),
        lax.psum_scatter(
            part_pair[None].astype(jnp.bfloat16), "dp", scatter_dimension=2, tiled=True
        ).astype(jnp.float32),
        lax.psum_scatter(
            part_outmat[None].astype(jnp.bfloat16), "dp", scatter_dimension=2, tiled=True
        ).astype(jnp.float32),
        lax.psum_scatter(
            part_outbias[None].astype(jnp.bfloat16), "dp", scatter_dimension=1, tiled=True
        ).astype(jnp.float32),
        lax.psum_scatter(
            part_expmat[None].astype(jnp.bfloat16), "dp", scatter_dimension=1, tiled=True
        ).astype(jnp.float32),
        lax.psum_scatter(
            part_expbias[None].astype(jnp.bfloat16), "dp", scatter_dimension=1, tiled=True
        ).astype(jnp.float32),
        lax.psum_scatter(
            part_conmat[None].astype(jnp.bfloat16), "dp", scatter_dimension=2, tiled=True
        ).astype(jnp.float32),
        *tuple(
            (
                part.astype(jnp.float32)
                for part in side_by_side(
                    (
                        part_conbias[None].astype(jnp.bfloat16),
                        part_gainone[None].astype(jnp.bfloat16),
                        part_shiftone[None].astype(jnp.bfloat16),
                        part_gaintwo[None].astype(jnp.bfloat16),
                        part_shifttwo[None].astype(jnp.bfloat16),
                    ),
                    "dp",
                    1,
                    0,
                )
            )
        ),
    )


def shards(
    inputs,
    cotangent,
    packed_weight,
    bias_pair,
    output_weight,
    output_bias,
    expand_weight,
    expand_bias,
    contract_weight,
    contract_bias,
    gain_first,
    shift_first,
    gain_second,
    shift_second,
):
    gathered = (
        lax.all_gather(packed_weight, "dp", axis=1, tiled=True),
        lax.all_gather(bias_pair, "dp", axis=2, tiled=True),
        lax.all_gather(output_weight, "dp", axis=2, tiled=True),
        lax.all_gather(output_bias, "dp", axis=1, tiled=True),
        lax.all_gather(expand_weight, "dp", axis=1, tiled=True),
        lax.all_gather(expand_bias, "dp", axis=1, tiled=True),
        lax.all_gather(contract_weight, "dp", axis=2, tiled=True),
        *in_one_piece(
            (contract_bias, gain_first, shift_first, gain_second, shift_second), "dp", 1, 0
        ),
    )
    weights = tuple((member[0] for member in gathered))
    is_first = lax.axis_index("section") == 0
    micro_count = inputs.shape[0]
    zero_block = jnp.zeros_like(inputs[0])
    received = zero_block
    returned = zero_block
    outputs_list = []
    kept_list = []
    backs_list = []
    grad_total = None
    for tick_index in range(micro_count + 2):
        if tick_index <= micro_count:
            own_input = inputs[tick_index] if tick_index < micro_count else zero_block
            stream = jnp.where(is_first, own_input, received)
            result, kept_values = layer_forward(stream, weights)
            outputs_list.append(result)
            kept_list.append(kept_values)
            if tick_index < micro_count:
                received = from_behind(result.astype(jnp.bfloat16), "section", 1).astype(
                    result.dtype
                )
        if tick_index >= 1:
            own_grad = cotangent[tick_index - 1] if tick_index - 1 < micro_count else zero_block
            out_grad = jnp.where(is_first, returned, own_grad)
            early_kept = kept_list[tick_index - 2] if tick_index >= 2 else kept_list[tick_index]
            late_kept = (
                kept_list[tick_index] if tick_index <= micro_count else kept_list[tick_index - 2]
            )
            chosen = jax.tree.map(
                lambda early_one, late_one: jnp.where(is_first, early_one, late_one),
                early_kept,
                late_kept,
            )
            input_grad, grads = layer_backward(out_grad, chosen, weights)
            backs_list.append(input_grad)
            if tick_index <= micro_count:
                returned = from_behind(input_grad.astype(jnp.bfloat16), "section", -1).astype(
                    input_grad.dtype
                )
            grad_total = grads if grad_total is None else jax.tree.map(jnp.add, grad_total, grads)
    reduced = sum_at_end(grad_total)
    section_outputs = jnp.stack(
        [
            jnp.where(is_first, outputs_list[slot_index], outputs_list[slot_index + 1])
            for slot_index in range(micro_count)
        ]
    )[None]
    section_grads = jnp.stack(
        [
            jnp.where(is_first, backs_list[slot_index + 1], backs_list[slot_index])
            for slot_index in range(micro_count)
        ]
    )[None]
    return (section_outputs, section_grads) + tuple(reduced)


def solution(mesh):
    in_specs = (
        P(None, "dp", None, "tensor"),
        P(None, "dp", None, "tensor"),
        P("section", "dp", None, "tensor"),
        P("section", None, ("tensor", "dp")),
        P("section", "tensor", "dp"),
        P("section", ("tensor", "dp")),
        P("section", "dp", "tensor"),
        P("section", ("tensor", "dp")),
        P("section", "tensor", "dp"),
        P("section", ("tensor", "dp")),
        P("section", ("tensor", "dp")),
        P("section", ("tensor", "dp")),
        P("section", ("tensor", "dp")),
        P("section", ("tensor", "dp")),
    )
    out_specs = (
        P("section", None, "dp", None, "tensor"),
        P("section", None, "dp", None, "tensor"),
        P("section", "dp", None, "tensor"),
        P("section", None, ("tensor", "dp")),
        P("section", "tensor", "dp"),
        P("section", ("tensor", "dp")),
        P("section", "dp", "tensor"),
        P("section", ("tensor", "dp")),
        P("section", "tensor", "dp"),
        P("section", ("tensor", "dp")),
        P("section", ("tensor", "dp")),
        P("section", ("tensor", "dp")),
        P("section", ("tensor", "dp")),
        P("section", ("tensor", "dp")),
    )
    return jax.shard_map(shards, mesh=mesh, in_specs=in_specs, out_specs=out_specs, check_vma=False)
```

```python
import math

import jax
import jax.numpy as jnp
from jax import lax
from jax.sharding import PartitionSpec as P

HEAD_DIM = 64


epsilon = 1e-05
gelu_coef = math.sqrt(2.0 / math.pi)
masked_value = -1e30


def sent_to_all(array, axis):
    copies = jnp.broadcast_to(array, (lax.axis_size(axis), *array.shape))
    return lax.all_to_all(copies, axis, split_axis=0, concat_axis=0, tiled=True)


def taken_together(array, axis):
    return sent_to_all(array, axis).sum(axis=0)


def in_one(arrays, axis):
    ends = [0]
    for a in arrays:
        ends.append(ends[-1] + a.size)
    subtotal = taken_together(jnp.concatenate([a.ravel() for a in arrays]), axis)
    return tuple((subtotal[b:e].reshape(a.shape) for a, b, e in zip(arrays, ends, ends[1:])))


def joined_along(parts, dim):
    parts = jnp.moveaxis(parts, 0, dim)
    shape = parts.shape
    return parts.reshape(*shape[:dim], shape[dim] * shape[dim + 1], *shape[dim + 2 :])


def collect(array, axis, dim):
    parts = sent_to_all(array, axis)
    return joined_along(parts, dim)


def in_blocks(array, dim, peers):
    before, after = (array.shape[:dim], array.shape[dim + 1 :])
    return jnp.moveaxis(array.reshape(*before, peers, -1, *after), dim, 0)


def summed_on_arrival(array, axis, dim):
    parts = in_blocks(array, dim, lax.axis_size(axis))
    arrived = lax.all_to_all(parts, axis, split_axis=0, concat_axis=0, tiled=True)
    return arrived.astype(jnp.float32).sum(axis=0)


def side_by_side(arrays, axis, dim, along):
    both = jnp.concatenate(arrays, axis=along)
    result, at, gathered = (lax.psum_scatter(both, axis, scatter_dimension=dim, tiled=True), 0, [])
    for a in arrays:
        gathered.append(lax.slice_in_dim(result, at, at + a.shape[along], axis=along))
        at += a.shape[along]
    return tuple(gathered)


def in_one_piece(arrays, axis, dim, along):
    both = jnp.concatenate(arrays, axis=along)
    result, at, gathered = (lax.all_gather(both, axis, axis=dim, tiled=True), 0, [])
    for a in arrays:
        gathered.append(lax.slice_in_dim(result, at, at + a.shape[along], axis=along))
        at += a.shape[along]
    return tuple(gathered)


def from_behind(array, axis, by):
    peers = lax.axis_size(axis)
    pairs = [(i, i + by) for i in range(peers) if 0 <= i + by < peers]
    return lax.ppermute(array, axis, pairs)


def gelu_tanh(values):
    return (
        0.5 * values * (1.0 + jnp.tanh(gelu_coef * (values + 0.044715 * values * values * values)))
    )


def norm_forward(stream, gain, offset):
    width_all = stream.shape[1] * lax.axis_size("tensor")
    totals, squares = in_one((jnp.sum(stream, axis=1), jnp.sum(stream * stream, axis=1)), "tensor")
    mean_row = (totals / width_all)[:, None]
    var_row = (squares / width_all)[:, None] - mean_row * mean_row
    inv_scale = lax.rsqrt(var_row + epsilon)
    normal_part = (stream - mean_row) * inv_scale
    normed = (normal_part * gain + offset).astype(jnp.bfloat16)
    return (collect(normed, "tensor", 1), normal_part, inv_scale)


def norm_backward(partial_term, normal_part, inv_scale, gain):
    width_all = partial_term.shape[1]
    d_normed = summed_on_arrival(partial_term.astype(jnp.bfloat16), "tensor", 1)
    gain_grad = jnp.sum(d_normed * normal_part, axis=0)
    offset_grad = jnp.sum(d_normed, axis=0)
    scaled = d_normed * gain
    first_sum, second_sum = in_one(
        (jnp.sum(scaled, axis=1), jnp.sum(scaled * normal_part, axis=1)), "tensor"
    )
    stream_grad = inv_scale * (
        scaled - first_sum[:, None] / width_all - normal_part * second_sum[:, None] / width_all
    )
    return (stream_grad, gain_grad, offset_grad)


def branch_sum(partial_term):
    return summed_on_arrival(partial_term.astype(jnp.bfloat16), "tensor", 1)


def branch_grad(stream_grad):
    return collect(stream_grad.astype(jnp.bfloat16), "tensor", 1)


def causal_scores(queries, keys_in):
    length = queries.shape[0]
    scale_factor = queries.shape[2] ** (-0.5)
    scores = (
        jnp.einsum("qhe,khe->hqk", queries, keys_in, preferred_element_type=jnp.float32)
        * scale_factor
    )
    causal = lax.broadcasted_iota(jnp.int32, (length, length), 0) >= lax.broadcasted_iota(
        jnp.int32, (length, length), 1
    )
    return (jnp.where(causal[None], scores, masked_value), scale_factor)


def attend(operands):
    queries, keys_in, values_in = operands
    masked, scale_factor = causal_scores(queries, keys_in)
    highest = jnp.max(masked, axis=2, keepdims=True)
    logsum = highest + jnp.log(jnp.sum(jnp.exp(masked - highest), axis=2, keepdims=True))
    weights_low = jnp.exp(masked - logsum).astype(jnp.bfloat16)
    mixture = jnp.einsum("hqk,khe->qhe", weights_low, values_in, preferred_element_type=jnp.float32)
    return (mixture.astype(jnp.bfloat16), logsum[:, :, 0])


def attend_back(operands):
    queries, keys_in, values_in, logsum, mixed_grad = operands
    masked, scale_factor = causal_scores(queries, keys_in)
    probs_full = jnp.exp(masked - logsum[:, :, None])
    probs_grad = jnp.einsum(
        "qhe,khe->hqk", mixed_grad, values_in, preferred_element_type=jnp.float32
    )
    row_dot = jnp.sum(probs_full * probs_grad, axis=2, keepdims=True)
    score_grad = (probs_full * (probs_grad - row_dot)).astype(jnp.bfloat16)
    query_grad = (
        jnp.einsum("hqk,khe->qhe", score_grad, keys_in, preferred_element_type=jnp.float32)
        * scale_factor
    )
    key_grad = (
        jnp.einsum("hqk,qhe->khe", score_grad, queries, preferred_element_type=jnp.float32)
        * scale_factor
    )
    value_grad = jnp.einsum(
        "hqk,qhe->khe",
        probs_full.astype(jnp.bfloat16),
        mixed_grad,
        preferred_element_type=jnp.float32,
    )
    return (
        query_grad.astype(jnp.bfloat16),
        key_grad.astype(jnp.bfloat16),
        value_grad.astype(jnp.bfloat16),
    )


def attention_forward(normed_one, packed_weight, bias_pair, shape_heads, rows_count, width_part):
    packed = jnp.einsum(
        "nd,dcf->ncf", normed_one, packed_weight, preferred_element_type=jnp.float32
    )
    queries = (packed[:, 0] + bias_pair[0]).astype(jnp.bfloat16)
    keys_in = packed[:, 1].astype(jnp.bfloat16)
    values_in = (packed[:, 2] + bias_pair[1]).astype(jnp.bfloat16)
    mixture, logsum = lax.map(
        attend,
        (
            queries.reshape(shape_heads),
            keys_in.reshape(shape_heads),
            values_in.reshape(shape_heads),
        ),
    )
    return (queries, keys_in, values_in, logsum, mixture.reshape(rows_count, width_part))


def attention_backward(branch_one, kept_part, output_weight, shape_heads, rows_count, width_part):
    queries, keys_in, values_in, logsum, mixed_rows, normed_one = kept_part
    output_weight_grad = jnp.einsum(
        "nf,nd->fd", mixed_rows, branch_one, preferred_element_type=jnp.float32
    )
    mixed_grad = jnp.einsum(
        "nd,fd->nf", branch_one, output_weight, preferred_element_type=jnp.float32
    ).astype(jnp.bfloat16)
    query_grad, key_grad, value_grad = lax.map(
        attend_back,
        (
            queries.reshape(shape_heads),
            keys_in.reshape(shape_heads),
            values_in.reshape(shape_heads),
            logsum,
            mixed_grad.reshape(shape_heads),
        ),
    )
    query_rows = query_grad.reshape(rows_count, width_part)
    key_rows = key_grad.reshape(rows_count, width_part)
    value_rows = value_grad.reshape(rows_count, width_part)
    packed_grad = jnp.stack([query_rows, key_rows, value_rows], axis=1)
    bias_pair_grad = jnp.stack(
        [
            jnp.sum(query_rows.astype(jnp.float32), axis=0),
            jnp.sum(value_rows.astype(jnp.float32), axis=0),
        ]
    )
    packed_weight_grad = jnp.einsum(
        "nd,ncf->dcf", normed_one, packed_grad, preferred_element_type=jnp.float32
    )
    return (packed_grad, packed_weight_grad, bias_pair_grad, output_weight_grad)


def layer_forward(stream, weights):
    (
        packed_weight,
        bias_pair,
        output_weight,
        output_bias,
        expand_weight,
        expand_bias,
        contract_weight,
        contract_bias,
        gain_first,
        shift_first,
        gain_second,
        shift_second,
    ) = weights
    seq_count, length, width_part = stream.shape
    rows_count = seq_count * length
    shape_heads = (seq_count, length, width_part // HEAD_DIM, HEAD_DIM)
    stream_rows = stream.reshape(rows_count, width_part)
    normed_one, normal_one, inv_one = norm_forward(stream_rows, gain_first, shift_first)
    queries, keys_in, values_in, logsum, mixed_rows = attention_forward(
        normed_one, packed_weight, bias_pair, shape_heads, rows_count, width_part
    )
    residual = (
        stream_rows
        + branch_sum(jnp.dot(mixed_rows, output_weight, preferred_element_type=jnp.float32))
        + output_bias
    )
    normed_two, normal_two, inv_two = norm_forward(residual, gain_second, shift_second)
    hidden_pre = (
        jnp.dot(normed_two, expand_weight, preferred_element_type=jnp.float32) + expand_bias
    )
    hidden = gelu_tanh(hidden_pre).astype(jnp.bfloat16)
    result = (
        residual
        + branch_sum(jnp.dot(hidden, contract_weight, preferred_element_type=jnp.float32))
        + contract_bias
    )
    kept_values = (
        normed_one,
        normal_one,
        inv_one,
        queries,
        keys_in,
        values_in,
        logsum,
        mixed_rows,
        normed_two,
        normal_two,
        inv_two,
        hidden_pre,
        hidden,
    )
    return (result.reshape(stream.shape), kept_values)


def layer_backward(out_grad, kept_values, weights):
    (
        packed_weight,
        bias_pair,
        output_weight,
        output_bias,
        expand_weight,
        expand_bias,
        contract_weight,
        contract_bias,
        gain_first,
        shift_first,
        gain_second,
        shift_second,
    ) = weights
    (
        normed_one,
        normal_one,
        inv_one,
        queries,
        keys_in,
        values_in,
        logsum,
        mixed_rows,
        normed_two,
        normal_two,
        inv_two,
        hidden_pre,
        hidden,
    ) = kept_values
    seq_count, length, width_part = out_grad.shape
    rows_count = seq_count * length
    shape_heads = (seq_count, length, width_part // HEAD_DIM, HEAD_DIM)
    grad_rows = out_grad.reshape(rows_count, width_part)
    contract_bias_grad = jnp.sum(grad_rows, axis=0)
    branch_two = branch_grad(grad_rows)
    contract_weight_grad = jnp.einsum(
        "nf,nd->fd", hidden, branch_two, preferred_element_type=jnp.float32
    )
    hidden_grad = jnp.einsum(
        "nd,fd->nf", branch_two, contract_weight, preferred_element_type=jnp.float32
    )
    pre_grad = jax.vjp(gelu_tanh, hidden_pre)[1](hidden_grad)[0].astype(jnp.bfloat16)
    expand_bias_grad = jnp.sum(pre_grad.astype(jnp.float32), axis=0)
    expand_weight_grad = jnp.einsum(
        "nd,nf->df", normed_two, pre_grad, preferred_element_type=jnp.float32
    )
    second_grad, gain_second_grad, shift_second_grad = norm_backward(
        jnp.einsum("nf,df->nd", pre_grad, expand_weight, preferred_element_type=jnp.float32),
        normal_two,
        inv_two,
        gain_second,
    )
    residual_grad = grad_rows + second_grad
    output_bias_grad = jnp.sum(residual_grad, axis=0)
    branch_one = branch_grad(residual_grad)
    packed_grad, packed_weight_grad, bias_pair_grad, output_weight_grad = attention_backward(
        branch_one,
        (queries, keys_in, values_in, logsum, mixed_rows, normed_one),
        output_weight,
        shape_heads,
        rows_count,
        width_part,
    )
    first_grad, gain_first_grad, shift_first_grad = norm_backward(
        jnp.einsum("ncf,dcf->nd", packed_grad, packed_weight, preferred_element_type=jnp.float32),
        normal_one,
        inv_one,
        gain_first,
    )
    input_grad = (residual_grad + first_grad).reshape(out_grad.shape)
    return (
        input_grad,
        (
            packed_weight_grad,
            bias_pair_grad,
            output_weight_grad,
            output_bias_grad,
            expand_weight_grad,
            expand_bias_grad,
            contract_weight_grad,
            contract_bias_grad,
            gain_first_grad,
            shift_first_grad,
            gain_second_grad,
            shift_second_grad,
        ),
    )


def as_blocks(array, dim, peers):
    before, after = (array.shape[:dim], array.shape[dim + 1 :])
    split = array.reshape(*before, peers, array.shape[dim] // peers, *after)
    return jnp.moveaxis(split, dim, 0).reshape(peers, -1)


def from_blocks(flat, shape, dim, peers):
    block_shape = (*shape[:dim], shape[dim] // peers, *shape[dim + 1 :])
    return flat.reshape(block_shape)


def sum_at_end(grads, dims):
    peers = lax.axis_size("dp")
    pieces = [as_blocks(g.astype(jnp.bfloat16), d, peers) for g, d in zip(grads, dims)]
    widths = [p.shape[1] for p in pieces]
    spare = -sum(widths) % 1024
    pieces.append(jnp.zeros((peers, spare), jnp.bfloat16))
    total = lax.psum_scatter(
        jnp.concatenate(pieces, axis=1).reshape(1, -1, 128), "dp", scatter_dimension=1, tiled=True
    ).reshape(1, -1)
    reduced, at = ([], 0)
    for g, d, w in zip(grads, dims, widths):
        piece = total[0, at : at + w].astype(jnp.float32)
        reduced.append(from_blocks(piece, g.shape, d, peers)[None])
        at += w
    return tuple(reduced)


def gather_all(weights, dims):
    peers = lax.axis_size("dp")
    size = sum(w.size for w in weights)
    flat = jnp.concatenate([w.reshape(-1) for w in weights] + [jnp.zeros((-size % 1024,), jnp.bfloat16)])
    every = lax.all_gather(flat[None], "dp", axis=0, tiled=True)
    gathered, at = ([], 0)
    for w, d in zip(weights, dims):
        part = every[:, at : at + w.size].reshape(peers, *w.shape)
        part = jnp.moveaxis(part, 0, d)
        shape = part.shape
        gathered.append(part.reshape(*shape[:d], shape[d] * shape[d + 1], *shape[d + 2 :]))
        at += w.size
    return tuple(gathered)


def shards(
    inputs,
    cotangent,
    packed_weight,
    bias_pair,
    output_weight,
    output_bias,
    expand_weight,
    expand_bias,
    contract_weight,
    contract_bias,
    gain_first,
    shift_first,
    gain_second,
    shift_second,
):
    gathered = gather_all(
        (
            packed_weight[0],
            bias_pair[0],
            output_weight[0],
            output_bias[0],
            expand_weight[0],
            expand_bias[0],
            contract_weight[0],
            contract_bias[0],
            gain_first[0],
            shift_first[0],
            gain_second[0],
            shift_second[0],
        ),
        (0, 1, 1, 0, 0, 0, 1, 0, 0, 0, 0, 0),
    )
    weights = gathered
    is_first = lax.axis_index("section") == 0
    micro_count = inputs.shape[0]
    zero_block = jnp.zeros_like(inputs[0])
    received = zero_block
    returned = zero_block
    outputs_list = []
    kept_list = []
    backs_list = []
    grad_total = None
    for tick_index in range(micro_count + 2):
        if tick_index <= micro_count:
            own_input = inputs[tick_index] if tick_index < micro_count else zero_block
            stream = jnp.where(is_first, own_input, received)
            result, kept_values = layer_forward(stream, weights)
            outputs_list.append(result)
            kept_list.append(kept_values)
            if tick_index < micro_count:
                received = from_behind(result.astype(jnp.bfloat16), "section", 1).astype(
                    result.dtype
                )
        if tick_index >= 1:
            own_grad = cotangent[tick_index - 1] if tick_index - 1 < micro_count else zero_block
            out_grad = jnp.where(is_first, returned, own_grad)
            early_kept = kept_list[tick_index - 2] if tick_index >= 2 else kept_list[tick_index]
            late_kept = (
                kept_list[tick_index] if tick_index <= micro_count else kept_list[tick_index - 2]
            )
            chosen = jax.tree.map(
                lambda early_one, late_one: jnp.where(is_first, early_one, late_one),
                early_kept,
                late_kept,
            )
            input_grad, grads = layer_backward(out_grad, chosen, weights)
            backs_list.append(input_grad)
            if tick_index <= micro_count:
                returned = from_behind(input_grad.astype(jnp.bfloat16), "section", -1).astype(
                    input_grad.dtype
                )
            grad_total = grads if grad_total is None else jax.tree.map(jnp.add, grad_total, grads)
    reduced = sum_at_end(grad_total, (0, 1, 1, 0, 0, 0, 1, 0, 0, 0, 0, 0))
    section_outputs = jnp.stack(
        [
            jnp.where(is_first, outputs_list[slot_index], outputs_list[slot_index + 1])
            for slot_index in range(micro_count)
        ]
    )[None]
    section_grads = jnp.stack(
        [
            jnp.where(is_first, backs_list[slot_index + 1], backs_list[slot_index])
            for slot_index in range(micro_count)
        ]
    )[None]
    return (section_outputs, section_grads) + tuple(reduced)


def solution(mesh):
    in_specs = (
        P(None, "dp", None, "tensor"),
        P(None, "dp", None, "tensor"),
        P("section", "dp", None, "tensor"),
        P("section", None, ("tensor", "dp")),
        P("section", "tensor", "dp"),
        P("section", ("tensor", "dp")),
        P("section", "dp", "tensor"),
        P("section", ("tensor", "dp")),
        P("section", "tensor", "dp"),
        P("section", ("tensor", "dp")),
        P("section", ("tensor", "dp")),
        P("section", ("tensor", "dp")),
        P("section", ("tensor", "dp")),
        P("section", ("tensor", "dp")),
    )
    out_specs = (
        P("section", None, "dp", None, "tensor"),
        P("section", None, "dp", None, "tensor"),
        P("section", "dp", None, "tensor"),
        P("section", None, ("tensor", "dp")),
        P("section", "tensor", "dp"),
        P("section", ("tensor", "dp")),
        P("section", "dp", "tensor"),
        P("section", ("tensor", "dp")),
        P("section", "tensor", "dp"),
        P("section", ("tensor", "dp")),
        P("section", ("tensor", "dp")),
        P("section", ("tensor", "dp")),
        P("section", ("tensor", "dp")),
        P("section", ("tensor", "dp")),
    )
    return jax.shard_map(shards, mesh=mesh, in_specs=in_specs, out_specs=out_specs, check_vma=False)
```

```python
import math

import jax
import jax.numpy as jnp
from jax import lax
from jax.sharding import PartitionSpec as P

HEAD_DIM = 64


epsilon = 1e-05
gelu_coef = math.sqrt(2.0 / math.pi)
masked_value = -1e30


def sent_to_all(array, axis):
    copies = jnp.broadcast_to(array, (lax.axis_size(axis), *array.shape))
    return lax.all_to_all(copies, axis, split_axis=0, concat_axis=0, tiled=True)


def taken_together(array, axis):
    return sent_to_all(array, axis).sum(axis=0)


def in_one(arrays, axis):
    ends = [0]
    for a in arrays:
        ends.append(ends[-1] + a.size)
    subtotal = taken_together(jnp.concatenate([a.ravel() for a in arrays]), axis)
    return tuple((subtotal[b:e].reshape(a.shape) for a, b, e in zip(arrays, ends, ends[1:])))


def joined_along(parts, dim):
    parts = jnp.moveaxis(parts, 0, dim)
    shape = parts.shape
    return parts.reshape(*shape[:dim], shape[dim] * shape[dim + 1], *shape[dim + 2 :])


def collect(array, axis, dim):
    parts = sent_to_all(array, axis)
    return joined_along(parts, dim)


def in_blocks(array, dim, peers):
    before, after = (array.shape[:dim], array.shape[dim + 1 :])
    return jnp.moveaxis(array.reshape(*before, peers, -1, *after), dim, 0)


def summed_on_arrival(array, axis, dim):
    parts = in_blocks(array, dim, lax.axis_size(axis))
    arrived = lax.all_to_all(parts, axis, split_axis=0, concat_axis=0, tiled=True)
    return arrived.astype(jnp.float32).sum(axis=0)


def side_by_side(arrays, axis, dim, along):
    both = jnp.concatenate(arrays, axis=along)
    result, at, gathered = (lax.psum_scatter(both, axis, scatter_dimension=dim, tiled=True), 0, [])
    for a in arrays:
        gathered.append(lax.slice_in_dim(result, at, at + a.shape[along], axis=along))
        at += a.shape[along]
    return tuple(gathered)


def in_one_piece(arrays, axis, dim, along):
    both = jnp.concatenate(arrays, axis=along)
    result, at, gathered = (lax.all_gather(both, axis, axis=dim, tiled=True), 0, [])
    for a in arrays:
        gathered.append(lax.slice_in_dim(result, at, at + a.shape[along], axis=along))
        at += a.shape[along]
    return tuple(gathered)


def from_behind(array, axis, by):
    peers = lax.axis_size(axis)
    pairs = [(i, i + by) for i in range(peers) if 0 <= i + by < peers]
    return lax.ppermute(array, axis, pairs)


def gelu_tanh(values):
    return (
        0.5 * values * (1.0 + jnp.tanh(gelu_coef * (values + 0.044715 * values * values * values)))
    )


def norm_forward(stream, gain, offset):
    width_all = stream.shape[1] * lax.axis_size("tensor")
    totals, squares = in_one((jnp.sum(stream, axis=1), jnp.sum(stream * stream, axis=1)), "tensor")
    mean_row = (totals / width_all)[:, None]
    var_row = (squares / width_all)[:, None] - mean_row * mean_row
    inv_scale = lax.rsqrt(var_row + epsilon)
    normal_part = (stream - mean_row) * inv_scale
    normed = (normal_part * gain + offset).astype(jnp.bfloat16)
    return (collect(normed, "tensor", 1), normal_part, inv_scale)


def norm_backward(partial_term, normal_part, inv_scale, gain):
    width_all = partial_term.shape[1]
    d_normed = summed_on_arrival(partial_term.astype(jnp.bfloat16), "tensor", 1)
    gain_grad = jnp.sum(d_normed * normal_part, axis=0)
    offset_grad = jnp.sum(d_normed, axis=0)
    scaled = d_normed * gain
    first_sum, second_sum = in_one(
        (jnp.sum(scaled, axis=1), jnp.sum(scaled * normal_part, axis=1)), "tensor"
    )
    stream_grad = inv_scale * (
        scaled - first_sum[:, None] / width_all - normal_part * second_sum[:, None] / width_all
    )
    return (stream_grad, gain_grad, offset_grad)


def branch_sum(partial_term):
    return summed_on_arrival(partial_term.astype(jnp.bfloat16), "tensor", 1)


def branch_grad(stream_grad):
    return collect(stream_grad.astype(jnp.bfloat16), "tensor", 1)


def causal_scores(queries, keys_in):
    length = queries.shape[0]
    scale_factor = queries.shape[2] ** (-0.5)
    scores = (
        jnp.einsum("qhe,khe->hqk", queries, keys_in, preferred_element_type=jnp.float32)
        * scale_factor
    )
    causal = lax.broadcasted_iota(jnp.int32, (length, length), 0) >= lax.broadcasted_iota(
        jnp.int32, (length, length), 1
    )
    return (jnp.where(causal[None], scores, masked_value), scale_factor)


def attend(operands):
    queries, keys_in, values_in = operands
    masked, scale_factor = causal_scores(queries, keys_in)
    highest = jnp.max(masked, axis=2, keepdims=True)
    logsum = highest + jnp.log(jnp.sum(jnp.exp(masked - highest), axis=2, keepdims=True))
    weights_low = jnp.exp(masked - logsum).astype(jnp.bfloat16)
    mixture = jnp.einsum("hqk,khe->qhe", weights_low, values_in, preferred_element_type=jnp.float32)
    return (mixture.astype(jnp.bfloat16), logsum[:, :, 0])


def attend_back(operands):
    queries, keys_in, values_in, logsum, mixed_grad = operands
    masked, scale_factor = causal_scores(queries, keys_in)
    probs_full = jnp.exp(masked - logsum[:, :, None])
    probs_grad = jnp.einsum(
        "qhe,khe->hqk", mixed_grad, values_in, preferred_element_type=jnp.float32
    )
    row_dot = jnp.sum(probs_full * probs_grad, axis=2, keepdims=True)
    score_grad = (probs_full * (probs_grad - row_dot)).astype(jnp.bfloat16)
    query_grad = (
        jnp.einsum("hqk,khe->qhe", score_grad, keys_in, preferred_element_type=jnp.float32)
        * scale_factor
    )
    key_grad = (
        jnp.einsum("hqk,qhe->khe", score_grad, queries, preferred_element_type=jnp.float32)
        * scale_factor
    )
    value_grad = jnp.einsum(
        "hqk,qhe->khe",
        probs_full.astype(jnp.bfloat16),
        mixed_grad,
        preferred_element_type=jnp.float32,
    )
    return (
        query_grad.astype(jnp.bfloat16),
        key_grad.astype(jnp.bfloat16),
        value_grad.astype(jnp.bfloat16),
    )


def attention_forward(normed_one, packed_weight, bias_pair, shape_heads, rows_count, width_part):
    packed = jnp.einsum(
        "nd,dcf->ncf", normed_one, packed_weight, preferred_element_type=jnp.float32
    )
    queries = (packed[:, 0] + bias_pair[0]).astype(jnp.bfloat16)
    keys_in = packed[:, 1].astype(jnp.bfloat16)
    values_in = (packed[:, 2] + bias_pair[1]).astype(jnp.bfloat16)
    mixture, logsum = lax.map(
        attend,
        (
            queries.reshape(shape_heads),
            keys_in.reshape(shape_heads),
            values_in.reshape(shape_heads),
        ),
    )
    return (queries, keys_in, values_in, logsum, mixture.reshape(rows_count, width_part))


def attention_backward(branch_one, kept_part, output_weight, shape_heads, rows_count, width_part):
    queries, keys_in, values_in, logsum, mixed_rows, normed_one = kept_part
    output_weight_grad = jnp.einsum(
        "nf,nd->fd", mixed_rows, branch_one, preferred_element_type=jnp.float32
    )
    mixed_grad = jnp.einsum(
        "nd,fd->nf", branch_one, output_weight, preferred_element_type=jnp.float32
    ).astype(jnp.bfloat16)
    query_grad, key_grad, value_grad = lax.map(
        attend_back,
        (
            queries.reshape(shape_heads),
            keys_in.reshape(shape_heads),
            values_in.reshape(shape_heads),
            logsum,
            mixed_grad.reshape(shape_heads),
        ),
    )
    query_rows = query_grad.reshape(rows_count, width_part)
    key_rows = key_grad.reshape(rows_count, width_part)
    value_rows = value_grad.reshape(rows_count, width_part)
    packed_grad = jnp.stack([query_rows, key_rows, value_rows], axis=1)
    bias_pair_grad = jnp.stack(
        [
            jnp.sum(query_rows.astype(jnp.float32), axis=0),
            jnp.sum(value_rows.astype(jnp.float32), axis=0),
        ]
    )
    packed_weight_grad = jnp.einsum(
        "nd,ncf->dcf", normed_one, packed_grad, preferred_element_type=jnp.float32
    )
    return (packed_grad, packed_weight_grad, bias_pair_grad, output_weight_grad)


def layer_forward(stream, weights):
    (
        packed_weight,
        bias_pair,
        output_weight,
        output_bias,
        expand_weight,
        expand_bias,
        contract_weight,
        contract_bias,
        gain_first,
        shift_first,
        gain_second,
        shift_second,
    ) = weights
    seq_count, length, width_part = stream.shape
    rows_count = seq_count * length
    shape_heads = (seq_count, length, width_part // HEAD_DIM, HEAD_DIM)
    stream_rows = stream.reshape(rows_count, width_part)
    normed_one, normal_one, inv_one = norm_forward(stream_rows, gain_first, shift_first)
    queries, keys_in, values_in, logsum, mixed_rows = attention_forward(
        normed_one, packed_weight, bias_pair, shape_heads, rows_count, width_part
    )
    residual = (
        stream_rows
        + branch_sum(jnp.dot(mixed_rows, output_weight, preferred_element_type=jnp.float32))
        + output_bias
    )
    normed_two, normal_two, inv_two = norm_forward(residual, gain_second, shift_second)
    hidden_pre = (
        jnp.dot(normed_two, expand_weight, preferred_element_type=jnp.float32) + expand_bias
    )
    hidden = gelu_tanh(hidden_pre).astype(jnp.bfloat16)
    result = (
        residual
        + branch_sum(jnp.dot(hidden, contract_weight, preferred_element_type=jnp.float32))
        + contract_bias
    )
    kept_values = (
        normed_one,
        normal_one,
        inv_one,
        queries,
        keys_in,
        values_in,
        logsum,
        mixed_rows,
        normed_two,
        normal_two,
        inv_two,
        hidden_pre,
        hidden,
    )
    return (result.reshape(stream.shape), kept_values)


def layer_backward(out_grad, kept_values, weights):
    (
        packed_weight,
        bias_pair,
        output_weight,
        output_bias,
        expand_weight,
        expand_bias,
        contract_weight,
        contract_bias,
        gain_first,
        shift_first,
        gain_second,
        shift_second,
    ) = weights
    (
        normed_one,
        normal_one,
        inv_one,
        queries,
        keys_in,
        values_in,
        logsum,
        mixed_rows,
        normed_two,
        normal_two,
        inv_two,
        hidden_pre,
        hidden,
    ) = kept_values
    seq_count, length, width_part = out_grad.shape
    rows_count = seq_count * length
    shape_heads = (seq_count, length, width_part // HEAD_DIM, HEAD_DIM)
    grad_rows = out_grad.reshape(rows_count, width_part)
    contract_bias_grad = jnp.sum(grad_rows, axis=0)
    branch_two = branch_grad(grad_rows)
    contract_weight_grad = jnp.einsum(
        "nf,nd->fd", hidden, branch_two, preferred_element_type=jnp.float32
    )
    hidden_grad = jnp.einsum(
        "nd,fd->nf", branch_two, contract_weight, preferred_element_type=jnp.float32
    )
    pre_grad = jax.vjp(gelu_tanh, hidden_pre)[1](hidden_grad)[0].astype(jnp.bfloat16)
    expand_bias_grad = jnp.sum(pre_grad.astype(jnp.float32), axis=0)
    expand_weight_grad = jnp.einsum(
        "nd,nf->df", normed_two, pre_grad, preferred_element_type=jnp.float32
    )
    second_grad, gain_second_grad, shift_second_grad = norm_backward(
        jnp.einsum("nf,df->nd", pre_grad, expand_weight, preferred_element_type=jnp.float32),
        normal_two,
        inv_two,
        gain_second,
    )
    residual_grad = grad_rows + second_grad
    output_bias_grad = jnp.sum(residual_grad, axis=0)
    branch_one = branch_grad(residual_grad)
    packed_grad, packed_weight_grad, bias_pair_grad, output_weight_grad = attention_backward(
        branch_one,
        (queries, keys_in, values_in, logsum, mixed_rows, normed_one),
        output_weight,
        shape_heads,
        rows_count,
        width_part,
    )
    first_grad, gain_first_grad, shift_first_grad = norm_backward(
        jnp.einsum("ncf,dcf->nd", packed_grad, packed_weight, preferred_element_type=jnp.float32),
        normal_one,
        inv_one,
        gain_first,
    )
    input_grad = (residual_grad + first_grad).reshape(out_grad.shape)
    return (
        input_grad,
        (
            packed_weight_grad,
            bias_pair_grad,
            output_weight_grad,
            output_bias_grad,
            expand_weight_grad,
            expand_bias_grad,
            contract_weight_grad,
            contract_bias_grad,
            gain_first_grad,
            shift_first_grad,
            gain_second_grad,
            shift_second_grad,
        ),
    )


def as_blocks(array, dim, peers):
    before, after = (array.shape[:dim], array.shape[dim + 1 :])
    split = array.reshape(*before, peers, array.shape[dim] // peers, *after)
    return jnp.moveaxis(split, dim, 0).reshape(peers, -1)


def from_blocks(flat, shape, dim, peers):
    block_shape = (*shape[:dim], shape[dim] // peers, *shape[dim + 1 :])
    return flat.reshape(block_shape)


def sum_at_end(grads_zero, grads_last, dims):
    peers = lax.axis_size("dp")
    pieces = [
        jnp.concatenate(
            [as_blocks(g0.astype(jnp.bfloat16), d, peers), as_blocks(g1.astype(jnp.bfloat16), d, peers)]
        )
        for g0, g1, d in zip(grads_zero, grads_last, dims)
    ]
    widths = [p.shape[1] for p in pieces]
    spare = -sum(widths) % 1024
    pieces.append(jnp.zeros((2 * peers, spare), jnp.bfloat16))
    total = lax.psum_scatter(
        jnp.concatenate(pieces, axis=1).reshape(1, -1, 128),
        ("section", "dp"),
        scatter_dimension=1,
        tiled=True,
    ).reshape(1, -1)
    reduced, at = ([], 0)
    for g, d, w in zip(grads_zero, dims, widths):
        piece = total[0, at : at + w].astype(jnp.float32)
        reduced.append(from_blocks(piece, g.shape, d, peers)[None])
        at += w
    return tuple(reduced)


def gather_all(weights, dims):
    peers = lax.axis_size("dp")
    size = sum(w.size for w in weights)
    flat = jnp.concatenate([w.reshape(-1) for w in weights] + [jnp.zeros((-size % 1024,), jnp.bfloat16)])
    every = lax.all_gather(flat[None], ("section", "dp"), axis=0, tiled=True)
    layers = []
    for layer_index in range(every.shape[0] // peers):
        rows = every[layer_index * peers : (layer_index + 1) * peers]
        gathered, at = ([], 0)
        for w, d in zip(weights, dims):
            part = rows[:, at : at + w.size].reshape(peers, *w.shape)
            part = jnp.moveaxis(part, 0, d)
            shape = part.shape
            gathered.append(part.reshape(*shape[:d], shape[d] * shape[d + 1], *shape[d + 2 :]))
            at += w.size
        layers.append(tuple(gathered))
    return layers


def shards(
    inputs,
    cotangent,
    packed_weight,
    bias_pair,
    output_weight,
    output_bias,
    expand_weight,
    expand_bias,
    contract_weight,
    contract_bias,
    gain_first,
    shift_first,
    gain_second,
    shift_second,
):
    dims = (0, 1, 1, 0, 0, 0, 1, 0, 0, 0, 0, 0)
    weights_zero, weights_last = gather_all(
        (
            packed_weight[0],
            bias_pair[0],
            output_weight[0],
            output_bias[0],
            expand_weight[0],
            expand_bias[0],
            contract_weight[0],
            contract_bias[0],
            gain_first[0],
            shift_first[0],
            gain_second[0],
            shift_second[0],
        ),
        dims,
    )
    section_index = lax.axis_index("section")
    is_first = section_index == 0
    stream = lax.dynamic_index_in_dim(inputs, section_index, axis=0, keepdims=False)
    out_grad = lax.dynamic_index_in_dim(cotangent, section_index, axis=0, keepdims=False)
    middle, kept_zero = layer_forward(stream, weights_zero)
    final, kept_last = layer_forward(middle, weights_last)
    swap = [(0, 1), (1, 0)]
    other_out = lax.ppermute(jnp.where(is_first, final, middle), "section", swap)
    middle_grad, grads_last = layer_backward(out_grad, kept_last, weights_last)
    input_grad, grads_zero = layer_backward(middle_grad, kept_zero, weights_zero)
    other_grad = lax.ppermute(jnp.where(is_first, middle_grad, input_grad), "section", swap)
    reduced = sum_at_end(grads_zero, grads_last, dims)
    section_outputs = jnp.where(
        is_first, jnp.stack([middle, other_out]), jnp.stack([other_out, final])
    )[None]
    section_grads = jnp.where(
        is_first, jnp.stack([input_grad, other_grad]), jnp.stack([other_grad, middle_grad])
    )[None]
    return (section_outputs, section_grads) + tuple(reduced)


def solution(mesh):
    in_specs = (
        P(None, "dp", None, "tensor"),
        P(None, "dp", None, "tensor"),
        P("section", "dp", None, "tensor"),
        P("section", None, ("tensor", "dp")),
        P("section", "tensor", "dp"),
        P("section", ("tensor", "dp")),
        P("section", "dp", "tensor"),
        P("section", ("tensor", "dp")),
        P("section", "tensor", "dp"),
        P("section", ("tensor", "dp")),
        P("section", ("tensor", "dp")),
        P("section", ("tensor", "dp")),
        P("section", ("tensor", "dp")),
        P("section", ("tensor", "dp")),
    )
    out_specs = (
        P("section", None, "dp", None, "tensor"),
        P("section", None, "dp", None, "tensor"),
        P("section", "dp", None, "tensor"),
        P("section", None, ("tensor", "dp")),
        P("section", "tensor", "dp"),
        P("section", ("tensor", "dp")),
        P("section", "dp", "tensor"),
        P("section", ("tensor", "dp")),
        P("section", "tensor", "dp"),
        P("section", ("tensor", "dp")),
        P("section", ("tensor", "dp")),
        P("section", ("tensor", "dp")),
        P("section", ("tensor", "dp")),
        P("section", ("tensor", "dp")),
    )
    return jax.shard_map(shards, mesh=mesh, in_specs=in_specs, out_specs=out_specs, check_vma=False)
```

```python
import math

import jax
import jax.numpy as jnp
from jax import lax
from jax.sharding import PartitionSpec as P

HEAD_DIM = 64


epsilon = 1e-05
gelu_coef = math.sqrt(2.0 / math.pi)
masked_value = -1e30
ROW_CHUNKS = 2


def sent_to_all(array, axis):
    copies = jnp.broadcast_to(array, (lax.axis_size(axis), *array.shape))
    return lax.all_to_all(copies, axis, split_axis=0, concat_axis=0, tiled=True)


def taken_together(array, axis):
    return sent_to_all(array, axis).sum(axis=0)


def in_one(arrays, axis):
    ends = [0]
    for a in arrays:
        ends.append(ends[-1] + a.size)
    subtotal = taken_together(jnp.concatenate([a.ravel() for a in arrays]), axis)
    return tuple((subtotal[b:e].reshape(a.shape) for a, b, e in zip(arrays, ends, ends[1:])))


def joined_along(parts, dim):
    parts = jnp.moveaxis(parts, 0, dim)
    shape = parts.shape
    return parts.reshape(*shape[:dim], shape[dim] * shape[dim + 1], *shape[dim + 2 :])


def collect(array, axis, dim):
    parts = sent_to_all(array, axis)
    return joined_along(parts, dim)


def in_blocks(array, dim, peers):
    before, after = (array.shape[:dim], array.shape[dim + 1 :])
    return jnp.moveaxis(array.reshape(*before, peers, -1, *after), dim, 0)


def summed_on_arrival(array, axis, dim):
    parts = in_blocks(array, dim, lax.axis_size(axis))
    arrived = lax.all_to_all(parts, axis, split_axis=0, concat_axis=0, tiled=True)
    return arrived.astype(jnp.float32).sum(axis=0)


def side_by_side(arrays, axis, dim, along):
    both = jnp.concatenate(arrays, axis=along)
    result, at, gathered = (lax.psum_scatter(both, axis, scatter_dimension=dim, tiled=True), 0, [])
    for a in arrays:
        gathered.append(lax.slice_in_dim(result, at, at + a.shape[along], axis=along))
        at += a.shape[along]
    return tuple(gathered)


def in_one_piece(arrays, axis, dim, along):
    both = jnp.concatenate(arrays, axis=along)
    result, at, gathered = (lax.all_gather(both, axis, axis=dim, tiled=True), 0, [])
    for a in arrays:
        gathered.append(lax.slice_in_dim(result, at, at + a.shape[along], axis=along))
        at += a.shape[along]
    return tuple(gathered)


def from_behind(array, axis, by):
    peers = lax.axis_size(axis)
    pairs = [(i, i + by) for i in range(peers) if 0 <= i + by < peers]
    return lax.ppermute(array, axis, pairs)


def gelu_tanh(values):
    return (
        0.5 * values * (1.0 + jnp.tanh(gelu_coef * (values + 0.044715 * values * values * values)))
    )


def norm_forward(stream, gain, offset):
    width_all = stream.shape[1] * lax.axis_size("tensor")
    totals, squares = in_one((jnp.sum(stream, axis=1), jnp.sum(stream * stream, axis=1)), "tensor")
    mean_row = (totals / width_all)[:, None]
    var_row = (squares / width_all)[:, None] - mean_row * mean_row
    inv_scale = lax.rsqrt(var_row + epsilon)
    normal_part = (stream - mean_row) * inv_scale
    normed = (normal_part * gain + offset).astype(jnp.bfloat16)
    return (collect(normed, "tensor", 1), normal_part, inv_scale)


def norm_backward(partial_term, normal_part, inv_scale, gain):
    width_all = partial_term.shape[1]
    d_normed = summed_on_arrival(partial_term.astype(jnp.bfloat16), "tensor", 1)
    gain_grad = jnp.sum(d_normed * normal_part, axis=0)
    offset_grad = jnp.sum(d_normed, axis=0)
    scaled = d_normed * gain
    first_sum, second_sum = in_one(
        (jnp.sum(scaled, axis=1), jnp.sum(scaled * normal_part, axis=1)), "tensor"
    )
    stream_grad = inv_scale * (
        scaled - first_sum[:, None] / width_all - normal_part * second_sum[:, None] / width_all
    )
    return (stream_grad, gain_grad, offset_grad)


def branch_sum(partial_term):
    return summed_on_arrival(partial_term.astype(jnp.bfloat16), "tensor", 1)


def branch_grad(stream_grad):
    return collect(stream_grad.astype(jnp.bfloat16), "tensor", 1)


def causal_scores(queries, keys_in):
    length = queries.shape[0]
    scale_factor = queries.shape[2] ** (-0.5)
    scores = (
        jnp.einsum("qhe,khe->hqk", queries, keys_in, preferred_element_type=jnp.float32)
        * scale_factor
    )
    causal = lax.broadcasted_iota(jnp.int32, (length, length), 0) >= lax.broadcasted_iota(
        jnp.int32, (length, length), 1
    )
    return (jnp.where(causal[None], scores, masked_value), scale_factor)


def attend(operands):
    queries, keys_in, values_in = operands
    masked, scale_factor = causal_scores(queries, keys_in)
    highest = jnp.max(masked, axis=2, keepdims=True)
    logsum = highest + jnp.log(jnp.sum(jnp.exp(masked - highest), axis=2, keepdims=True))
    weights_low = jnp.exp(masked - logsum).astype(jnp.bfloat16)
    mixture = jnp.einsum("hqk,khe->qhe", weights_low, values_in, preferred_element_type=jnp.float32)
    return (mixture.astype(jnp.bfloat16), logsum[:, :, 0])


def attend_back(operands):
    queries, keys_in, values_in, logsum, mixed_grad = operands
    masked, scale_factor = causal_scores(queries, keys_in)
    probs_full = jnp.exp(masked - logsum[:, :, None])
    probs_grad = jnp.einsum(
        "qhe,khe->hqk", mixed_grad, values_in, preferred_element_type=jnp.float32
    )
    row_dot = jnp.sum(probs_full * probs_grad, axis=2, keepdims=True)
    score_grad = (probs_full * (probs_grad - row_dot)).astype(jnp.bfloat16)
    query_grad = (
        jnp.einsum("hqk,khe->qhe", score_grad, keys_in, preferred_element_type=jnp.float32)
        * scale_factor
    )
    key_grad = (
        jnp.einsum("hqk,qhe->khe", score_grad, queries, preferred_element_type=jnp.float32)
        * scale_factor
    )
    value_grad = jnp.einsum(
        "hqk,qhe->khe",
        probs_full.astype(jnp.bfloat16),
        mixed_grad,
        preferred_element_type=jnp.float32,
    )
    return (
        query_grad.astype(jnp.bfloat16),
        key_grad.astype(jnp.bfloat16),
        value_grad.astype(jnp.bfloat16),
    )


def attention_forward(normed_one, packed_weight, bias_pair, shape_heads, rows_count, width_part):
    packed = jnp.einsum(
        "nd,dcf->ncf", normed_one, packed_weight, preferred_element_type=jnp.float32
    )
    queries = (packed[:, 0] + bias_pair[0]).astype(jnp.bfloat16)
    keys_in = packed[:, 1].astype(jnp.bfloat16)
    values_in = (packed[:, 2] + bias_pair[1]).astype(jnp.bfloat16)
    mixture, logsum = lax.map(
        attend,
        (
            queries.reshape(shape_heads),
            keys_in.reshape(shape_heads),
            values_in.reshape(shape_heads),
        ),
    )
    return (queries, keys_in, values_in, logsum, mixture.reshape(rows_count, width_part))


def attention_backward(branch_one, kept_part, output_weight, shape_heads, rows_count, width_part):
    queries, keys_in, values_in, logsum, mixed_rows, normed_one = kept_part
    output_weight_grad = jnp.einsum(
        "nf,nd->fd", mixed_rows, branch_one, preferred_element_type=jnp.float32
    )
    mixed_grad = jnp.einsum(
        "nd,fd->nf", branch_one, output_weight, preferred_element_type=jnp.float32
    ).astype(jnp.bfloat16)
    query_grad, key_grad, value_grad = lax.map(
        attend_back,
        (
            queries.reshape(shape_heads),
            keys_in.reshape(shape_heads),
            values_in.reshape(shape_heads),
            logsum,
            mixed_grad.reshape(shape_heads),
        ),
    )
    query_rows = query_grad.reshape(rows_count, width_part)
    key_rows = key_grad.reshape(rows_count, width_part)
    value_rows = value_grad.reshape(rows_count, width_part)
    packed_grad = jnp.stack([query_rows, key_rows, value_rows], axis=1)
    bias_pair_grad = jnp.stack(
        [
            jnp.sum(query_rows.astype(jnp.float32), axis=0),
            jnp.sum(value_rows.astype(jnp.float32), axis=0),
        ]
    )
    packed_weight_grad = jnp.einsum(
        "nd,ncf->dcf", normed_one, packed_grad, preferred_element_type=jnp.float32
    )
    return (packed_grad, packed_weight_grad, bias_pair_grad, output_weight_grad)


def split_rows(array, parts):
    cut = array.shape[0] // parts
    return [array[i * cut : (i + 1) * cut] for i in range(parts)]


def joined(arrays):
    return jnp.concatenate(arrays, axis=0)


def layer_forward(stream, weights):
    (
        packed_weight,
        bias_pair,
        output_weight,
        output_bias,
        expand_weight,
        expand_bias,
        contract_weight,
        contract_bias,
        gain_first,
        shift_first,
        gain_second,
        shift_second,
    ) = weights
    seq_count, length, width_part = stream.shape
    rows_count = seq_count * length
    shape_heads = (seq_count, length, width_part // HEAD_DIM, HEAD_DIM)
    pieces = split_rows(stream.reshape(rows_count, width_part), ROW_CHUNKS)
    firsts = [norm_forward(piece, gain_first, shift_first) for piece in pieces]
    packs = [
        jnp.einsum("nd,dcf->ncf", first[0], packed_weight, preferred_element_type=jnp.float32)
        for first in firsts
    ]
    queries = joined([(pack[:, 0] + bias_pair[0]).astype(jnp.bfloat16) for pack in packs])
    keys_in = joined([pack[:, 1].astype(jnp.bfloat16) for pack in packs])
    values_in = joined([(pack[:, 2] + bias_pair[1]).astype(jnp.bfloat16) for pack in packs])
    mixture, logsum = lax.map(
        attend,
        (
            queries.reshape(shape_heads),
            keys_in.reshape(shape_heads),
            values_in.reshape(shape_heads),
        ),
    )
    mixed_rows = mixture.reshape(rows_count, width_part)
    results, seconds = ([], [])
    for piece, mixed in zip(pieces, split_rows(mixed_rows, ROW_CHUNKS)):
        residual = (
            piece
            + branch_sum(jnp.dot(mixed, output_weight, preferred_element_type=jnp.float32))
            + output_bias
        )
        normed_two, normal_two, inv_two = norm_forward(residual, gain_second, shift_second)
        hidden_pre = (
            jnp.dot(normed_two, expand_weight, preferred_element_type=jnp.float32) + expand_bias
        )
        hidden = gelu_tanh(hidden_pre).astype(jnp.bfloat16)
        results.append(
            residual
            + branch_sum(jnp.dot(hidden, contract_weight, preferred_element_type=jnp.float32))
            + contract_bias
        )
        seconds.append((normed_two, normal_two, inv_two, hidden_pre, hidden))
    kept_values = (
        joined([first[0] for first in firsts]),
        joined([first[1] for first in firsts]),
        joined([first[2] for first in firsts]),
        queries,
        keys_in,
        values_in,
        logsum,
        mixed_rows,
    ) + tuple(joined([second[i] for second in seconds]) for i in range(5))
    return (joined(results).reshape(stream.shape), kept_values)


def layer_backward(out_grad, kept_values, weights):
    (
        packed_weight,
        bias_pair,
        output_weight,
        output_bias,
        expand_weight,
        expand_bias,
        contract_weight,
        contract_bias,
        gain_first,
        shift_first,
        gain_second,
        shift_second,
    ) = weights
    (
        normed_one,
        normal_one,
        inv_one,
        queries,
        keys_in,
        values_in,
        logsum,
        mixed_rows,
        normed_two,
        normal_two,
        inv_two,
        hidden_pre,
        hidden,
    ) = kept_values
    seq_count, length, width_part = out_grad.shape
    rows_count = seq_count * length
    shape_heads = (seq_count, length, width_part // HEAD_DIM, HEAD_DIM)
    grad_rows = out_grad.reshape(rows_count, width_part)
    contract_bias_grad = jnp.sum(grad_rows, axis=0)
    parts = [split_rows(a, ROW_CHUNKS) for a in (grad_rows, hidden_pre, normal_two, inv_two)]
    branch_twos, pre_grads, residual_grads, branch_ones, mixed_grads = ([], [], [], [], [])
    gain_second_grad, shift_second_grad = (0.0, 0.0)
    for grad_part, pre_part, normal_part, inv_part in zip(*parts):
        branch_two = branch_grad(grad_part)
        hidden_grad = jnp.einsum(
            "nd,fd->nf", branch_two, contract_weight, preferred_element_type=jnp.float32
        )
        pre_grad = jax.vjp(gelu_tanh, pre_part)[1](hidden_grad)[0].astype(jnp.bfloat16)
        second_grad, gain_part, shift_part = norm_backward(
            jnp.einsum("nf,df->nd", pre_grad, expand_weight, preferred_element_type=jnp.float32),
            normal_part,
            inv_part,
            gain_second,
        )
        residual_grad = grad_part + second_grad
        branch_one = branch_grad(residual_grad)
        mixed_grads.append(
            jnp.einsum(
                "nd,fd->nf", branch_one, output_weight, preferred_element_type=jnp.float32
            ).astype(jnp.bfloat16)
        )
        branch_twos.append(branch_two)
        pre_grads.append(pre_grad)
        residual_grads.append(residual_grad)
        branch_ones.append(branch_one)
        gain_second_grad = gain_second_grad + gain_part
        shift_second_grad = shift_second_grad + shift_part
    contract_weight_grad = jnp.einsum(
        "nf,nd->fd", hidden, joined(branch_twos), preferred_element_type=jnp.float32
    )
    pre_grad = joined(pre_grads)
    expand_bias_grad = jnp.sum(pre_grad.astype(jnp.float32), axis=0)
    expand_weight_grad = jnp.einsum(
        "nd,nf->df", normed_two, pre_grad, preferred_element_type=jnp.float32
    )
    output_bias_grad = jnp.sum(joined(residual_grads), axis=0)
    output_weight_grad = jnp.einsum(
        "nf,nd->fd", mixed_rows, joined(branch_ones), preferred_element_type=jnp.float32
    )
    mixed_grad = joined(mixed_grads)
    query_grad, key_grad, value_grad = lax.map(
        attend_back,
        (
            queries.reshape(shape_heads),
            keys_in.reshape(shape_heads),
            values_in.reshape(shape_heads),
            logsum,
            mixed_grad.reshape(shape_heads),
        ),
    )
    query_rows = query_grad.reshape(rows_count, width_part)
    key_rows = key_grad.reshape(rows_count, width_part)
    value_rows = value_grad.reshape(rows_count, width_part)
    packed_grad = jnp.stack([query_rows, key_rows, value_rows], axis=1)
    bias_pair_grad = jnp.stack(
        [
            jnp.sum(query_rows.astype(jnp.float32), axis=0),
            jnp.sum(value_rows.astype(jnp.float32), axis=0),
        ]
    )
    packed_weight_grad = jnp.einsum(
        "nd,ncf->dcf", normed_one, packed_grad, preferred_element_type=jnp.float32
    )
    input_grads = []
    gain_first_grad, shift_first_grad = (0.0, 0.0)
    for packed_part, normal_part, inv_part, residual_grad in zip(
        split_rows(packed_grad, ROW_CHUNKS),
        split_rows(normal_one, ROW_CHUNKS),
        split_rows(inv_one, ROW_CHUNKS),
        residual_grads,
    ):
        first_grad, gain_part, shift_part = norm_backward(
            jnp.einsum(
                "ncf,dcf->nd", packed_part, packed_weight, preferred_element_type=jnp.float32
            ),
            normal_part,
            inv_part,
            gain_first,
        )
        input_grads.append(residual_grad + first_grad)
        gain_first_grad = gain_first_grad + gain_part
        shift_first_grad = shift_first_grad + shift_part
    input_grad = joined(input_grads).reshape(out_grad.shape)
    return (
        input_grad,
        (
            packed_weight_grad,
            bias_pair_grad,
            output_weight_grad,
            output_bias_grad,
            expand_weight_grad,
            expand_bias_grad,
            contract_weight_grad,
            contract_bias_grad,
            gain_first_grad,
            shift_first_grad,
            gain_second_grad,
            shift_second_grad,
        ),
    )


def as_blocks(array, dim, peers):
    before, after = (array.shape[:dim], array.shape[dim + 1 :])
    split = array.reshape(*before, peers, array.shape[dim] // peers, *after)
    return jnp.moveaxis(split, dim, 0).reshape(peers, -1)


def from_blocks(flat, shape, dim, peers):
    block_shape = (*shape[:dim], shape[dim] // peers, *shape[dim + 1 :])
    return flat.reshape(block_shape)


def sum_at_end(grads_zero, grads_last, dims):
    peers = lax.axis_size("dp")
    pieces = [
        jnp.concatenate(
            [as_blocks(g0.astype(jnp.bfloat16), d, peers), as_blocks(g1.astype(jnp.bfloat16), d, peers)]
        )
        for g0, g1, d in zip(grads_zero, grads_last, dims)
    ]
    widths = [p.shape[1] for p in pieces]
    spare = -sum(widths) % 1024
    pieces.append(jnp.zeros((2 * peers, spare), jnp.bfloat16))
    total = lax.psum_scatter(
        jnp.concatenate(pieces, axis=1).reshape(1, -1, 128),
        ("section", "dp"),
        scatter_dimension=1,
        tiled=True,
    ).reshape(1, -1)
    reduced, at = ([], 0)
    for g, d, w in zip(grads_zero, dims, widths):
        piece = total[0, at : at + w].astype(jnp.float32)
        reduced.append(from_blocks(piece, g.shape, d, peers)[None])
        at += w
    return tuple(reduced)


def gather_all(weights, dims):
    peers = lax.axis_size("dp")
    size = sum(w.size for w in weights)
    flat = jnp.concatenate([w.reshape(-1) for w in weights] + [jnp.zeros((-size % 1024,), jnp.bfloat16)])
    every = lax.all_gather(flat[None], ("section", "dp"), axis=0, tiled=True)
    layers = []
    for layer_index in range(every.shape[0] // peers):
        rows = every[layer_index * peers : (layer_index + 1) * peers]
        gathered, at = ([], 0)
        for w, d in zip(weights, dims):
            part = rows[:, at : at + w.size].reshape(peers, *w.shape)
            part = jnp.moveaxis(part, 0, d)
            shape = part.shape
            gathered.append(part.reshape(*shape[:d], shape[d] * shape[d + 1], *shape[d + 2 :]))
            at += w.size
        layers.append(tuple(gathered))
    return layers


def shards(
    inputs,
    cotangent,
    packed_weight,
    bias_pair,
    output_weight,
    output_bias,
    expand_weight,
    expand_bias,
    contract_weight,
    contract_bias,
    gain_first,
    shift_first,
    gain_second,
    shift_second,
):
    dims = (0, 1, 1, 0, 0, 0, 1, 0, 0, 0, 0, 0)
    weights_zero, weights_last = gather_all(
        (
            packed_weight[0],
            bias_pair[0],
            output_weight[0],
            output_bias[0],
            expand_weight[0],
            expand_bias[0],
            contract_weight[0],
            contract_bias[0],
            gain_first[0],
            shift_first[0],
            gain_second[0],
            shift_second[0],
        ),
        dims,
    )
    section_index = lax.axis_index("section")
    is_first = section_index == 0
    stream = lax.dynamic_index_in_dim(inputs, section_index, axis=0, keepdims=False)
    out_grad = lax.dynamic_index_in_dim(cotangent, section_index, axis=0, keepdims=False)
    middle, kept_zero = layer_forward(stream, weights_zero)
    final, kept_last = layer_forward(middle, weights_last)
    swap = [(0, 1), (1, 0)]
    other_out = lax.ppermute(jnp.where(is_first, final, middle), "section", swap)
    middle_grad, grads_last = layer_backward(out_grad, kept_last, weights_last)
    input_grad, grads_zero = layer_backward(middle_grad, kept_zero, weights_zero)
    other_grad = lax.ppermute(jnp.where(is_first, middle_grad, input_grad), "section", swap)
    reduced = sum_at_end(grads_zero, grads_last, dims)
    section_outputs = jnp.where(
        is_first, jnp.stack([middle, other_out]), jnp.stack([other_out, final])
    )[None]
    section_grads = jnp.where(
        is_first, jnp.stack([input_grad, other_grad]), jnp.stack([other_grad, middle_grad])
    )[None]
    return (section_outputs, section_grads) + tuple(reduced)


def solution(mesh):
    in_specs = (
        P(None, "dp", None, "tensor"),
        P(None, "dp", None, "tensor"),
        P("section", "dp", None, "tensor"),
        P("section", None, ("tensor", "dp")),
        P("section", "tensor", "dp"),
        P("section", ("tensor", "dp")),
        P("section", "dp", "tensor"),
        P("section", ("tensor", "dp")),
        P("section", "tensor", "dp"),
        P("section", ("tensor", "dp")),
        P("section", ("tensor", "dp")),
        P("section", ("tensor", "dp")),
        P("section", ("tensor", "dp")),
        P("section", ("tensor", "dp")),
    )
    out_specs = (
        P("section", None, "dp", None, "tensor"),
        P("section", None, "dp", None, "tensor"),
        P("section", "dp", None, "tensor"),
        P("section", None, ("tensor", "dp")),
        P("section", "tensor", "dp"),
        P("section", ("tensor", "dp")),
        P("section", "dp", "tensor"),
        P("section", ("tensor", "dp")),
        P("section", "tensor", "dp"),
        P("section", ("tensor", "dp")),
        P("section", ("tensor", "dp")),
        P("section", ("tensor", "dp")),
        P("section", ("tensor", "dp")),
        P("section", ("tensor", "dp")),
    )
    return jax.shard_map(shards, mesh=mesh, in_specs=in_specs, out_specs=out_specs, check_vma=False)
```

```python
import math

import jax
import jax.numpy as jnp
from jax import lax
from jax.sharding import PartitionSpec as P

HEAD_DIM = 64


epsilon = 1e-05
gelu_coef = math.sqrt(2.0 / math.pi)
masked_value = -1e30


def sent_to_all(array, axis):
    copies = jnp.broadcast_to(array, (lax.axis_size(axis), *array.shape))
    return lax.all_to_all(copies, axis, split_axis=0, concat_axis=0, tiled=True)


def taken_together(array, axis):
    return sent_to_all(array, axis).sum(axis=0)


def in_one(arrays, axis):
    ends = [0]
    for a in arrays:
        ends.append(ends[-1] + a.size)
    subtotal = taken_together(jnp.concatenate([a.ravel() for a in arrays]), axis)
    return tuple((subtotal[b:e].reshape(a.shape) for a, b, e in zip(arrays, ends, ends[1:])))


def joined_along(parts, dim):
    parts = jnp.moveaxis(parts, 0, dim)
    shape = parts.shape
    return parts.reshape(*shape[:dim], shape[dim] * shape[dim + 1], *shape[dim + 2 :])


def collect(array, axis, dim):
    parts = sent_to_all(array, axis)
    return joined_along(parts, dim)


def in_blocks(array, dim, peers):
    before, after = (array.shape[:dim], array.shape[dim + 1 :])
    return jnp.moveaxis(array.reshape(*before, peers, -1, *after), dim, 0)


def summed_on_arrival(array, axis, dim):
    parts = in_blocks(array, dim, lax.axis_size(axis))
    arrived = lax.all_to_all(parts, axis, split_axis=0, concat_axis=0, tiled=True)
    return arrived.astype(jnp.float32).sum(axis=0)


def side_by_side(arrays, axis, dim, along):
    both = jnp.concatenate(arrays, axis=along)
    result, at, gathered = (lax.psum_scatter(both, axis, scatter_dimension=dim, tiled=True), 0, [])
    for a in arrays:
        gathered.append(lax.slice_in_dim(result, at, at + a.shape[along], axis=along))
        at += a.shape[along]
    return tuple(gathered)


def in_one_piece(arrays, axis, dim, along):
    both = jnp.concatenate(arrays, axis=along)
    result, at, gathered = (lax.all_gather(both, axis, axis=dim, tiled=True), 0, [])
    for a in arrays:
        gathered.append(lax.slice_in_dim(result, at, at + a.shape[along], axis=along))
        at += a.shape[along]
    return tuple(gathered)


def from_behind(array, axis, by):
    peers = lax.axis_size(axis)
    pairs = [(i, i + by) for i in range(peers) if 0 <= i + by < peers]
    return lax.ppermute(array, axis, pairs)


def gelu_tanh(values):
    return (
        0.5 * values * (1.0 + jnp.tanh(gelu_coef * (values + 0.044715 * values * values * values)))
    )


def norm_forward(stream, gain_full, offset_full):
    full = collect(stream, "tensor", 1)
    mean_row = jnp.mean(full, axis=1, keepdims=True)
    var_row = jnp.mean(full * full, axis=1, keepdims=True) - mean_row * mean_row
    inv_scale = lax.rsqrt(var_row + epsilon)
    normed = ((full - mean_row) * inv_scale * gain_full + offset_full).astype(jnp.bfloat16)
    normal_part = (stream - mean_row) * inv_scale
    return (normed, normal_part, inv_scale)


def norm_backward(partial_term, normal_part, inv_scale, gain):
    width_all = partial_term.shape[1]
    d_normed = summed_on_arrival(partial_term.astype(jnp.bfloat16), "tensor", 1)
    gain_grad = jnp.sum(d_normed * normal_part, axis=0)
    offset_grad = jnp.sum(d_normed, axis=0)
    scaled = d_normed * gain
    first_sum, second_sum = in_one(
        (jnp.sum(scaled, axis=1), jnp.sum(scaled * normal_part, axis=1)), "tensor"
    )
    stream_grad = inv_scale * (
        scaled - first_sum[:, None] / width_all - normal_part * second_sum[:, None] / width_all
    )
    return (stream_grad, gain_grad, offset_grad)


def branch_sum(partial_term):
    return summed_on_arrival(partial_term.astype(jnp.bfloat16), "tensor", 1)


def branch_grad(stream_grad):
    return collect(stream_grad.astype(jnp.bfloat16), "tensor", 1)


def causal_scores(queries, keys_in):
    length = queries.shape[0]
    scale_factor = queries.shape[2] ** (-0.5)
    scores = (
        jnp.einsum("qhe,khe->hqk", queries, keys_in, preferred_element_type=jnp.float32)
        * scale_factor
    )
    causal = lax.broadcasted_iota(jnp.int32, (length, length), 0) >= lax.broadcasted_iota(
        jnp.int32, (length, length), 1
    )
    return (jnp.where(causal[None], scores, masked_value), scale_factor)


def attend(operands):
    queries, keys_in, values_in = operands
    masked, scale_factor = causal_scores(queries, keys_in)
    highest = jnp.max(masked, axis=2, keepdims=True)
    logsum = highest + jnp.log(jnp.sum(jnp.exp(masked - highest), axis=2, keepdims=True))
    weights_low = jnp.exp(masked - logsum).astype(jnp.bfloat16)
    mixture = jnp.einsum("hqk,khe->qhe", weights_low, values_in, preferred_element_type=jnp.float32)
    return (mixture.astype(jnp.bfloat16), logsum[:, :, 0])


def attend_back(operands):
    queries, keys_in, values_in, logsum, mixed_grad = operands
    masked, scale_factor = causal_scores(queries, keys_in)
    probs_full = jnp.exp(masked - logsum[:, :, None])
    probs_grad = jnp.einsum(
        "qhe,khe->hqk", mixed_grad, values_in, preferred_element_type=jnp.float32
    )
    row_dot = jnp.sum(probs_full * probs_grad, axis=2, keepdims=True)
    score_grad = (probs_full * (probs_grad - row_dot)).astype(jnp.bfloat16)
    query_grad = (
        jnp.einsum("hqk,khe->qhe", score_grad, keys_in, preferred_element_type=jnp.float32)
        * scale_factor
    )
    key_grad = (
        jnp.einsum("hqk,qhe->khe", score_grad, queries, preferred_element_type=jnp.float32)
        * scale_factor
    )
    value_grad = jnp.einsum(
        "hqk,qhe->khe",
        probs_full.astype(jnp.bfloat16),
        mixed_grad,
        preferred_element_type=jnp.float32,
    )
    return (
        query_grad.astype(jnp.bfloat16),
        key_grad.astype(jnp.bfloat16),
        value_grad.astype(jnp.bfloat16),
    )


def attention_forward(normed_one, packed_weight, bias_pair, shape_heads, rows_count, width_part):
    packed = jnp.einsum(
        "nd,dcf->ncf", normed_one, packed_weight, preferred_element_type=jnp.float32
    )
    queries = (packed[:, 0] + bias_pair[0]).astype(jnp.bfloat16)
    keys_in = packed[:, 1].astype(jnp.bfloat16)
    values_in = (packed[:, 2] + bias_pair[1]).astype(jnp.bfloat16)
    mixture, logsum = lax.map(
        attend,
        (
            queries.reshape(shape_heads),
            keys_in.reshape(shape_heads),
            values_in.reshape(shape_heads),
        ),
    )
    return (queries, keys_in, values_in, logsum, mixture.reshape(rows_count, width_part))


def attention_backward(branch_one, kept_part, output_weight, shape_heads, rows_count, width_part):
    queries, keys_in, values_in, logsum, mixed_rows, normed_one = kept_part
    output_weight_grad = jnp.einsum(
        "nf,nd->fd", mixed_rows, branch_one, preferred_element_type=jnp.float32
    )
    mixed_grad = jnp.einsum(
        "nd,fd->nf", branch_one, output_weight, preferred_element_type=jnp.float32
    ).astype(jnp.bfloat16)
    query_grad, key_grad, value_grad = lax.map(
        attend_back,
        (
            queries.reshape(shape_heads),
            keys_in.reshape(shape_heads),
            values_in.reshape(shape_heads),
            logsum,
            mixed_grad.reshape(shape_heads),
        ),
    )
    query_rows = query_grad.reshape(rows_count, width_part)
    key_rows = key_grad.reshape(rows_count, width_part)
    value_rows = value_grad.reshape(rows_count, width_part)
    packed_grad = jnp.stack([query_rows, key_rows, value_rows], axis=1)
    bias_pair_grad = jnp.stack(
        [
            jnp.sum(query_rows.astype(jnp.float32), axis=0),
            jnp.sum(value_rows.astype(jnp.float32), axis=0),
        ]
    )
    packed_weight_grad = jnp.einsum(
        "nd,ncf->dcf", normed_one, packed_grad, preferred_element_type=jnp.float32
    )
    return (packed_grad, packed_weight_grad, bias_pair_grad, output_weight_grad)


def layer_forward(stream, weights, full_norms):
    (
        packed_weight,
        bias_pair,
        output_weight,
        output_bias,
        expand_weight,
        expand_bias,
        contract_weight,
        contract_bias,
        gain_first,
        shift_first,
        gain_second,
        shift_second,
    ) = weights
    seq_count, length, width_part = stream.shape
    rows_count = seq_count * length
    shape_heads = (seq_count, length, width_part // HEAD_DIM, HEAD_DIM)
    stream_rows = stream.reshape(rows_count, width_part)
    normed_one, normal_one, inv_one = norm_forward(stream_rows, full_norms[0], full_norms[1])
    queries, keys_in, values_in, logsum, mixed_rows = attention_forward(
        normed_one, packed_weight, bias_pair, shape_heads, rows_count, width_part
    )
    residual = (
        stream_rows
        + branch_sum(jnp.dot(mixed_rows, output_weight, preferred_element_type=jnp.float32))
        + output_bias
    )
    normed_two, normal_two, inv_two = norm_forward(residual, full_norms[2], full_norms[3])
    hidden_pre = (
        jnp.dot(normed_two, expand_weight, preferred_element_type=jnp.float32) + expand_bias
    )
    hidden = gelu_tanh(hidden_pre).astype(jnp.bfloat16)
    result = (
        residual
        + branch_sum(jnp.dot(hidden, contract_weight, preferred_element_type=jnp.float32))
        + contract_bias
    )
    kept_values = (
        normed_one,
        normal_one,
        inv_one,
        queries,
        keys_in,
        values_in,
        logsum,
        mixed_rows,
        normed_two,
        normal_two,
        inv_two,
        hidden_pre,
        hidden,
    )
    return (result.reshape(stream.shape), kept_values)


def layer_backward(out_grad, kept_values, weights):
    (
        packed_weight,
        bias_pair,
        output_weight,
        output_bias,
        expand_weight,
        expand_bias,
        contract_weight,
        contract_bias,
        gain_first,
        shift_first,
        gain_second,
        shift_second,
    ) = weights
    (
        normed_one,
        normal_one,
        inv_one,
        queries,
        keys_in,
        values_in,
        logsum,
        mixed_rows,
        normed_two,
        normal_two,
        inv_two,
        hidden_pre,
        hidden,
    ) = kept_values
    seq_count, length, width_part = out_grad.shape
    rows_count = seq_count * length
    shape_heads = (seq_count, length, width_part // HEAD_DIM, HEAD_DIM)
    grad_rows = out_grad.reshape(rows_count, width_part)
    contract_bias_grad = jnp.sum(grad_rows, axis=0)
    branch_two = branch_grad(grad_rows)
    contract_weight_grad = jnp.einsum(
        "nf,nd->fd", hidden, branch_two, preferred_element_type=jnp.float32
    )
    hidden_grad = jnp.einsum(
        "nd,fd->nf", branch_two, contract_weight, preferred_element_type=jnp.float32
    )
    pre_grad = jax.vjp(gelu_tanh, hidden_pre)[1](hidden_grad)[0].astype(jnp.bfloat16)
    expand_bias_grad = jnp.sum(pre_grad.astype(jnp.float32), axis=0)
    expand_weight_grad = jnp.einsum(
        "nd,nf->df", normed_two, pre_grad, preferred_element_type=jnp.float32
    )
    second_grad, gain_second_grad, shift_second_grad = norm_backward(
        jnp.einsum("nf,df->nd", pre_grad, expand_weight, preferred_element_type=jnp.float32),
        normal_two,
        inv_two,
        gain_second,
    )
    residual_grad = grad_rows + second_grad
    output_bias_grad = jnp.sum(residual_grad, axis=0)
    branch_one = branch_grad(residual_grad)
    packed_grad, packed_weight_grad, bias_pair_grad, output_weight_grad = attention_backward(
        branch_one,
        (queries, keys_in, values_in, logsum, mixed_rows, normed_one),
        output_weight,
        shape_heads,
        rows_count,
        width_part,
    )
    first_grad, gain_first_grad, shift_first_grad = norm_backward(
        jnp.einsum("ncf,dcf->nd", packed_grad, packed_weight, preferred_element_type=jnp.float32),
        normal_one,
        inv_one,
        gain_first,
    )
    input_grad = (residual_grad + first_grad).reshape(out_grad.shape)
    return (
        input_grad,
        (
            packed_weight_grad,
            bias_pair_grad,
            output_weight_grad,
            output_bias_grad,
            expand_weight_grad,
            expand_bias_grad,
            contract_weight_grad,
            contract_bias_grad,
            gain_first_grad,
            shift_first_grad,
            gain_second_grad,
            shift_second_grad,
        ),
    )


def as_blocks(array, dim, peers):
    before, after = (array.shape[:dim], array.shape[dim + 1 :])
    split = array.reshape(*before, peers, array.shape[dim] // peers, *after)
    return jnp.moveaxis(split, dim, 0).reshape(peers, -1)


def from_blocks(flat, shape, dim, peers):
    block_shape = (*shape[:dim], shape[dim] // peers, *shape[dim + 1 :])
    return flat.reshape(block_shape)


def sum_at_end(grads_zero, grads_last, dims):
    peers = lax.axis_size("dp")
    pieces = [
        jnp.concatenate(
            [as_blocks(g0.astype(jnp.bfloat16), d, peers), as_blocks(g1.astype(jnp.bfloat16), d, peers)]
        )
        for g0, g1, d in zip(grads_zero, grads_last, dims)
    ]
    widths = [p.shape[1] for p in pieces]
    spare = -sum(widths) % 1024
    pieces.append(jnp.zeros((2 * peers, spare), jnp.bfloat16))
    total = lax.psum_scatter(
        jnp.concatenate(pieces, axis=1).reshape(1, -1, 128),
        ("section", "dp"),
        scatter_dimension=1,
        tiled=True,
    ).reshape(1, -1)
    reduced, at = ([], 0)
    for g, d, w in zip(grads_zero, dims, widths):
        piece = total[0, at : at + w].astype(jnp.float32)
        reduced.append(from_blocks(piece, g.shape, d, peers)[None])
        at += w
    return tuple(reduced)


def gather_all(weights, dims):
    peers = lax.axis_size("dp")
    size = sum(w.size for w in weights)
    flat = jnp.concatenate([w.reshape(-1) for w in weights] + [jnp.zeros((-size % 1024,), jnp.bfloat16)])
    every = lax.all_gather(flat[None], ("section", "dp"), axis=0, tiled=True)
    layers = []
    for layer_index in range(every.shape[0] // peers):
        rows = every[layer_index * peers : (layer_index + 1) * peers]
        gathered, at = ([], 0)
        for w, d in zip(weights, dims):
            part = rows[:, at : at + w.size].reshape(peers, *w.shape)
            part = jnp.moveaxis(part, 0, d)
            shape = part.shape
            gathered.append(part.reshape(*shape[:d], shape[d] * shape[d + 1], *shape[d + 2 :]))
            at += w.size
        layers.append(tuple(gathered))
    return layers


def shards(
    inputs,
    cotangent,
    packed_weight,
    bias_pair,
    output_weight,
    output_bias,
    expand_weight,
    expand_bias,
    contract_weight,
    contract_bias,
    gain_first,
    shift_first,
    gain_second,
    shift_second,
):
    dims = (0, 1, 1, 0, 0, 0, 1, 0, 0, 0, 0, 0)
    weights_zero, weights_last = gather_all(
        (
            packed_weight[0],
            bias_pair[0],
            output_weight[0],
            output_bias[0],
            expand_weight[0],
            expand_bias[0],
            contract_weight[0],
            contract_bias[0],
            gain_first[0],
            shift_first[0],
            gain_second[0],
            shift_second[0],
        ),
        dims,
    )
    norm_params = jnp.stack([w[i] for w in (weights_zero, weights_last) for i in (8, 9, 10, 11)])
    full_norms = collect(norm_params, "tensor", 1)
    section_index = lax.axis_index("section")
    is_first = section_index == 0
    stream = lax.dynamic_index_in_dim(inputs, section_index, axis=0, keepdims=False)
    out_grad = lax.dynamic_index_in_dim(cotangent, section_index, axis=0, keepdims=False)
    middle, kept_zero = layer_forward(stream, weights_zero, full_norms[:4])
    final, kept_last = layer_forward(middle, weights_last, full_norms[4:])
    swap = [(0, 1), (1, 0)]
    other_out = lax.ppermute(jnp.where(is_first, final, middle), "section", swap)
    middle_grad, grads_last = layer_backward(out_grad, kept_last, weights_last)
    input_grad, grads_zero = layer_backward(middle_grad, kept_zero, weights_zero)
    other_grad = lax.ppermute(jnp.where(is_first, middle_grad, input_grad), "section", swap)
    reduced = sum_at_end(grads_zero, grads_last, dims)
    section_outputs = jnp.where(
        is_first, jnp.stack([middle, other_out]), jnp.stack([other_out, final])
    )[None]
    section_grads = jnp.where(
        is_first, jnp.stack([input_grad, other_grad]), jnp.stack([other_grad, middle_grad])
    )[None]
    return (section_outputs, section_grads) + tuple(reduced)


def solution(mesh):
    in_specs = (
        P(None, "dp", None, "tensor"),
        P(None, "dp", None, "tensor"),
        P("section", "dp", None, "tensor"),
        P("section", None, ("tensor", "dp")),
        P("section", "tensor", "dp"),
        P("section", ("tensor", "dp")),
        P("section", "dp", "tensor"),
        P("section", ("tensor", "dp")),
        P("section", "tensor", "dp"),
        P("section", ("tensor", "dp")),
        P("section", ("tensor", "dp")),
        P("section", ("tensor", "dp")),
        P("section", ("tensor", "dp")),
        P("section", ("tensor", "dp")),
    )
    out_specs = (
        P("section", None, "dp", None, "tensor"),
        P("section", None, "dp", None, "tensor"),
        P("section", "dp", None, "tensor"),
        P("section", None, ("tensor", "dp")),
        P("section", "tensor", "dp"),
        P("section", ("tensor", "dp")),
        P("section", "dp", "tensor"),
        P("section", ("tensor", "dp")),
        P("section", "tensor", "dp"),
        P("section", ("tensor", "dp")),
        P("section", ("tensor", "dp")),
        P("section", ("tensor", "dp")),
        P("section", ("tensor", "dp")),
        P("section", ("tensor", "dp")),
    )
    return jax.shard_map(shards, mesh=mesh, in_specs=in_specs, out_specs=out_specs, check_vma=False)
```

```python
import math

import jax
import jax.numpy as jnp
from jax import lax
from jax.sharding import PartitionSpec as P

HEAD_DIM = 64


epsilon = 1e-05
gelu_coef = math.sqrt(2.0 / math.pi)
masked_value = -1e30


def sent_to_all(array, axis):
    copies = jnp.broadcast_to(array, (lax.axis_size(axis), *array.shape))
    return lax.all_to_all(copies, axis, split_axis=0, concat_axis=0, tiled=True)


def taken_together(array, axis):
    return sent_to_all(array, axis).sum(axis=0)


def in_one(arrays, axis):
    ends = [0]
    for a in arrays:
        ends.append(ends[-1] + a.size)
    subtotal = taken_together(jnp.concatenate([a.ravel() for a in arrays]), axis)
    return tuple((subtotal[b:e].reshape(a.shape) for a, b, e in zip(arrays, ends, ends[1:])))


def joined_along(parts, dim):
    parts = jnp.moveaxis(parts, 0, dim)
    shape = parts.shape
    return parts.reshape(*shape[:dim], shape[dim] * shape[dim + 1], *shape[dim + 2 :])


def collect(array, axis, dim):
    parts = sent_to_all(array, axis)
    return joined_along(parts, dim)


def in_blocks(array, dim, peers):
    before, after = (array.shape[:dim], array.shape[dim + 1 :])
    return jnp.moveaxis(array.reshape(*before, peers, -1, *after), dim, 0)


def summed_on_arrival(array, axis, dim):
    parts = in_blocks(array, dim, lax.axis_size(axis))
    arrived = lax.all_to_all(parts, axis, split_axis=0, concat_axis=0, tiled=True)
    return arrived.astype(jnp.float32).sum(axis=0)


def side_by_side(arrays, axis, dim, along):
    both = jnp.concatenate(arrays, axis=along)
    result, at, gathered = (lax.psum_scatter(both, axis, scatter_dimension=dim, tiled=True), 0, [])
    for a in arrays:
        gathered.append(lax.slice_in_dim(result, at, at + a.shape[along], axis=along))
        at += a.shape[along]
    return tuple(gathered)


def in_one_piece(arrays, axis, dim, along):
    both = jnp.concatenate(arrays, axis=along)
    result, at, gathered = (lax.all_gather(both, axis, axis=dim, tiled=True), 0, [])
    for a in arrays:
        gathered.append(lax.slice_in_dim(result, at, at + a.shape[along], axis=along))
        at += a.shape[along]
    return tuple(gathered)


def from_behind(array, axis, by):
    peers = lax.axis_size(axis)
    pairs = [(i, i + by) for i in range(peers) if 0 <= i + by < peers]
    return lax.ppermute(array, axis, pairs)


def gelu_tanh(values):
    return (
        0.5 * values * (1.0 + jnp.tanh(gelu_coef * (values + 0.044715 * values * values * values)))
    )


def norm_forward(stream, gain, offset):
    width_all = stream.shape[1] * lax.axis_size("tensor")
    totals, squares = in_one((jnp.sum(stream, axis=1), jnp.sum(stream * stream, axis=1)), "tensor")
    mean_row = (totals / width_all)[:, None]
    var_row = (squares / width_all)[:, None] - mean_row * mean_row
    inv_scale = lax.rsqrt(var_row + epsilon)
    normal_part = (stream - mean_row) * inv_scale
    normed = (normal_part * gain + offset).astype(jnp.bfloat16)
    return (collect(normed, "tensor", 1), normal_part, inv_scale)


def norm_backward(partial_term, normal_part, inv_scale, gain):
    width_all = partial_term.shape[1]
    d_normed = summed_on_arrival(partial_term.astype(jnp.bfloat16), "tensor", 1)
    gain_grad = jnp.sum(d_normed * normal_part, axis=0)
    offset_grad = jnp.sum(d_normed, axis=0)
    scaled = d_normed * gain
    first_sum, second_sum = in_one(
        (jnp.sum(scaled, axis=1), jnp.sum(scaled * normal_part, axis=1)), "tensor"
    )
    stream_grad = inv_scale * (
        scaled - first_sum[:, None] / width_all - normal_part * second_sum[:, None] / width_all
    )
    return (stream_grad, gain_grad, offset_grad)


def branch_sum(partial_term):
    return summed_on_arrival(partial_term.astype(jnp.bfloat16), "tensor", 1)


def branch_grad(stream_grad):
    return collect(stream_grad.astype(jnp.bfloat16), "tensor", 1)


def causal_scores(queries, keys_in):
    length = queries.shape[0]
    scale_factor = queries.shape[2] ** (-0.5)
    scores = (
        jnp.einsum("qhe,khe->hqk", queries, keys_in, preferred_element_type=jnp.float32)
        * scale_factor
    )
    causal = lax.broadcasted_iota(jnp.int32, (length, length), 0) >= lax.broadcasted_iota(
        jnp.int32, (length, length), 1
    )
    return (jnp.where(causal[None], scores, masked_value), scale_factor)


def attend(operands):
    queries, keys_in, values_in = operands
    masked, scale_factor = causal_scores(queries, keys_in)
    highest = jnp.max(masked, axis=2, keepdims=True)
    logsum = highest + jnp.log(jnp.sum(jnp.exp(masked - highest), axis=2, keepdims=True))
    weights_low = jnp.exp(masked - logsum).astype(jnp.bfloat16)
    mixture = jnp.einsum("hqk,khe->qhe", weights_low, values_in, preferred_element_type=jnp.float32)
    return (mixture.astype(jnp.bfloat16), logsum[:, :, 0])


def attend_back(operands):
    queries, keys_in, values_in, logsum, mixed_grad = operands
    masked, scale_factor = causal_scores(queries, keys_in)
    probs_full = jnp.exp(masked - logsum[:, :, None])
    probs_grad = jnp.einsum(
        "qhe,khe->hqk", mixed_grad, values_in, preferred_element_type=jnp.float32
    )
    row_dot = jnp.sum(probs_full * probs_grad, axis=2, keepdims=True)
    score_grad = (probs_full * (probs_grad - row_dot)).astype(jnp.bfloat16)
    query_grad = (
        jnp.einsum("hqk,khe->qhe", score_grad, keys_in, preferred_element_type=jnp.float32)
        * scale_factor
    )
    key_grad = (
        jnp.einsum("hqk,qhe->khe", score_grad, queries, preferred_element_type=jnp.float32)
        * scale_factor
    )
    value_grad = jnp.einsum(
        "hqk,qhe->khe",
        probs_full.astype(jnp.bfloat16),
        mixed_grad,
        preferred_element_type=jnp.float32,
    )
    return (
        query_grad.astype(jnp.bfloat16),
        key_grad.astype(jnp.bfloat16),
        value_grad.astype(jnp.bfloat16),
    )


def attention_forward(normed_one, packed_weight, bias_pair, shape_heads, rows_count, width_part):
    packed = jnp.einsum(
        "nd,dcf->ncf", normed_one, packed_weight, preferred_element_type=jnp.float32
    )
    queries = (packed[:, 0] + bias_pair[0]).astype(jnp.bfloat16)
    keys_in = packed[:, 1].astype(jnp.bfloat16)
    values_in = (packed[:, 2] + bias_pair[1]).astype(jnp.bfloat16)
    mixture, logsum = lax.map(
        attend,
        (
            queries.reshape(shape_heads),
            keys_in.reshape(shape_heads),
            values_in.reshape(shape_heads),
        ),
    )
    return (queries, keys_in, values_in, logsum, mixture.reshape(rows_count, width_part))


def attention_backward(branch_one, kept_part, output_weight, shape_heads, rows_count, width_part):
    queries, keys_in, values_in, logsum, mixed_rows, normed_one = kept_part
    output_weight_grad = jnp.einsum(
        "nf,nd->fd", mixed_rows, branch_one, preferred_element_type=jnp.float32
    )
    mixed_grad = jnp.einsum(
        "nd,fd->nf", branch_one, output_weight, preferred_element_type=jnp.float32
    ).astype(jnp.bfloat16)
    query_grad, key_grad, value_grad = lax.map(
        attend_back,
        (
            queries.reshape(shape_heads),
            keys_in.reshape(shape_heads),
            values_in.reshape(shape_heads),
            logsum,
            mixed_grad.reshape(shape_heads),
        ),
    )
    query_rows = query_grad.reshape(rows_count, width_part)
    key_rows = key_grad.reshape(rows_count, width_part)
    value_rows = value_grad.reshape(rows_count, width_part)
    packed_grad = jnp.stack([query_rows, key_rows, value_rows], axis=1)
    bias_pair_grad = jnp.stack(
        [
            jnp.sum(query_rows.astype(jnp.float32), axis=0),
            jnp.sum(value_rows.astype(jnp.float32), axis=0),
        ]
    )
    packed_weight_grad = jnp.einsum(
        "nd,ncf->dcf", normed_one, packed_grad, preferred_element_type=jnp.float32
    )
    return (packed_grad, packed_weight_grad, bias_pair_grad, output_weight_grad)


def layer_forward(stream, weights):
    (
        packed_weight,
        bias_pair,
        output_weight,
        output_bias,
        expand_weight,
        expand_bias,
        contract_weight,
        contract_bias,
        gain_first,
        shift_first,
        gain_second,
        shift_second,
    ) = weights
    seq_count, length, width_part = stream.shape
    rows_count = seq_count * length
    shape_heads = (seq_count, length, width_part // HEAD_DIM, HEAD_DIM)
    stream_rows = stream.reshape(rows_count, width_part)
    normed_one, normal_one, inv_one = norm_forward(stream_rows, gain_first, shift_first)
    queries, keys_in, values_in, logsum, mixed_rows = attention_forward(
        normed_one, packed_weight, bias_pair, shape_heads, rows_count, width_part
    )
    residual = (
        stream_rows
        + branch_sum(jnp.dot(mixed_rows, output_weight, preferred_element_type=jnp.float32))
        + output_bias
    )
    normed_two, normal_two, inv_two = norm_forward(residual, gain_second, shift_second)
    hidden_pre = (
        jnp.dot(normed_two, expand_weight, preferred_element_type=jnp.float32) + expand_bias
    )
    hidden = gelu_tanh(hidden_pre).astype(jnp.bfloat16)
    result = (
        residual
        + branch_sum(jnp.dot(hidden, contract_weight, preferred_element_type=jnp.float32))
        + contract_bias
    )
    kept_values = (
        normed_one,
        normal_one,
        inv_one,
        queries,
        keys_in,
        values_in,
        logsum,
        mixed_rows,
        normed_two,
        normal_two,
        inv_two,
        hidden_pre,
        hidden,
    )
    return (result.reshape(stream.shape), kept_values)


def layer_backward(out_grad, kept_values, weights):
    (
        packed_weight,
        bias_pair,
        output_weight,
        output_bias,
        expand_weight,
        expand_bias,
        contract_weight,
        contract_bias,
        gain_first,
        shift_first,
        gain_second,
        shift_second,
    ) = weights
    (
        normed_one,
        normal_one,
        inv_one,
        queries,
        keys_in,
        values_in,
        logsum,
        mixed_rows,
        normed_two,
        normal_two,
        inv_two,
        hidden_pre,
        hidden,
    ) = kept_values
    seq_count, length, width_part = out_grad.shape
    rows_count = seq_count * length
    shape_heads = (seq_count, length, width_part // HEAD_DIM, HEAD_DIM)
    grad_rows = out_grad.reshape(rows_count, width_part)
    contract_bias_grad = jnp.sum(grad_rows, axis=0)
    branch_two = branch_grad(grad_rows)
    contract_weight_grad = jnp.einsum(
        "nf,nd->fd", hidden, branch_two, preferred_element_type=jnp.float32
    )
    hidden_grad = jnp.einsum(
        "nd,fd->nf", branch_two, contract_weight, preferred_element_type=jnp.float32
    )
    pre_grad = jax.vjp(gelu_tanh, hidden_pre)[1](hidden_grad)[0].astype(jnp.bfloat16)
    expand_bias_grad = jnp.sum(pre_grad.astype(jnp.float32), axis=0)
    expand_weight_grad = jnp.einsum(
        "nd,nf->df", normed_two, pre_grad, preferred_element_type=jnp.float32
    )
    second_grad, gain_second_grad, shift_second_grad = norm_backward(
        jnp.einsum("nf,df->nd", pre_grad, expand_weight, preferred_element_type=jnp.float32),
        normal_two,
        inv_two,
        gain_second,
    )
    residual_grad = grad_rows + second_grad
    output_bias_grad = jnp.sum(residual_grad, axis=0)
    branch_one = branch_grad(residual_grad)
    packed_grad, packed_weight_grad, bias_pair_grad, output_weight_grad = attention_backward(
        branch_one,
        (queries, keys_in, values_in, logsum, mixed_rows, normed_one),
        output_weight,
        shape_heads,
        rows_count,
        width_part,
    )
    first_grad, gain_first_grad, shift_first_grad = norm_backward(
        jnp.einsum("ncf,dcf->nd", packed_grad, packed_weight, preferred_element_type=jnp.float32),
        normal_one,
        inv_one,
        gain_first,
    )
    input_grad = (residual_grad + first_grad).reshape(out_grad.shape)
    return (
        input_grad,
        (
            packed_weight_grad,
            bias_pair_grad,
            output_weight_grad,
            output_bias_grad,
            expand_weight_grad,
            expand_bias_grad,
            contract_weight_grad,
            contract_bias_grad,
            gain_first_grad,
            shift_first_grad,
            gain_second_grad,
            shift_second_grad,
        ),
    )


def as_blocks(array, dim, peers):
    before, after = (array.shape[:dim], array.shape[dim + 1 :])
    split = array.reshape(*before, peers, array.shape[dim] // peers, *after)
    return jnp.moveaxis(split, dim, 0).reshape(peers, -1)


def from_blocks(flat, shape, dim, peers):
    block_shape = (*shape[:dim], shape[dim] // peers, *shape[dim + 1 :])
    return flat.reshape(block_shape)


def sum_at_end(grads_zero, grads_last, dims):
    peers = lax.axis_size("dp")
    pieces = [
        jnp.concatenate(
            [as_blocks(g0.astype(jnp.bfloat16), d, peers), as_blocks(g1.astype(jnp.bfloat16), d, peers)]
        )
        for g0, g1, d in zip(grads_zero, grads_last, dims)
    ]
    widths = [p.shape[1] for p in pieces]
    spare = -sum(widths) % 1024
    pieces.append(jnp.zeros((2 * peers, spare), jnp.bfloat16))
    total = lax.psum_scatter(
        jnp.concatenate(pieces, axis=1).reshape(1, -1, 128),
        ("section", "dp"),
        scatter_dimension=1,
        tiled=True,
    ).reshape(1, -1)
    reduced, at = ([], 0)
    for g, d, w in zip(grads_zero, dims, widths):
        piece = total[0, at : at + w].astype(jnp.float32)
        reduced.append(from_blocks(piece, g.shape, d, peers)[None])
        at += w
    return tuple(reduced)


def unpack_layer(rows, weights, dims):
    peers = rows.shape[0]
    gathered, at = ([], 0)
    for w, d in zip(weights, dims):
        part = rows[:, at : at + w.size].reshape(peers, *w.shape)
        part = jnp.moveaxis(part, 0, d)
        shape = part.shape
        gathered.append(part.reshape(*shape[:d], shape[d] * shape[d + 1], *shape[d + 2 :]))
        at += w.size
    return tuple(gathered)


def gather_all(weights, dims, is_first):
    size = sum(w.size for w in weights)
    own = jnp.concatenate([w.reshape(-1) for w in weights] + [jnp.zeros((-size % 1024,), jnp.bfloat16)])
    other = lax.ppermute(own, "section", [(0, 1), (1, 0)])
    first_rows = lax.all_gather(jnp.where(is_first, own, other)[None], "dp", axis=0, tiled=True)
    last_rows = lax.all_gather(jnp.where(is_first, other, own)[None], "dp", axis=0, tiled=True)
    return (unpack_layer(first_rows, weights, dims), unpack_layer(last_rows, weights, dims))


def shards(
    inputs,
    cotangent,
    packed_weight,
    bias_pair,
    output_weight,
    output_bias,
    expand_weight,
    expand_bias,
    contract_weight,
    contract_bias,
    gain_first,
    shift_first,
    gain_second,
    shift_second,
):
    dims = (0, 1, 1, 0, 0, 0, 1, 0, 0, 0, 0, 0)
    section_index = lax.axis_index("section")
    is_first = section_index == 0
    weights_zero, weights_last = gather_all(
        (
            packed_weight[0],
            bias_pair[0],
            output_weight[0],
            output_bias[0],
            expand_weight[0],
            expand_bias[0],
            contract_weight[0],
            contract_bias[0],
            gain_first[0],
            shift_first[0],
            gain_second[0],
            shift_second[0],
        ),
        dims,
        is_first,
    )
    stream = lax.dynamic_index_in_dim(inputs, section_index, axis=0, keepdims=False)
    out_grad = lax.dynamic_index_in_dim(cotangent, section_index, axis=0, keepdims=False)
    middle, kept_zero = layer_forward(stream, weights_zero)
    final, kept_last = layer_forward(middle, weights_last)
    other_middle = lax.ppermute(middle, "section", [(1, 0)])
    other_final = lax.ppermute(final, "section", [(0, 1)])
    middle_grad, grads_last = layer_backward(out_grad, kept_last, weights_last)
    other_middle_grad = lax.ppermute(middle_grad, "section", [(0, 1)])
    input_grad, grads_zero = layer_backward(middle_grad, kept_zero, weights_zero)
    other_input_grad = lax.ppermute(input_grad, "section", [(1, 0)])
    reduced = sum_at_end(grads_zero, grads_last, dims)
    section_outputs = jnp.where(
        is_first, jnp.stack([middle, other_middle]), jnp.stack([other_final, final])
    )[None]
    section_grads = jnp.where(
        is_first,
        jnp.stack([input_grad, other_input_grad]),
        jnp.stack([other_middle_grad, middle_grad]),
    )[None]
    return (section_outputs, section_grads) + tuple(reduced)


def solution(mesh):
    in_specs = (
        P(None, "dp", None, "tensor"),
        P(None, "dp", None, "tensor"),
        P("section", "dp", None, "tensor"),
        P("section", None, ("tensor", "dp")),
        P("section", "tensor", "dp"),
        P("section", ("tensor", "dp")),
        P("section", "dp", "tensor"),
        P("section", ("tensor", "dp")),
        P("section", "tensor", "dp"),
        P("section", ("tensor", "dp")),
        P("section", ("tensor", "dp")),
        P("section", ("tensor", "dp")),
        P("section", ("tensor", "dp")),
        P("section", ("tensor", "dp")),
    )
    out_specs = (
        P("section", None, "dp", None, "tensor"),
        P("section", None, "dp", None, "tensor"),
        P("section", "dp", None, "tensor"),
        P("section", None, ("tensor", "dp")),
        P("section", "tensor", "dp"),
        P("section", ("tensor", "dp")),
        P("section", "dp", "tensor"),
        P("section", ("tensor", "dp")),
        P("section", "tensor", "dp"),
        P("section", ("tensor", "dp")),
        P("section", ("tensor", "dp")),
        P("section", ("tensor", "dp")),
        P("section", ("tensor", "dp")),
        P("section", ("tensor", "dp")),
    )
    return jax.shard_map(shards, mesh=mesh, in_specs=in_specs, out_specs=out_specs, check_vma=False)
```

```python
import math

import jax
import jax.numpy as jnp
from jax import lax
from jax.sharding import PartitionSpec as P

HEAD_DIM = 64


epsilon = 1e-05
gelu_coef = math.sqrt(2.0 / math.pi)
masked_value = -1e30


def sent_to_all(array, axis):
    copies = jnp.broadcast_to(array, (lax.axis_size(axis), *array.shape))
    return lax.all_to_all(copies, axis, split_axis=0, concat_axis=0, tiled=True)


def taken_together(array, axis):
    return sent_to_all(array, axis).sum(axis=0)


def in_one(arrays, axis):
    ends = [0]
    for a in arrays:
        ends.append(ends[-1] + a.size)
    subtotal = taken_together(jnp.concatenate([a.ravel() for a in arrays]), axis)
    return tuple((subtotal[b:e].reshape(a.shape) for a, b, e in zip(arrays, ends, ends[1:])))


def joined_along(parts, dim):
    parts = jnp.moveaxis(parts, 0, dim)
    shape = parts.shape
    return parts.reshape(*shape[:dim], shape[dim] * shape[dim + 1], *shape[dim + 2 :])


def collect(array, axis, dim):
    parts = sent_to_all(array, axis)
    return joined_along(parts, dim)


def in_blocks(array, dim, peers):
    before, after = (array.shape[:dim], array.shape[dim + 1 :])
    return jnp.moveaxis(array.reshape(*before, peers, -1, *after), dim, 0)


def summed_on_arrival(array, axis, dim):
    parts = in_blocks(array, dim, lax.axis_size(axis))
    arrived = lax.all_to_all(parts, axis, split_axis=0, concat_axis=0, tiled=True)
    return arrived.astype(jnp.float32).sum(axis=0)


def side_by_side(arrays, axis, dim, along):
    both = jnp.concatenate(arrays, axis=along)
    result, at, gathered = (lax.psum_scatter(both, axis, scatter_dimension=dim, tiled=True), 0, [])
    for a in arrays:
        gathered.append(lax.slice_in_dim(result, at, at + a.shape[along], axis=along))
        at += a.shape[along]
    return tuple(gathered)


def in_one_piece(arrays, axis, dim, along):
    both = jnp.concatenate(arrays, axis=along)
    result, at, gathered = (lax.all_gather(both, axis, axis=dim, tiled=True), 0, [])
    for a in arrays:
        gathered.append(lax.slice_in_dim(result, at, at + a.shape[along], axis=along))
        at += a.shape[along]
    return tuple(gathered)


def from_behind(array, axis, by):
    peers = lax.axis_size(axis)
    pairs = [(i, i + by) for i in range(peers) if 0 <= i + by < peers]
    return lax.ppermute(array, axis, pairs)


def gelu_tanh(values):
    return (
        0.5 * values * (1.0 + jnp.tanh(gelu_coef * (values + 0.044715 * values * values * values)))
    )


def norm_forward(stream, gain, offset):
    width_all = stream.shape[1] * lax.axis_size("tensor")
    totals, squares = in_one((jnp.sum(stream, axis=1), jnp.sum(stream * stream, axis=1)), "tensor")
    mean_row = (totals / width_all)[:, None]
    var_row = (squares / width_all)[:, None] - mean_row * mean_row
    inv_scale = lax.rsqrt(var_row + epsilon)
    normal_part = (stream - mean_row) * inv_scale
    normed = (normal_part * gain + offset).astype(jnp.bfloat16)
    return (collect(normed, "tensor", 1), normal_part, inv_scale)


def norm_backward(partial_term, normal_part, inv_scale, gain):
    width_all = partial_term.shape[1]
    d_normed = summed_on_arrival(partial_term.astype(jnp.bfloat16), "tensor", 1)
    gain_grad = jnp.sum(d_normed * normal_part, axis=0)
    offset_grad = jnp.sum(d_normed, axis=0)
    scaled = d_normed * gain
    first_sum, second_sum = in_one(
        (jnp.sum(scaled, axis=1), jnp.sum(scaled * normal_part, axis=1)), "tensor"
    )
    stream_grad = inv_scale * (
        scaled - first_sum[:, None] / width_all - normal_part * second_sum[:, None] / width_all
    )
    return (stream_grad, gain_grad, offset_grad)


def branch_sum(partial_term):
    return summed_on_arrival(partial_term.astype(jnp.bfloat16), "tensor", 1)


def branch_grad(stream_grad):
    return collect(stream_grad.astype(jnp.bfloat16), "tensor", 1)


def causal_scores(queries, keys_in):
    length = queries.shape[0]
    scale_factor = queries.shape[2] ** (-0.5)
    scores = (
        jnp.einsum("qhe,khe->hqk", queries, keys_in, preferred_element_type=jnp.float32)
        * scale_factor
    )
    causal = lax.broadcasted_iota(jnp.int32, (length, length), 0) >= lax.broadcasted_iota(
        jnp.int32, (length, length), 1
    )
    return (jnp.where(causal[None], scores, masked_value), scale_factor)


def attend(operands):
    queries, keys_in, values_in = operands
    masked, scale_factor = causal_scores(queries, keys_in)
    highest = jnp.max(masked, axis=2, keepdims=True)
    logsum = highest + jnp.log(jnp.sum(jnp.exp(masked - highest), axis=2, keepdims=True))
    weights_low = jnp.exp(masked - logsum).astype(jnp.bfloat16)
    mixture = jnp.einsum("hqk,khe->qhe", weights_low, values_in, preferred_element_type=jnp.float32)
    return (mixture.astype(jnp.bfloat16), logsum[:, :, 0])


def attend_back(operands):
    queries, keys_in, values_in, logsum, mixed_grad = operands
    masked, scale_factor = causal_scores(queries, keys_in)
    probs_full = jnp.exp(masked - logsum[:, :, None])
    probs_grad = jnp.einsum(
        "qhe,khe->hqk", mixed_grad, values_in, preferred_element_type=jnp.float32
    )
    row_dot = jnp.sum(probs_full * probs_grad, axis=2, keepdims=True)
    score_grad = (probs_full * (probs_grad - row_dot)).astype(jnp.bfloat16)
    query_grad = (
        jnp.einsum("hqk,khe->qhe", score_grad, keys_in, preferred_element_type=jnp.float32)
        * scale_factor
    )
    key_grad = (
        jnp.einsum("hqk,qhe->khe", score_grad, queries, preferred_element_type=jnp.float32)
        * scale_factor
    )
    value_grad = jnp.einsum(
        "hqk,qhe->khe",
        probs_full.astype(jnp.bfloat16),
        mixed_grad,
        preferred_element_type=jnp.float32,
    )
    return (
        query_grad.astype(jnp.bfloat16),
        key_grad.astype(jnp.bfloat16),
        value_grad.astype(jnp.bfloat16),
    )


def attention_forward(normed_one, packed_weight, bias_pair, shape_heads, rows_count, width_part):
    packed = jnp.einsum(
        "nd,dcf->ncf", normed_one, packed_weight, preferred_element_type=jnp.float32
    )
    queries = (packed[:, 0] + bias_pair[0]).astype(jnp.bfloat16)
    keys_in = packed[:, 1].astype(jnp.bfloat16)
    values_in = (packed[:, 2] + bias_pair[1]).astype(jnp.bfloat16)
    mixture, logsum = lax.map(
        attend,
        (
            queries.reshape(shape_heads),
            keys_in.reshape(shape_heads),
            values_in.reshape(shape_heads),
        ),
    )
    return (queries, keys_in, values_in, logsum, mixture.reshape(rows_count, width_part))


def attention_backward(branch_one, kept_part, output_weight, shape_heads, rows_count, width_part):
    queries, keys_in, values_in, logsum, mixed_rows, normed_one = kept_part
    output_weight_grad = jnp.einsum(
        "nf,nd->fd", mixed_rows, branch_one, preferred_element_type=jnp.float32
    )
    mixed_grad = jnp.einsum(
        "nd,fd->nf", branch_one, output_weight, preferred_element_type=jnp.float32
    ).astype(jnp.bfloat16)
    query_grad, key_grad, value_grad = lax.map(
        attend_back,
        (
            queries.reshape(shape_heads),
            keys_in.reshape(shape_heads),
            values_in.reshape(shape_heads),
            logsum,
            mixed_grad.reshape(shape_heads),
        ),
    )
    query_rows = query_grad.reshape(rows_count, width_part)
    key_rows = key_grad.reshape(rows_count, width_part)
    value_rows = value_grad.reshape(rows_count, width_part)
    packed_grad = jnp.stack([query_rows, key_rows, value_rows], axis=1)
    bias_pair_grad = jnp.stack(
        [
            jnp.sum(query_rows.astype(jnp.float32), axis=0),
            jnp.sum(value_rows.astype(jnp.float32), axis=0),
        ]
    )
    packed_weight_grad = jnp.einsum(
        "nd,ncf->dcf", normed_one, packed_grad, preferred_element_type=jnp.float32
    )
    return (packed_grad, packed_weight_grad, bias_pair_grad, output_weight_grad)


def layer_forward(stream, weights):
    (
        packed_weight,
        bias_pair,
        output_weight,
        output_bias,
        expand_weight,
        expand_bias,
        contract_weight,
        contract_bias,
        gain_first,
        shift_first,
        gain_second,
        shift_second,
    ) = weights
    seq_count, length, width_part = stream.shape
    rows_count = seq_count * length
    shape_heads = (seq_count, length, width_part // HEAD_DIM, HEAD_DIM)
    stream_rows = stream.reshape(rows_count, width_part)
    normed_one, normal_one, inv_one = norm_forward(stream_rows, gain_first, shift_first)
    queries, keys_in, values_in, logsum, mixed_rows = attention_forward(
        normed_one, packed_weight, bias_pair, shape_heads, rows_count, width_part
    )
    residual = (
        stream_rows
        + branch_sum(jnp.dot(mixed_rows, output_weight, preferred_element_type=jnp.float32))
        + output_bias
    )
    normed_two, normal_two, inv_two = norm_forward(residual, gain_second, shift_second)
    hidden_pre = (
        jnp.dot(normed_two, expand_weight, preferred_element_type=jnp.float32) + expand_bias
    )
    hidden = gelu_tanh(hidden_pre).astype(jnp.bfloat16)
    result = (
        residual
        + branch_sum(jnp.dot(hidden, contract_weight, preferred_element_type=jnp.float32))
        + contract_bias
    )
    kept_values = (
        normed_one,
        normal_one,
        inv_one,
        queries,
        keys_in,
        values_in,
        logsum,
        mixed_rows,
        normed_two,
        normal_two,
        inv_two,
        hidden_pre,
        hidden,
    )
    return (result.reshape(stream.shape), kept_values)


def layer_backward(out_grad, kept_values, weights):
    (
        packed_weight,
        bias_pair,
        output_weight,
        output_bias,
        expand_weight,
        expand_bias,
        contract_weight,
        contract_bias,
        gain_first,
        shift_first,
        gain_second,
        shift_second,
    ) = weights
    (
        normed_one,
        normal_one,
        inv_one,
        queries,
        keys_in,
        values_in,
        logsum,
        mixed_rows,
        normed_two,
        normal_two,
        inv_two,
        hidden_pre,
        hidden,
    ) = kept_values
    seq_count, length, width_part = out_grad.shape
    rows_count = seq_count * length
    shape_heads = (seq_count, length, width_part // HEAD_DIM, HEAD_DIM)
    grad_rows = out_grad.reshape(rows_count, width_part)
    contract_bias_grad = jnp.sum(grad_rows, axis=0)
    branch_two = branch_grad(grad_rows)
    contract_weight_grad = jnp.einsum(
        "nf,nd->fd", hidden, branch_two, preferred_element_type=jnp.float32
    )
    hidden_grad = jnp.einsum(
        "nd,fd->nf", branch_two, contract_weight, preferred_element_type=jnp.float32
    )
    pre_grad = jax.vjp(gelu_tanh, hidden_pre)[1](hidden_grad)[0].astype(jnp.bfloat16)
    expand_bias_grad = jnp.sum(pre_grad.astype(jnp.float32), axis=0)
    expand_weight_grad = jnp.einsum(
        "nd,nf->df", normed_two, pre_grad, preferred_element_type=jnp.float32
    )
    second_grad, gain_second_grad, shift_second_grad = norm_backward(
        jnp.einsum("nf,df->nd", pre_grad, expand_weight, preferred_element_type=jnp.float32),
        normal_two,
        inv_two,
        gain_second,
    )
    residual_grad = grad_rows + second_grad
    output_bias_grad = jnp.sum(residual_grad, axis=0)
    branch_one = branch_grad(residual_grad)
    packed_grad, packed_weight_grad, bias_pair_grad, output_weight_grad = attention_backward(
        branch_one,
        (queries, keys_in, values_in, logsum, mixed_rows, normed_one),
        output_weight,
        shape_heads,
        rows_count,
        width_part,
    )
    first_grad, gain_first_grad, shift_first_grad = norm_backward(
        jnp.einsum("ncf,dcf->nd", packed_grad, packed_weight, preferred_element_type=jnp.float32),
        normal_one,
        inv_one,
        gain_first,
    )
    input_grad = (residual_grad + first_grad).reshape(out_grad.shape)
    return (
        input_grad,
        (
            packed_weight_grad,
            bias_pair_grad,
            output_weight_grad,
            output_bias_grad,
            expand_weight_grad,
            expand_bias_grad,
            contract_weight_grad,
            contract_bias_grad,
            gain_first_grad,
            shift_first_grad,
            gain_second_grad,
            shift_second_grad,
        ),
    )


def as_blocks(array, dim, peers):
    before, after = (array.shape[:dim], array.shape[dim + 1 :])
    split = array.reshape(*before, peers, array.shape[dim] // peers, *after)
    return jnp.moveaxis(split, dim, 0).reshape(peers, -1)


def from_blocks(flat, shape, dim, peers):
    block_shape = (*shape[:dim], shape[dim] // peers, *shape[dim + 1 :])
    return flat.reshape(block_shape)


def split_by_size(arrays):
    big = [i for i, a in enumerate(arrays) if a[0].size % 128 == 0]
    small = [i for i, a in enumerate(arrays) if a[0].size % 128 != 0]
    return (big, small)


def in_rows(blocks, big, small):
    count = blocks[0].shape[0]
    rest = jnp.concatenate([blocks[i].reshape(count, -1) for i in small], axis=1)
    spare = -rest.shape[1] % 2048
    rest = jnp.concatenate([rest, jnp.zeros((count, spare), rest.dtype)], axis=1)
    rows = [blocks[i].reshape(count, -1, 128) for i in big] + [rest.reshape(count, -1, 128)]
    return jnp.concatenate(rows, axis=1)


def out_of_rows(rows, shapes, big, small):
    count = rows.shape[0]
    parts, at = ({}, 0)
    for i in big:
        height = math.prod(shapes[i]) // 128
        parts[i] = rows[:, at : at + height].reshape(count, *shapes[i])
        at += height
    rest = rows[:, at:].reshape(count, -1)
    at = 0
    for i in small:
        width = math.prod(shapes[i])
        parts[i] = rest[:, at : at + width].reshape(count, *shapes[i])
        at += width
    return [parts[i] for i in range(len(shapes))]


def sum_at_end(grads_zero, grads_last, dims):
    peers = lax.axis_size("dp")
    blocks = [
        jnp.concatenate(
            [as_blocks(g0.astype(jnp.bfloat16), d, peers), as_blocks(g1.astype(jnp.bfloat16), d, peers)]
        )
        for g0, g1, d in zip(grads_zero, grads_last, dims)
    ]
    big, small = split_by_size(blocks)
    rows = in_rows(blocks, big, small)
    total = lax.psum_scatter(
        rows.reshape(-1, 128), ("section", "dp"), scatter_dimension=0, tiled=True
    )
    shapes = [block.shape[1:] for block in blocks]
    parts = out_of_rows(total[None], shapes, big, small)
    return tuple(
        from_blocks(part[0].astype(jnp.float32), g.shape, d, peers)[None]
        for part, g, d in zip(parts, grads_zero, dims)
    )


def unpack_layer(gathered_rows, weights, dims, big, small):
    parts = out_of_rows(gathered_rows, [w.shape for w in weights], big, small)
    gathered = []
    for part, d in zip(parts, dims):
        part = jnp.moveaxis(part, 0, d)
        shape = part.shape
        gathered.append(part.reshape(*shape[:d], shape[d] * shape[d + 1], *shape[d + 2 :]))
    return tuple(gathered)


def gather_all(weights, dims, is_first):
    big, small = split_by_size([w[None] for w in weights])
    own = in_rows([w[None] for w in weights], big, small)[0]
    other = lax.ppermute(own, "section", [(0, 1), (1, 0)])
    first_rows = lax.all_gather(jnp.where(is_first, own, other), "dp", axis=0, tiled=False)
    last_rows = lax.all_gather(jnp.where(is_first, other, own), "dp", axis=0, tiled=False)
    return (
        unpack_layer(first_rows, weights, dims, big, small),
        unpack_layer(last_rows, weights, dims, big, small),
    )


def shards(
    inputs,
    cotangent,
    packed_weight,
    bias_pair,
    output_weight,
    output_bias,
    expand_weight,
    expand_bias,
    contract_weight,
    contract_bias,
    gain_first,
    shift_first,
    gain_second,
    shift_second,
):
    dims = (0, 1, 1, 0, 0, 0, 1, 0, 0, 0, 0, 0)
    section_index = lax.axis_index("section")
    is_first = section_index == 0
    weights_zero, weights_last = gather_all(
        (
            packed_weight[0],
            bias_pair[0],
            output_weight[0],
            output_bias[0],
            expand_weight[0],
            expand_bias[0],
            contract_weight[0],
            contract_bias[0],
            gain_first[0],
            shift_first[0],
            gain_second[0],
            shift_second[0],
        ),
        dims,
        is_first,
    )
    stream = lax.dynamic_index_in_dim(inputs, section_index, axis=0, keepdims=False)
    out_grad = lax.dynamic_index_in_dim(cotangent, section_index, axis=0, keepdims=False)
    middle, kept_zero = layer_forward(stream, weights_zero)
    final, kept_last = layer_forward(middle, weights_last)
    other_middle = lax.ppermute(middle, "section", [(1, 0)])
    other_final = lax.ppermute(final, "section", [(0, 1)])
    middle_grad, grads_last = layer_backward(out_grad, kept_last, weights_last)
    other_middle_grad = lax.ppermute(middle_grad, "section", [(0, 1)])
    input_grad, grads_zero = layer_backward(middle_grad, kept_zero, weights_zero)
    other_input_grad = lax.ppermute(input_grad, "section", [(1, 0)])
    reduced = sum_at_end(grads_zero, grads_last, dims)
    section_outputs = jnp.where(
        is_first, jnp.stack([middle, other_middle]), jnp.stack([other_final, final])
    )[None]
    section_grads = jnp.where(
        is_first,
        jnp.stack([input_grad, other_input_grad]),
        jnp.stack([other_middle_grad, middle_grad]),
    )[None]
    return (section_outputs, section_grads) + tuple(reduced)


def solution(mesh):
    in_specs = (
        P(None, "dp", None, "tensor"),
        P(None, "dp", None, "tensor"),
        P("section", "dp", None, "tensor"),
        P("section", None, ("tensor", "dp")),
        P("section", "tensor", "dp"),
        P("section", ("tensor", "dp")),
        P("section", "dp", "tensor"),
        P("section", ("tensor", "dp")),
        P("section", "tensor", "dp"),
        P("section", ("tensor", "dp")),
        P("section", ("tensor", "dp")),
        P("section", ("tensor", "dp")),
        P("section", ("tensor", "dp")),
        P("section", ("tensor", "dp")),
    )
    out_specs = (
        P("section", None, "dp", None, "tensor"),
        P("section", None, "dp", None, "tensor"),
        P("section", "dp", None, "tensor"),
        P("section", None, ("tensor", "dp")),
        P("section", "tensor", "dp"),
        P("section", ("tensor", "dp")),
        P("section", "dp", "tensor"),
        P("section", ("tensor", "dp")),
        P("section", "tensor", "dp"),
        P("section", ("tensor", "dp")),
        P("section", ("tensor", "dp")),
        P("section", ("tensor", "dp")),
        P("section", ("tensor", "dp")),
        P("section", ("tensor", "dp")),
    )
    return jax.shard_map(shards, mesh=mesh, in_specs=in_specs, out_specs=out_specs, check_vma=False)
```

```python
import math

import jax
import jax.numpy as jnp
from jax import lax
from jax.sharding import PartitionSpec as P

HEAD_DIM = 64


epsilon = 1e-05
gelu_coef = math.sqrt(2.0 / math.pi)
masked_value = -1e30


def sent_to_all(array, axis):
    copies = jnp.broadcast_to(array, (lax.axis_size(axis), *array.shape))
    return lax.all_to_all(copies, axis, split_axis=0, concat_axis=0, tiled=True)


def taken_together(array, axis):
    return sent_to_all(array, axis).sum(axis=0)


def in_one(arrays, axis):
    ends = [0]
    for a in arrays:
        ends.append(ends[-1] + a.size)
    subtotal = taken_together(jnp.concatenate([a.ravel() for a in arrays]), axis)
    return tuple((subtotal[b:e].reshape(a.shape) for a, b, e in zip(arrays, ends, ends[1:])))


def joined_along(parts, dim):
    parts = jnp.moveaxis(parts, 0, dim)
    shape = parts.shape
    return parts.reshape(*shape[:dim], shape[dim] * shape[dim + 1], *shape[dim + 2 :])


def collect(array, axis, dim):
    parts = sent_to_all(array, axis)
    return joined_along(parts, dim)


def in_blocks(array, dim, peers):
    before, after = (array.shape[:dim], array.shape[dim + 1 :])
    return jnp.moveaxis(array.reshape(*before, peers, -1, *after), dim, 0)


def summed_on_arrival(array, axis, dim):
    parts = in_blocks(array, dim, lax.axis_size(axis))
    arrived = lax.all_to_all(parts, axis, split_axis=0, concat_axis=0, tiled=True)
    return arrived.astype(jnp.float32).sum(axis=0)


def side_by_side(arrays, axis, dim, along):
    both = jnp.concatenate(arrays, axis=along)
    result, at, gathered = (lax.psum_scatter(both, axis, scatter_dimension=dim, tiled=True), 0, [])
    for a in arrays:
        gathered.append(lax.slice_in_dim(result, at, at + a.shape[along], axis=along))
        at += a.shape[along]
    return tuple(gathered)


def in_one_piece(arrays, axis, dim, along):
    both = jnp.concatenate(arrays, axis=along)
    result, at, gathered = (lax.all_gather(both, axis, axis=dim, tiled=True), 0, [])
    for a in arrays:
        gathered.append(lax.slice_in_dim(result, at, at + a.shape[along], axis=along))
        at += a.shape[along]
    return tuple(gathered)


def from_behind(array, axis, by):
    peers = lax.axis_size(axis)
    pairs = [(i, i + by) for i in range(peers) if 0 <= i + by < peers]
    return lax.ppermute(array, axis, pairs)


def gelu_tanh(values):
    return (
        0.5 * values * (1.0 + jnp.tanh(gelu_coef * (values + 0.044715 * values * values * values)))
    )


def norm_forward(stream, gain, offset):
    width_all = stream.shape[1] * lax.axis_size("tensor")
    totals, squares = in_one((jnp.sum(stream, axis=1), jnp.sum(stream * stream, axis=1)), "tensor")
    mean_row = (totals / width_all)[:, None]
    var_row = (squares / width_all)[:, None] - mean_row * mean_row
    inv_scale = lax.rsqrt(var_row + epsilon)
    normal_part = (stream - mean_row) * inv_scale
    normed = (normal_part * gain + offset).astype(jnp.bfloat16)
    return (collect(normed, "tensor", 1), normal_part, inv_scale)


def norm_backward(partial_term, normal_part, inv_scale, gain):
    width_all = partial_term.shape[1]
    d_normed = summed_on_arrival(partial_term.astype(jnp.bfloat16), "tensor", 1)
    gain_grad = jnp.sum(d_normed * normal_part, axis=0)
    offset_grad = jnp.sum(d_normed, axis=0)
    scaled = d_normed * gain
    first_sum, second_sum = in_one(
        (jnp.sum(scaled, axis=1), jnp.sum(scaled * normal_part, axis=1)), "tensor"
    )
    stream_grad = inv_scale * (
        scaled - first_sum[:, None] / width_all - normal_part * second_sum[:, None] / width_all
    )
    return (stream_grad, gain_grad, offset_grad)


def branch_sum(partial_term):
    return summed_on_arrival(partial_term.astype(jnp.bfloat16), "tensor", 1)


def branch_grad(stream_grad):
    return collect(stream_grad.astype(jnp.bfloat16), "tensor", 1)


def causal_scores(queries, keys_in):
    length = queries.shape[0]
    scale_factor = queries.shape[2] ** (-0.5)
    scores = (
        jnp.einsum("qhe,khe->hqk", queries, keys_in, preferred_element_type=jnp.float32)
        * scale_factor
    )
    causal = lax.broadcasted_iota(jnp.int32, (length, length), 0) >= lax.broadcasted_iota(
        jnp.int32, (length, length), 1
    )
    return (jnp.where(causal[None], scores, masked_value), scale_factor)


def attend(operands):
    queries, keys_in, values_in = operands
    masked, scale_factor = causal_scores(queries, keys_in)
    highest = jnp.max(masked, axis=2, keepdims=True)
    logsum = highest + jnp.log(jnp.sum(jnp.exp(masked - highest), axis=2, keepdims=True))
    weights_low = jnp.exp(masked - logsum).astype(jnp.bfloat16)
    mixture = jnp.einsum("hqk,khe->qhe", weights_low, values_in, preferred_element_type=jnp.float32)
    return (mixture.astype(jnp.bfloat16), logsum[:, :, 0])


def attend_back(operands):
    queries, keys_in, values_in, logsum, mixed_grad = operands
    masked, scale_factor = causal_scores(queries, keys_in)
    probs_full = jnp.exp(masked - logsum[:, :, None])
    probs_grad = jnp.einsum(
        "qhe,khe->hqk", mixed_grad, values_in, preferred_element_type=jnp.float32
    )
    row_dot = jnp.sum(probs_full * probs_grad, axis=2, keepdims=True)
    score_grad = (probs_full * (probs_grad - row_dot)).astype(jnp.bfloat16)
    query_grad = (
        jnp.einsum("hqk,khe->qhe", score_grad, keys_in, preferred_element_type=jnp.float32)
        * scale_factor
    )
    key_grad = (
        jnp.einsum("hqk,qhe->khe", score_grad, queries, preferred_element_type=jnp.float32)
        * scale_factor
    )
    value_grad = jnp.einsum(
        "hqk,qhe->khe",
        probs_full.astype(jnp.bfloat16),
        mixed_grad,
        preferred_element_type=jnp.float32,
    )
    return (
        query_grad.astype(jnp.bfloat16),
        key_grad.astype(jnp.bfloat16),
        value_grad.astype(jnp.bfloat16),
    )


def attention_forward(normed_one, packed_weight, bias_pair, shape_heads, rows_count, width_part):
    packed = jnp.einsum(
        "nd,dcf->ncf", normed_one, packed_weight, preferred_element_type=jnp.float32
    )
    queries = (packed[:, 0] + bias_pair[0]).astype(jnp.bfloat16)
    keys_in = packed[:, 1].astype(jnp.bfloat16)
    values_in = (packed[:, 2] + bias_pair[1]).astype(jnp.bfloat16)
    mixture, logsum = lax.map(
        attend,
        (
            queries.reshape(shape_heads),
            keys_in.reshape(shape_heads),
            values_in.reshape(shape_heads),
        ),
    )
    return (queries, keys_in, values_in, logsum, mixture.reshape(rows_count, width_part))


def attention_backward(branch_one, kept_part, output_weight, shape_heads, rows_count, width_part):
    queries, keys_in, values_in, logsum, mixed_rows, normed_one = kept_part
    output_weight_grad = jnp.einsum(
        "nf,nd->fd", mixed_rows, branch_one, preferred_element_type=jnp.float32
    )
    mixed_grad = jnp.einsum(
        "nd,fd->nf", branch_one, output_weight, preferred_element_type=jnp.float32
    ).astype(jnp.bfloat16)
    query_grad, key_grad, value_grad = lax.map(
        attend_back,
        (
            queries.reshape(shape_heads),
            keys_in.reshape(shape_heads),
            values_in.reshape(shape_heads),
            logsum,
            mixed_grad.reshape(shape_heads),
        ),
    )
    query_rows = query_grad.reshape(rows_count, width_part)
    key_rows = key_grad.reshape(rows_count, width_part)
    value_rows = value_grad.reshape(rows_count, width_part)
    packed_grad = jnp.stack([query_rows, key_rows, value_rows], axis=1)
    bias_pair_grad = jnp.stack(
        [
            jnp.sum(query_rows.astype(jnp.float32), axis=0),
            jnp.sum(value_rows.astype(jnp.float32), axis=0),
        ]
    )
    packed_weight_grad = jnp.einsum(
        "nd,ncf->dcf", normed_one, packed_grad, preferred_element_type=jnp.float32
    )
    return (packed_grad, packed_weight_grad, bias_pair_grad, output_weight_grad)


def layer_forward(stream, weights):
    (
        packed_weight,
        bias_pair,
        output_weight,
        output_bias,
        expand_weight,
        expand_bias,
        contract_weight,
        contract_bias,
        gain_first,
        shift_first,
        gain_second,
        shift_second,
    ) = weights
    seq_count, length, width_part = stream.shape
    rows_count = seq_count * length
    shape_heads = (seq_count, length, width_part // HEAD_DIM, HEAD_DIM)
    stream_rows = stream.reshape(rows_count, width_part)
    normed_one, normal_one, inv_one = norm_forward(stream_rows, gain_first, shift_first)
    queries, keys_in, values_in, logsum, mixed_rows = attention_forward(
        normed_one, packed_weight, bias_pair, shape_heads, rows_count, width_part
    )
    residual = (
        stream_rows
        + branch_sum(jnp.dot(mixed_rows, output_weight, preferred_element_type=jnp.float32))
        + output_bias
    )
    normed_two, normal_two, inv_two = norm_forward(residual, gain_second, shift_second)
    hidden_pre = (
        jnp.dot(normed_two, expand_weight, preferred_element_type=jnp.float32) + expand_bias
    )
    hidden = gelu_tanh(hidden_pre).astype(jnp.bfloat16)
    result = (
        residual
        + branch_sum(jnp.dot(hidden, contract_weight, preferred_element_type=jnp.float32))
        + contract_bias
    )
    kept_values = (
        normed_one,
        normal_one,
        inv_one,
        queries,
        keys_in,
        values_in,
        logsum,
        mixed_rows,
        normed_two,
        normal_two,
        inv_two,
        hidden_pre,
        hidden,
    )
    return (result.reshape(stream.shape), kept_values)


def layer_backward(out_grad, kept_values, weights):
    (
        packed_weight,
        bias_pair,
        output_weight,
        output_bias,
        expand_weight,
        expand_bias,
        contract_weight,
        contract_bias,
        gain_first,
        shift_first,
        gain_second,
        shift_second,
    ) = weights
    (
        normed_one,
        normal_one,
        inv_one,
        queries,
        keys_in,
        values_in,
        logsum,
        mixed_rows,
        normed_two,
        normal_two,
        inv_two,
        hidden_pre,
        hidden,
    ) = kept_values
    seq_count, length, width_part = out_grad.shape
    rows_count = seq_count * length
    shape_heads = (seq_count, length, width_part // HEAD_DIM, HEAD_DIM)
    grad_rows = out_grad.reshape(rows_count, width_part)
    contract_bias_grad = jnp.sum(grad_rows, axis=0)
    branch_two = branch_grad(grad_rows)
    contract_weight_grad = jnp.einsum(
        "nf,nd->fd", hidden, branch_two, preferred_element_type=jnp.float32
    )
    hidden_grad = jnp.einsum(
        "nd,fd->nf", branch_two, contract_weight, preferred_element_type=jnp.float32
    )
    pre_grad = jax.vjp(gelu_tanh, hidden_pre)[1](hidden_grad)[0].astype(jnp.bfloat16)
    expand_bias_grad = jnp.sum(pre_grad.astype(jnp.float32), axis=0)
    expand_weight_grad = jnp.einsum(
        "nd,nf->df", normed_two, pre_grad, preferred_element_type=jnp.float32
    )
    second_grad, gain_second_grad, shift_second_grad = norm_backward(
        jnp.einsum("nf,df->nd", pre_grad, expand_weight, preferred_element_type=jnp.float32),
        normal_two,
        inv_two,
        gain_second,
    )
    residual_grad = grad_rows + second_grad
    output_bias_grad = jnp.sum(residual_grad, axis=0)
    branch_one = branch_grad(residual_grad)
    packed_grad, packed_weight_grad, bias_pair_grad, output_weight_grad = attention_backward(
        branch_one,
        (queries, keys_in, values_in, logsum, mixed_rows, normed_one),
        output_weight,
        shape_heads,
        rows_count,
        width_part,
    )
    first_grad, gain_first_grad, shift_first_grad = norm_backward(
        jnp.einsum("ncf,dcf->nd", packed_grad, packed_weight, preferred_element_type=jnp.float32),
        normal_one,
        inv_one,
        gain_first,
    )
    input_grad = (residual_grad + first_grad).reshape(out_grad.shape)
    return (
        input_grad,
        (
            packed_weight_grad,
            bias_pair_grad,
            output_weight_grad,
            output_bias_grad,
            expand_weight_grad,
            expand_bias_grad,
            contract_weight_grad,
            contract_bias_grad,
            gain_first_grad,
            shift_first_grad,
            gain_second_grad,
            shift_second_grad,
        ),
    )


def as_blocks(array, dim, peers):
    before, after = (array.shape[:dim], array.shape[dim + 1 :])
    split = array.reshape(*before, peers, array.shape[dim] // peers, *after)
    return jnp.moveaxis(split, dim, 0).reshape(peers, -1)


def from_blocks(flat, shape, dim, peers):
    block_shape = (*shape[:dim], shape[dim] // peers, *shape[dim + 1 :])
    return flat.reshape(block_shape)


def split_by_size(arrays):
    big = [i for i, a in enumerate(arrays) if a[0].size % 128 == 0]
    small = [i for i, a in enumerate(arrays) if a[0].size % 128 != 0]
    return (big, small)


def in_rows(blocks, big, small):
    count = blocks[0].shape[0]
    rest = jnp.concatenate([blocks[i].reshape(count, -1) for i in small], axis=1)
    spare = -rest.shape[1] % 2048
    rest = jnp.concatenate([rest, jnp.zeros((count, spare), rest.dtype)], axis=1)
    rows = [blocks[i].reshape(count, -1, 128) for i in big] + [rest.reshape(count, -1, 128)]
    return jnp.concatenate(rows, axis=1)


def out_of_rows(rows, shapes, big, small):
    count = rows.shape[0]
    parts, at = ({}, 0)
    for i in big:
        height = math.prod(shapes[i]) // 128
        parts[i] = rows[:, at : at + height].reshape(count, *shapes[i])
        at += height
    rest = rows[:, at:].reshape(count, -1)
    at = 0
    for i in small:
        width = math.prod(shapes[i])
        parts[i] = rest[:, at : at + width].reshape(count, *shapes[i])
        at += width
    return [parts[i] for i in range(len(shapes))]


def reduce_blocks(blocks):
    big, small = split_by_size(blocks)
    rows = in_rows(blocks, big, small)
    total = lax.psum_scatter(
        rows.reshape(-1, 128), ("section", "dp"), scatter_dimension=0, tiled=True
    )
    return [part[0] for part in out_of_rows(total[None], [b.shape[1:] for b in blocks], big, small)]


def sum_at_end(grads_zero, grads_last, dims, late):
    peers = lax.axis_size("dp")
    blocks = [
        jnp.concatenate(
            [as_blocks(g0.astype(jnp.bfloat16), d, peers), as_blocks(g1.astype(jnp.bfloat16), d, peers)]
        )
        for g0, g1, d in zip(grads_zero, grads_last, dims)
    ]
    early = [i for i in range(len(blocks)) if i not in late]
    parts = dict(zip(early, reduce_blocks([blocks[i] for i in early])))
    parts.update(zip(late, reduce_blocks([blocks[i] for i in late])))
    return tuple(
        from_blocks(parts[i].astype(jnp.float32), g.shape, d, peers)[None]
        for i, (g, d) in enumerate(zip(grads_zero, dims))
    )


def unpack_layer(gathered_rows, weights, dims, big, small):
    parts = out_of_rows(gathered_rows, [w.shape for w in weights], big, small)
    gathered = []
    for part, d in zip(parts, dims):
        part = jnp.moveaxis(part, 0, d)
        shape = part.shape
        gathered.append(part.reshape(*shape[:d], shape[d] * shape[d + 1], *shape[d + 2 :]))
    return tuple(gathered)


def gather_all(weights, dims, is_first):
    big, small = split_by_size([w[None] for w in weights])
    own = in_rows([w[None] for w in weights], big, small)[0]
    other = lax.ppermute(own, "section", [(0, 1), (1, 0)])
    first_rows = lax.all_gather(jnp.where(is_first, own, other), "dp", axis=0, tiled=False)
    last_rows = lax.all_gather(jnp.where(is_first, other, own), "dp", axis=0, tiled=False)
    return (
        unpack_layer(first_rows, weights, dims, big, small),
        unpack_layer(last_rows, weights, dims, big, small),
    )


def shards(
    inputs,
    cotangent,
    packed_weight,
    bias_pair,
    output_weight,
    output_bias,
    expand_weight,
    expand_bias,
    contract_weight,
    contract_bias,
    gain_first,
    shift_first,
    gain_second,
    shift_second,
):
    dims = (0, 1, 1, 0, 0, 0, 1, 0, 0, 0, 0, 0)
    section_index = lax.axis_index("section")
    is_first = section_index == 0
    weights_zero, weights_last = gather_all(
        (
            packed_weight[0],
            bias_pair[0],
            output_weight[0],
            output_bias[0],
            expand_weight[0],
            expand_bias[0],
            contract_weight[0],
            contract_bias[0],
            gain_first[0],
            shift_first[0],
            gain_second[0],
            shift_second[0],
        ),
        dims,
        is_first,
    )
    stream = lax.dynamic_index_in_dim(inputs, section_index, axis=0, keepdims=False)
    out_grad = lax.dynamic_index_in_dim(cotangent, section_index, axis=0, keepdims=False)
    middle, kept_zero = layer_forward(stream, weights_zero)
    final, kept_last = layer_forward(middle, weights_last)
    other_middle = lax.ppermute(middle, "section", [(1, 0)])
    other_final = lax.ppermute(final, "section", [(0, 1)])
    middle_grad, grads_last = layer_backward(out_grad, kept_last, weights_last)
    other_middle_grad = lax.ppermute(middle_grad, "section", [(0, 1)])
    input_grad, grads_zero = layer_backward(middle_grad, kept_zero, weights_zero)
    other_input_grad = lax.ppermute(input_grad, "section", [(1, 0)])
    reduced = sum_at_end(grads_zero, grads_last, dims, (0, 1, 8, 9))
    section_outputs = jnp.where(
        is_first, jnp.stack([middle, other_middle]), jnp.stack([other_final, final])
    )[None]
    section_grads = jnp.where(
        is_first,
        jnp.stack([input_grad, other_input_grad]),
        jnp.stack([other_middle_grad, middle_grad]),
    )[None]
    return (section_outputs, section_grads) + tuple(reduced)


def solution(mesh):
    in_specs = (
        P(None, "dp", None, "tensor"),
        P(None, "dp", None, "tensor"),
        P("section", "dp", None, "tensor"),
        P("section", None, ("tensor", "dp")),
        P("section", "tensor", "dp"),
        P("section", ("tensor", "dp")),
        P("section", "dp", "tensor"),
        P("section", ("tensor", "dp")),
        P("section", "tensor", "dp"),
        P("section", ("tensor", "dp")),
        P("section", ("tensor", "dp")),
        P("section", ("tensor", "dp")),
        P("section", ("tensor", "dp")),
        P("section", ("tensor", "dp")),
    )
    out_specs = (
        P("section", None, "dp", None, "tensor"),
        P("section", None, "dp", None, "tensor"),
        P("section", "dp", None, "tensor"),
        P("section", None, ("tensor", "dp")),
        P("section", "tensor", "dp"),
        P("section", ("tensor", "dp")),
        P("section", "dp", "tensor"),
        P("section", ("tensor", "dp")),
        P("section", "tensor", "dp"),
        P("section", ("tensor", "dp")),
        P("section", ("tensor", "dp")),
        P("section", ("tensor", "dp")),
        P("section", ("tensor", "dp")),
        P("section", ("tensor", "dp")),
    )
    return jax.shard_map(shards, mesh=mesh, in_specs=in_specs, out_specs=out_specs, check_vma=False)
```

```python
import math

import jax
import jax.numpy as jnp
from jax import lax
from jax.sharding import PartitionSpec as P

HEAD_DIM = 64


epsilon = 1e-05
gelu_coef = math.sqrt(2.0 / math.pi)
masked_value = -1e30


def sent_to_all(array, axis):
    copies = jnp.broadcast_to(array, (lax.axis_size(axis), *array.shape))
    return lax.all_to_all(copies, axis, split_axis=0, concat_axis=0, tiled=True)


def taken_together(array, axis):
    return sent_to_all(array, axis).sum(axis=0)


def in_one(arrays, axis):
    ends = [0]
    for a in arrays:
        ends.append(ends[-1] + a.size)
    subtotal = taken_together(jnp.concatenate([a.ravel() for a in arrays]), axis)
    return tuple((subtotal[b:e].reshape(a.shape) for a, b, e in zip(arrays, ends, ends[1:])))


def joined_along(parts, dim):
    parts = jnp.moveaxis(parts, 0, dim)
    shape = parts.shape
    return parts.reshape(*shape[:dim], shape[dim] * shape[dim + 1], *shape[dim + 2 :])


def collect(array, axis, dim):
    parts = sent_to_all(array, axis)
    return joined_along(parts, dim)


def in_blocks(array, dim, peers):
    before, after = (array.shape[:dim], array.shape[dim + 1 :])
    return jnp.moveaxis(array.reshape(*before, peers, -1, *after), dim, 0)


def summed_on_arrival(array, axis, dim):
    parts = in_blocks(array, dim, lax.axis_size(axis))
    arrived = lax.all_to_all(parts, axis, split_axis=0, concat_axis=0, tiled=True)
    return arrived.astype(jnp.float32).sum(axis=0)


def side_by_side(arrays, axis, dim, along):
    both = jnp.concatenate(arrays, axis=along)
    result, at, gathered = (lax.psum_scatter(both, axis, scatter_dimension=dim, tiled=True), 0, [])
    for a in arrays:
        gathered.append(lax.slice_in_dim(result, at, at + a.shape[along], axis=along))
        at += a.shape[along]
    return tuple(gathered)


def in_one_piece(arrays, axis, dim, along):
    both = jnp.concatenate(arrays, axis=along)
    result, at, gathered = (lax.all_gather(both, axis, axis=dim, tiled=True), 0, [])
    for a in arrays:
        gathered.append(lax.slice_in_dim(result, at, at + a.shape[along], axis=along))
        at += a.shape[along]
    return tuple(gathered)


def from_behind(array, axis, by):
    peers = lax.axis_size(axis)
    pairs = [(i, i + by) for i in range(peers) if 0 <= i + by < peers]
    return lax.ppermute(array, axis, pairs)


def gelu_tanh(values):
    return (
        0.5 * values * (1.0 + jnp.tanh(gelu_coef * (values + 0.044715 * values * values * values)))
    )


def norm_forward(stream, gain, offset, extra=None):
    width_all = stream.shape[1] * lax.axis_size("tensor")
    totals, squares = in_one((jnp.sum(stream, axis=1), jnp.sum(stream * stream, axis=1)), "tensor")
    mean_row = (totals / width_all)[:, None]
    var_row = (squares / width_all)[:, None] - mean_row * mean_row
    inv_scale = lax.rsqrt(var_row + epsilon)
    normal_part = (stream - mean_row) * inv_scale
    normed = (normal_part * gain + offset).astype(jnp.bfloat16)
    if extra is None:
        return (collect(normed, "tensor", 1), normal_part, inv_scale, None)
    both = collect(jnp.stack([normed, extra]), "tensor", 2)
    return (both[0], normal_part, inv_scale, both[1])


def norm_backward(partial_term, normal_part, inv_scale, gain):
    width_all = partial_term.shape[1]
    d_normed = summed_on_arrival(partial_term.astype(jnp.bfloat16), "tensor", 1)
    gain_grad = jnp.sum(d_normed * normal_part, axis=0)
    offset_grad = jnp.sum(d_normed, axis=0)
    scaled = d_normed * gain
    first_sum, second_sum = in_one(
        (jnp.sum(scaled, axis=1), jnp.sum(scaled * normal_part, axis=1)), "tensor"
    )
    stream_grad = inv_scale * (
        scaled - first_sum[:, None] / width_all - normal_part * second_sum[:, None] / width_all
    )
    return (stream_grad, gain_grad, offset_grad)


def branch_sum(partial_term):
    return summed_on_arrival(partial_term.astype(jnp.bfloat16), "tensor", 1)


def branch_grad(stream_grad):
    return collect(stream_grad.astype(jnp.bfloat16), "tensor", 1)


def causal_scores(queries, keys_in):
    length = queries.shape[0]
    scale_factor = queries.shape[2] ** (-0.5)
    scores = (
        jnp.einsum("qhe,khe->hqk", queries, keys_in, preferred_element_type=jnp.float32)
        * scale_factor
    )
    causal = lax.broadcasted_iota(jnp.int32, (length, length), 0) >= lax.broadcasted_iota(
        jnp.int32, (length, length), 1
    )
    return (jnp.where(causal[None], scores, masked_value), scale_factor)


def attend(operands):
    queries, keys_in, values_in = operands
    masked, scale_factor = causal_scores(queries, keys_in)
    highest = jnp.max(masked, axis=2, keepdims=True)
    logsum = highest + jnp.log(jnp.sum(jnp.exp(masked - highest), axis=2, keepdims=True))
    weights_low = jnp.exp(masked - logsum).astype(jnp.bfloat16)
    mixture = jnp.einsum("hqk,khe->qhe", weights_low, values_in, preferred_element_type=jnp.float32)
    return (mixture.astype(jnp.bfloat16), logsum[:, :, 0])


def attend_back(operands):
    queries, keys_in, values_in, logsum, mixed_grad = operands
    masked, scale_factor = causal_scores(queries, keys_in)
    probs_full = jnp.exp(masked - logsum[:, :, None])
    probs_grad = jnp.einsum(
        "qhe,khe->hqk", mixed_grad, values_in, preferred_element_type=jnp.float32
    )
    row_dot = jnp.sum(probs_full * probs_grad, axis=2, keepdims=True)
    score_grad = (probs_full * (probs_grad - row_dot)).astype(jnp.bfloat16)
    query_grad = (
        jnp.einsum("hqk,khe->qhe", score_grad, keys_in, preferred_element_type=jnp.float32)
        * scale_factor
    )
    key_grad = (
        jnp.einsum("hqk,qhe->khe", score_grad, queries, preferred_element_type=jnp.float32)
        * scale_factor
    )
    value_grad = jnp.einsum(
        "hqk,qhe->khe",
        probs_full.astype(jnp.bfloat16),
        mixed_grad,
        preferred_element_type=jnp.float32,
    )
    return (
        query_grad.astype(jnp.bfloat16),
        key_grad.astype(jnp.bfloat16),
        value_grad.astype(jnp.bfloat16),
    )


def attention_forward(normed_one, packed_weight, bias_pair, shape_heads, rows_count, width_part):
    packed = jnp.einsum(
        "nd,dcf->ncf", normed_one, packed_weight, preferred_element_type=jnp.float32
    )
    queries = (packed[:, 0] + bias_pair[0]).astype(jnp.bfloat16)
    keys_in = packed[:, 1].astype(jnp.bfloat16)
    values_in = (packed[:, 2] + bias_pair[1]).astype(jnp.bfloat16)
    mixture, logsum = lax.map(
        attend,
        (
            queries.reshape(shape_heads),
            keys_in.reshape(shape_heads),
            values_in.reshape(shape_heads),
        ),
    )
    return (queries, keys_in, values_in, logsum, mixture.reshape(rows_count, width_part))


def attention_backward(branch_one, kept_part, output_weight, shape_heads, rows_count, width_part):
    queries, keys_in, values_in, logsum, mixed_rows, normed_one = kept_part
    output_weight_grad = jnp.einsum(
        "nf,nd->fd", mixed_rows, branch_one, preferred_element_type=jnp.float32
    )
    mixed_grad = jnp.einsum(
        "nd,fd->nf", branch_one, output_weight, preferred_element_type=jnp.float32
    ).astype(jnp.bfloat16)
    query_grad, key_grad, value_grad = lax.map(
        attend_back,
        (
            queries.reshape(shape_heads),
            keys_in.reshape(shape_heads),
            values_in.reshape(shape_heads),
            logsum,
            mixed_grad.reshape(shape_heads),
        ),
    )
    query_rows = query_grad.reshape(rows_count, width_part)
    key_rows = key_grad.reshape(rows_count, width_part)
    value_rows = value_grad.reshape(rows_count, width_part)
    packed_grad = jnp.stack([query_rows, key_rows, value_rows], axis=1)
    bias_pair_grad = jnp.stack(
        [
            jnp.sum(query_rows.astype(jnp.float32), axis=0),
            jnp.sum(value_rows.astype(jnp.float32), axis=0),
        ]
    )
    packed_weight_grad = jnp.einsum(
        "nd,ncf->dcf", normed_one, packed_grad, preferred_element_type=jnp.float32
    )
    return (packed_grad, packed_weight_grad, bias_pair_grad, output_weight_grad)


def layer_forward(stream, weights, extra=None):
    (
        packed_weight,
        bias_pair,
        output_weight,
        output_bias,
        expand_weight,
        expand_bias,
        contract_weight,
        contract_bias,
        gain_first,
        shift_first,
        gain_second,
        shift_second,
    ) = weights
    seq_count, length, width_part = stream.shape
    rows_count = seq_count * length
    shape_heads = (seq_count, length, width_part // HEAD_DIM, HEAD_DIM)
    stream_rows = stream.reshape(rows_count, width_part)
    normed_one, normal_one, inv_one, extra_full = norm_forward(
        stream_rows, gain_first, shift_first, extra
    )
    queries, keys_in, values_in, logsum, mixed_rows = attention_forward(
        normed_one, packed_weight, bias_pair, shape_heads, rows_count, width_part
    )
    residual = (
        stream_rows
        + branch_sum(jnp.dot(mixed_rows, output_weight, preferred_element_type=jnp.float32))
        + output_bias
    )
    normed_two, normal_two, inv_two, _ = norm_forward(residual, gain_second, shift_second)
    hidden_pre = (
        jnp.dot(normed_two, expand_weight, preferred_element_type=jnp.float32) + expand_bias
    )
    hidden = gelu_tanh(hidden_pre).astype(jnp.bfloat16)
    result = (
        residual
        + branch_sum(jnp.dot(hidden, contract_weight, preferred_element_type=jnp.float32))
        + contract_bias
    )
    kept_values = (
        normed_one,
        normal_one,
        inv_one,
        queries,
        keys_in,
        values_in,
        logsum,
        mixed_rows,
        normed_two,
        normal_two,
        inv_two,
        hidden_pre,
        hidden,
    )
    return (result.reshape(stream.shape), kept_values, extra_full)


def layer_backward(out_grad, kept_values, weights, branch_two=None):
    (
        packed_weight,
        bias_pair,
        output_weight,
        output_bias,
        expand_weight,
        expand_bias,
        contract_weight,
        contract_bias,
        gain_first,
        shift_first,
        gain_second,
        shift_second,
    ) = weights
    (
        normed_one,
        normal_one,
        inv_one,
        queries,
        keys_in,
        values_in,
        logsum,
        mixed_rows,
        normed_two,
        normal_two,
        inv_two,
        hidden_pre,
        hidden,
    ) = kept_values
    seq_count, length, width_part = out_grad.shape
    rows_count = seq_count * length
    shape_heads = (seq_count, length, width_part // HEAD_DIM, HEAD_DIM)
    grad_rows = out_grad.reshape(rows_count, width_part)
    contract_bias_grad = jnp.sum(grad_rows, axis=0)
    if branch_two is None:
        branch_two = branch_grad(grad_rows)
    contract_weight_grad = jnp.einsum(
        "nf,nd->fd", hidden, branch_two, preferred_element_type=jnp.float32
    )
    hidden_grad = jnp.einsum(
        "nd,fd->nf", branch_two, contract_weight, preferred_element_type=jnp.float32
    )
    pre_grad = jax.vjp(gelu_tanh, hidden_pre)[1](hidden_grad)[0].astype(jnp.bfloat16)
    expand_bias_grad = jnp.sum(pre_grad.astype(jnp.float32), axis=0)
    expand_weight_grad = jnp.einsum(
        "nd,nf->df", normed_two, pre_grad, preferred_element_type=jnp.float32
    )
    second_grad, gain_second_grad, shift_second_grad = norm_backward(
        jnp.einsum("nf,df->nd", pre_grad, expand_weight, preferred_element_type=jnp.float32),
        normal_two,
        inv_two,
        gain_second,
    )
    residual_grad = grad_rows + second_grad
    output_bias_grad = jnp.sum(residual_grad, axis=0)
    branch_one = branch_grad(residual_grad)
    packed_grad, packed_weight_grad, bias_pair_grad, output_weight_grad = attention_backward(
        branch_one,
        (queries, keys_in, values_in, logsum, mixed_rows, normed_one),
        output_weight,
        shape_heads,
        rows_count,
        width_part,
    )
    first_grad, gain_first_grad, shift_first_grad = norm_backward(
        jnp.einsum("ncf,dcf->nd", packed_grad, packed_weight, preferred_element_type=jnp.float32),
        normal_one,
        inv_one,
        gain_first,
    )
    input_grad = (residual_grad + first_grad).reshape(out_grad.shape)
    return (
        input_grad,
        (
            packed_weight_grad,
            bias_pair_grad,
            output_weight_grad,
            output_bias_grad,
            expand_weight_grad,
            expand_bias_grad,
            contract_weight_grad,
            contract_bias_grad,
            gain_first_grad,
            shift_first_grad,
            gain_second_grad,
            shift_second_grad,
        ),
    )


def as_blocks(array, dim, peers):
    before, after = (array.shape[:dim], array.shape[dim + 1 :])
    split = array.reshape(*before, peers, array.shape[dim] // peers, *after)
    return jnp.moveaxis(split, dim, 0).reshape(peers, -1)


def from_blocks(flat, shape, dim, peers):
    block_shape = (*shape[:dim], shape[dim] // peers, *shape[dim + 1 :])
    return flat.reshape(block_shape)


def split_by_size(arrays):
    big = [i for i, a in enumerate(arrays) if a[0].size % 128 == 0]
    small = [i for i, a in enumerate(arrays) if a[0].size % 128 != 0]
    return (big, small)


def in_rows(blocks, big, small):
    count = blocks[0].shape[0]
    rest = jnp.concatenate([blocks[i].reshape(count, -1) for i in small], axis=1)
    spare = -rest.shape[1] % 2048
    rest = jnp.concatenate([rest, jnp.zeros((count, spare), rest.dtype)], axis=1)
    rows = [blocks[i].reshape(count, -1, 128) for i in big] + [rest.reshape(count, -1, 128)]
    return jnp.concatenate(rows, axis=1)


def out_of_rows(rows, shapes, big, small):
    count = rows.shape[0]
    parts, at = ({}, 0)
    for i in big:
        height = math.prod(shapes[i]) // 128
        parts[i] = rows[:, at : at + height].reshape(count, *shapes[i])
        at += height
    rest = rows[:, at:].reshape(count, -1)
    at = 0
    for i in small:
        width = math.prod(shapes[i])
        parts[i] = rest[:, at : at + width].reshape(count, *shapes[i])
        at += width
    return [parts[i] for i in range(len(shapes))]


def sum_at_end(grads_zero, grads_last, dims):
    peers = lax.axis_size("dp")
    blocks = [
        jnp.concatenate(
            [as_blocks(g0.astype(jnp.bfloat16), d, peers), as_blocks(g1.astype(jnp.bfloat16), d, peers)]
        )
        for g0, g1, d in zip(grads_zero, grads_last, dims)
    ]
    big, small = split_by_size(blocks)
    rows = in_rows(blocks, big, small)
    total = lax.psum_scatter(
        rows.reshape(-1, 128), ("section", "dp"), scatter_dimension=0, tiled=True
    )
    shapes = [block.shape[1:] for block in blocks]
    parts = out_of_rows(total[None], shapes, big, small)
    return tuple(
        from_blocks(part[0].astype(jnp.float32), g.shape, d, peers)[None]
        for part, g, d in zip(parts, grads_zero, dims)
    )


def unpack_layer(gathered_rows, weights, dims, big, small):
    parts = out_of_rows(gathered_rows, [w.shape for w in weights], big, small)
    gathered = []
    for part, d in zip(parts, dims):
        part = jnp.moveaxis(part, 0, d)
        shape = part.shape
        gathered.append(part.reshape(*shape[:d], shape[d] * shape[d + 1], *shape[d + 2 :]))
    return tuple(gathered)


def gather_all(weights, dims, is_first):
    big, small = split_by_size([w[None] for w in weights])
    own = in_rows([w[None] for w in weights], big, small)[0]
    other = lax.ppermute(own, "section", [(0, 1), (1, 0)])
    first_rows = lax.all_gather(jnp.where(is_first, own, other), "dp", axis=0, tiled=False)
    last_rows = lax.all_gather(jnp.where(is_first, other, own), "dp", axis=0, tiled=False)
    return (
        unpack_layer(first_rows, weights, dims, big, small),
        unpack_layer(last_rows, weights, dims, big, small),
    )


def shards(
    inputs,
    cotangent,
    packed_weight,
    bias_pair,
    output_weight,
    output_bias,
    expand_weight,
    expand_bias,
    contract_weight,
    contract_bias,
    gain_first,
    shift_first,
    gain_second,
    shift_second,
):
    dims = (0, 1, 1, 0, 0, 0, 1, 0, 0, 0, 0, 0)
    section_index = lax.axis_index("section")
    is_first = section_index == 0
    weights_zero, weights_last = gather_all(
        (
            packed_weight[0],
            bias_pair[0],
            output_weight[0],
            output_bias[0],
            expand_weight[0],
            expand_bias[0],
            contract_weight[0],
            contract_bias[0],
            gain_first[0],
            shift_first[0],
            gain_second[0],
            shift_second[0],
        ),
        dims,
        is_first,
    )
    stream = lax.dynamic_index_in_dim(inputs, section_index, axis=0, keepdims=False)
    out_grad = lax.dynamic_index_in_dim(cotangent, section_index, axis=0, keepdims=False)
    grad_rows = out_grad.reshape(-1, out_grad.shape[-1]).astype(jnp.bfloat16)
    middle, kept_zero, grad_full = layer_forward(stream, weights_zero, grad_rows)
    final, kept_last, _ = layer_forward(middle, weights_last)
    other_middle = lax.ppermute(middle, "section", [(1, 0)])
    other_final = lax.ppermute(final, "section", [(0, 1)])
    middle_grad, grads_last = layer_backward(out_grad, kept_last, weights_last, grad_full)
    other_middle_grad = lax.ppermute(middle_grad, "section", [(0, 1)])
    input_grad, grads_zero = layer_backward(middle_grad, kept_zero, weights_zero)
    other_input_grad = lax.ppermute(input_grad, "section", [(1, 0)])
    reduced = sum_at_end(grads_zero, grads_last, dims)
    section_outputs = jnp.where(
        is_first, jnp.stack([middle, other_middle]), jnp.stack([other_final, final])
    )[None]
    section_grads = jnp.where(
        is_first,
        jnp.stack([input_grad, other_input_grad]),
        jnp.stack([other_middle_grad, middle_grad]),
    )[None]
    return (section_outputs, section_grads) + tuple(reduced)


def solution(mesh):
    in_specs = (
        P(None, "dp", None, "tensor"),
        P(None, "dp", None, "tensor"),
        P("section", "dp", None, "tensor"),
        P("section", None, ("tensor", "dp")),
        P("section", "tensor", "dp"),
        P("section", ("tensor", "dp")),
        P("section", "dp", "tensor"),
        P("section", ("tensor", "dp")),
        P("section", "tensor", "dp"),
        P("section", ("tensor", "dp")),
        P("section", ("tensor", "dp")),
        P("section", ("tensor", "dp")),
        P("section", ("tensor", "dp")),
        P("section", ("tensor", "dp")),
    )
    out_specs = (
        P("section", None, "dp", None, "tensor"),
        P("section", None, "dp", None, "tensor"),
        P("section", "dp", None, "tensor"),
        P("section", None, ("tensor", "dp")),
        P("section", "tensor", "dp"),
        P("section", ("tensor", "dp")),
        P("section", "dp", "tensor"),
        P("section", ("tensor", "dp")),
        P("section", "tensor", "dp"),
        P("section", ("tensor", "dp")),
        P("section", ("tensor", "dp")),
        P("section", ("tensor", "dp")),
        P("section", ("tensor", "dp")),
        P("section", ("tensor", "dp")),
    )
    return jax.shard_map(shards, mesh=mesh, in_specs=in_specs, out_specs=out_specs, check_vma=False)
```

```python
import math

import jax
import jax.numpy as jnp
from jax import lax
from jax.sharding import PartitionSpec as P

HEAD_DIM = 64


epsilon = 1e-05
gelu_coef = math.sqrt(2.0 / math.pi)
masked_value = -1e30


def sent_to_all(array, axis):
    copies = jnp.broadcast_to(array, (lax.axis_size(axis), *array.shape))
    return lax.all_to_all(copies, axis, split_axis=0, concat_axis=0, tiled=True)


def taken_together(array, axis):
    return sent_to_all(array, axis).sum(axis=0)


def in_one(arrays, axis):
    ends = [0]
    for a in arrays:
        ends.append(ends[-1] + a.size)
    subtotal = taken_together(jnp.concatenate([a.ravel() for a in arrays]), axis)
    return tuple((subtotal[b:e].reshape(a.shape) for a, b, e in zip(arrays, ends, ends[1:])))


def joined_along(parts, dim):
    parts = jnp.moveaxis(parts, 0, dim)
    shape = parts.shape
    return parts.reshape(*shape[:dim], shape[dim] * shape[dim + 1], *shape[dim + 2 :])


def collect(array, axis, dim):
    parts = sent_to_all(array, axis)
    return joined_along(parts, dim)


def in_blocks(array, dim, peers):
    before, after = (array.shape[:dim], array.shape[dim + 1 :])
    return jnp.moveaxis(array.reshape(*before, peers, -1, *after), dim, 0)


def summed_on_arrival(array, axis, dim):
    parts = in_blocks(array, dim, lax.axis_size(axis))
    arrived = lax.all_to_all(parts, axis, split_axis=0, concat_axis=0, tiled=True)
    return arrived.astype(jnp.float32).sum(axis=0)


def side_by_side(arrays, axis, dim, along):
    both = jnp.concatenate(arrays, axis=along)
    result, at, gathered = (lax.psum_scatter(both, axis, scatter_dimension=dim, tiled=True), 0, [])
    for a in arrays:
        gathered.append(lax.slice_in_dim(result, at, at + a.shape[along], axis=along))
        at += a.shape[along]
    return tuple(gathered)


def in_one_piece(arrays, axis, dim, along):
    both = jnp.concatenate(arrays, axis=along)
    result, at, gathered = (lax.all_gather(both, axis, axis=dim, tiled=True), 0, [])
    for a in arrays:
        gathered.append(lax.slice_in_dim(result, at, at + a.shape[along], axis=along))
        at += a.shape[along]
    return tuple(gathered)


def from_behind(array, axis, by):
    peers = lax.axis_size(axis)
    pairs = [(i, i + by) for i in range(peers) if 0 <= i + by < peers]
    return lax.ppermute(array, axis, pairs)


def gelu_tanh(values):
    return (
        0.5 * values * (1.0 + jnp.tanh(gelu_coef * (values + 0.044715 * values * values * values)))
    )


def norm_forward(stream, gain, offset, extra=None):
    width_all = stream.shape[1] * lax.axis_size("tensor")
    totals, squares = in_one((jnp.sum(stream, axis=1), jnp.sum(stream * stream, axis=1)), "tensor")
    mean_row = (totals / width_all)[:, None]
    var_row = (squares / width_all)[:, None] - mean_row * mean_row
    inv_scale = lax.rsqrt(var_row + epsilon)
    normal_part = (stream - mean_row) * inv_scale
    normed = (normal_part * gain + offset).astype(jnp.bfloat16)
    if extra is None:
        return (collect(normed, "tensor", 1), normal_part, inv_scale, None)
    both = collect(jnp.stack([normed, extra]), "tensor", 2)
    return (both[0], normal_part, inv_scale, both[1])


def norm_backward(partial_term, normal_part, inv_scale, gain):
    width_all = partial_term.shape[1]
    d_normed = summed_on_arrival(partial_term.astype(jnp.bfloat16), "tensor", 1)
    gain_grad = jnp.sum(d_normed * normal_part, axis=0)
    offset_grad = jnp.sum(d_normed, axis=0)
    scaled = d_normed * gain
    first_sum, second_sum = in_one(
        (jnp.sum(scaled, axis=1), jnp.sum(scaled * normal_part, axis=1)), "tensor"
    )
    stream_grad = inv_scale * (
        scaled - first_sum[:, None] / width_all - normal_part * second_sum[:, None] / width_all
    )
    return (stream_grad, gain_grad, offset_grad)


def branch_sum(partial_term):
    return summed_on_arrival(partial_term.astype(jnp.bfloat16), "tensor", 1)


def branch_grad(stream_grad):
    return collect(stream_grad.astype(jnp.bfloat16), "tensor", 1)


def causal_scores(queries, keys_in):
    length = queries.shape[0]
    scale_factor = queries.shape[2] ** (-0.5)
    scores = (
        jnp.einsum("qhe,khe->hqk", queries, keys_in, preferred_element_type=jnp.float32)
        * scale_factor
    )
    causal = lax.broadcasted_iota(jnp.int32, (length, length), 0) >= lax.broadcasted_iota(
        jnp.int32, (length, length), 1
    )
    return (jnp.where(causal[None], scores, masked_value), scale_factor)


def attend(operands):
    queries, keys_in, values_in = operands
    masked, scale_factor = causal_scores(queries, keys_in)
    highest = jnp.max(masked, axis=2, keepdims=True)
    logsum = highest + jnp.log(jnp.sum(jnp.exp(masked - highest), axis=2, keepdims=True))
    weights_low = jnp.exp(masked - logsum).astype(jnp.bfloat16)
    mixture = jnp.einsum("hqk,khe->qhe", weights_low, values_in, preferred_element_type=jnp.float32)
    return (mixture.astype(jnp.bfloat16), logsum[:, :, 0])


def attend_back(operands):
    queries, keys_in, values_in, logsum, mixed_grad = operands
    masked, scale_factor = causal_scores(queries, keys_in)
    probs_full = jnp.exp(masked - logsum[:, :, None])
    probs_grad = jnp.einsum(
        "qhe,khe->hqk", mixed_grad, values_in, preferred_element_type=jnp.float32
    )
    row_dot = jnp.sum(probs_full * probs_grad, axis=2, keepdims=True)
    score_grad = (probs_full * (probs_grad - row_dot)).astype(jnp.bfloat16)
    query_grad = (
        jnp.einsum("hqk,khe->qhe", score_grad, keys_in, preferred_element_type=jnp.float32)
        * scale_factor
    )
    key_grad = (
        jnp.einsum("hqk,qhe->khe", score_grad, queries, preferred_element_type=jnp.float32)
        * scale_factor
    )
    value_grad = jnp.einsum(
        "hqk,qhe->khe",
        probs_full.astype(jnp.bfloat16),
        mixed_grad,
        preferred_element_type=jnp.float32,
    )
    return (
        query_grad.astype(jnp.bfloat16),
        key_grad.astype(jnp.bfloat16),
        value_grad.astype(jnp.bfloat16),
    )


def attention_forward(normed_one, packed_weight, bias_pair, shape_heads, rows_count, width_part):
    packed = jnp.einsum(
        "nd,dcf->ncf", normed_one, packed_weight, preferred_element_type=jnp.float32
    )
    queries = (packed[:, 0] + bias_pair[0]).astype(jnp.bfloat16)
    keys_in = packed[:, 1].astype(jnp.bfloat16)
    values_in = (packed[:, 2] + bias_pair[1]).astype(jnp.bfloat16)
    mixture, logsum = lax.map(
        attend,
        (
            queries.reshape(shape_heads),
            keys_in.reshape(shape_heads),
            values_in.reshape(shape_heads),
        ),
    )
    return (queries, keys_in, values_in, logsum, mixture.reshape(rows_count, width_part))


def attention_backward(branch_one, kept_part, output_weight, shape_heads, rows_count, width_part):
    queries, keys_in, values_in, logsum, mixed_rows, normed_one = kept_part
    output_weight_grad = jnp.einsum(
        "nf,nd->fd", mixed_rows, branch_one, preferred_element_type=jnp.float32
    )
    mixed_grad = jnp.einsum(
        "nd,fd->nf", branch_one, output_weight, preferred_element_type=jnp.float32
    ).astype(jnp.bfloat16)
    query_grad, key_grad, value_grad = lax.map(
        attend_back,
        (
            queries.reshape(shape_heads),
            keys_in.reshape(shape_heads),
            values_in.reshape(shape_heads),
            logsum,
            mixed_grad.reshape(shape_heads),
        ),
    )
    query_rows = query_grad.reshape(rows_count, width_part)
    key_rows = key_grad.reshape(rows_count, width_part)
    value_rows = value_grad.reshape(rows_count, width_part)
    packed_grad = jnp.stack([query_rows, key_rows, value_rows], axis=1)
    bias_pair_grad = jnp.stack(
        [
            jnp.sum(query_rows.astype(jnp.float32), axis=0),
            jnp.sum(value_rows.astype(jnp.float32), axis=0),
        ]
    )
    packed_weight_grad = jnp.einsum(
        "nd,ncf->dcf", normed_one, packed_grad, preferred_element_type=jnp.float32
    )
    return (packed_grad, packed_weight_grad, bias_pair_grad, output_weight_grad)


def layer_forward(stream, weights, extra=None):
    (
        packed_weight,
        bias_pair,
        output_weight,
        output_bias,
        expand_weight,
        expand_bias,
        contract_weight,
        contract_bias,
        gain_first,
        shift_first,
        gain_second,
        shift_second,
    ) = weights
    seq_count, length, width_part = stream.shape
    rows_count = seq_count * length
    shape_heads = (seq_count, length, width_part // HEAD_DIM, HEAD_DIM)
    stream_rows = stream.reshape(rows_count, width_part)
    normed_one, normal_one, inv_one, extra_full = norm_forward(
        stream_rows, gain_first, shift_first, extra
    )
    queries, keys_in, values_in, logsum, mixed_rows = attention_forward(
        normed_one, packed_weight, bias_pair, shape_heads, rows_count, width_part
    )
    residual = (
        stream_rows
        + branch_sum(jnp.dot(mixed_rows, output_weight, preferred_element_type=jnp.float32))
        + output_bias
    )
    normed_two, normal_two, inv_two, _ = norm_forward(residual, gain_second, shift_second)
    hidden_pre = (
        jnp.dot(normed_two, expand_weight, preferred_element_type=jnp.float32) + expand_bias
    )
    hidden = gelu_tanh(hidden_pre).astype(jnp.bfloat16)
    result = (
        residual
        + branch_sum(jnp.dot(hidden, contract_weight, preferred_element_type=jnp.float32))
        + contract_bias
    )
    kept_values = (
        normed_one,
        normal_one,
        inv_one,
        queries,
        keys_in,
        values_in,
        logsum,
        mixed_rows,
        normed_two,
        normal_two,
        inv_two,
        hidden_pre,
        hidden,
    )
    return (result.reshape(stream.shape), kept_values, extra_full)


def layer_backward(out_grad, kept_values, weights, branch_two=None):
    (
        packed_weight,
        bias_pair,
        output_weight,
        output_bias,
        expand_weight,
        expand_bias,
        contract_weight,
        contract_bias,
        gain_first,
        shift_first,
        gain_second,
        shift_second,
    ) = weights
    (
        normed_one,
        normal_one,
        inv_one,
        queries,
        keys_in,
        values_in,
        logsum,
        mixed_rows,
        normed_two,
        normal_two,
        inv_two,
        hidden_pre,
        hidden,
    ) = kept_values
    seq_count, length, width_part = out_grad.shape
    rows_count = seq_count * length
    shape_heads = (seq_count, length, width_part // HEAD_DIM, HEAD_DIM)
    grad_rows = out_grad.reshape(rows_count, width_part)
    contract_bias_grad = jnp.sum(grad_rows, axis=0)
    if branch_two is None:
        branch_two = branch_grad(grad_rows)
    contract_weight_grad = jnp.einsum(
        "nf,nd->fd", hidden, branch_two, preferred_element_type=jnp.float32
    )
    hidden_grad = jnp.einsum(
        "nd,fd->nf", branch_two, contract_weight, preferred_element_type=jnp.float32
    )
    pre_grad = jax.vjp(gelu_tanh, hidden_pre)[1](hidden_grad)[0].astype(jnp.bfloat16)
    expand_bias_grad = jnp.sum(pre_grad.astype(jnp.float32), axis=0)
    expand_weight_grad = jnp.einsum(
        "nd,nf->df", normed_two, pre_grad, preferred_element_type=jnp.float32
    )
    second_grad, gain_second_grad, shift_second_grad = norm_backward(
        jnp.einsum("nf,df->nd", pre_grad, expand_weight, preferred_element_type=jnp.float32),
        normal_two,
        inv_two,
        gain_second,
    )
    residual_grad = grad_rows + second_grad
    output_bias_grad = jnp.sum(residual_grad, axis=0)
    branch_one = branch_grad(residual_grad)
    packed_grad, packed_weight_grad, bias_pair_grad, output_weight_grad = attention_backward(
        branch_one,
        (queries, keys_in, values_in, logsum, mixed_rows, normed_one),
        output_weight,
        shape_heads,
        rows_count,
        width_part,
    )
    first_grad, gain_first_grad, shift_first_grad = norm_backward(
        jnp.einsum("ncf,dcf->nd", packed_grad, packed_weight, preferred_element_type=jnp.float32),
        normal_one,
        inv_one,
        gain_first,
    )
    input_grad = (residual_grad + first_grad).reshape(out_grad.shape)
    return (
        input_grad,
        (
            packed_weight_grad,
            bias_pair_grad,
            output_weight_grad,
            output_bias_grad,
            expand_weight_grad,
            expand_bias_grad,
            contract_weight_grad,
            contract_bias_grad,
            gain_first_grad,
            shift_first_grad,
            gain_second_grad,
            shift_second_grad,
        ),
    )


def as_blocks(array, dim, peers):
    before, after = (array.shape[:dim], array.shape[dim + 1 :])
    split = array.reshape(*before, peers, array.shape[dim] // peers, *after)
    return jnp.moveaxis(split, dim, 0).reshape(peers, -1)


def from_blocks(flat, shape, dim, peers):
    block_shape = (*shape[:dim], shape[dim] // peers, *shape[dim + 1 :])
    return flat.reshape(block_shape)


def split_by_size(arrays):
    big = [i for i, a in enumerate(arrays) if a[0].size % 128 == 0]
    small = [i for i, a in enumerate(arrays) if a[0].size % 128 != 0]
    return (big, small)


def in_rows(blocks, big, small):
    count = blocks[0].shape[0]
    rest = jnp.concatenate([blocks[i].reshape(count, -1) for i in small], axis=1)
    spare = -rest.shape[1] % 2048
    rest = jnp.concatenate([rest, jnp.zeros((count, spare), rest.dtype)], axis=1)
    rows = [blocks[i].reshape(count, -1, 128) for i in big] + [rest.reshape(count, -1, 128)]
    return jnp.concatenate(rows, axis=1)


def out_of_rows(rows, shapes, big, small):
    count = rows.shape[0]
    parts, at = ({}, 0)
    for i in big:
        height = math.prod(shapes[i]) // 128
        parts[i] = rows[:, at : at + height].reshape(count, *shapes[i])
        at += height
    rest = rows[:, at:].reshape(count, -1)
    at = 0
    for i in small:
        width = math.prod(shapes[i])
        parts[i] = rest[:, at : at + width].reshape(count, *shapes[i])
        at += width
    return [parts[i] for i in range(len(shapes))]


def sum_at_end(grads_zero, grads_last, dims):
    peers = lax.axis_size("dp")
    blocks = [
        jnp.concatenate(
            [as_blocks(g0.astype(jnp.bfloat16), d, peers), as_blocks(g1.astype(jnp.bfloat16), d, peers)]
        )
        for g0, g1, d in zip(grads_zero, grads_last, dims)
    ]
    big, small = split_by_size(blocks)
    rows = in_rows(blocks, big, small)
    total = lax.psum_scatter(
        rows.reshape(-1, 128), ("section", "dp"), scatter_dimension=0, tiled=True
    )
    shapes = [block.shape[1:] for block in blocks]
    parts = out_of_rows(total[None], shapes, big, small)
    return tuple(
        from_blocks(part[0].astype(jnp.float32), g.shape, d, peers)[None]
        for part, g, d in zip(parts, grads_zero, dims)
    )


def unpack_layer(gathered_rows, weights, dims, big, small):
    parts = out_of_rows(gathered_rows, [w.shape for w in weights], big, small)
    gathered = []
    for part, d in zip(parts, dims):
        part = jnp.moveaxis(part, 0, d)
        shape = part.shape
        gathered.append(part.reshape(*shape[:d], shape[d] * shape[d + 1], *shape[d + 2 :]))
    return tuple(gathered)


def gather_all(weights, dims, is_first):
    big, small = split_by_size([w[None] for w in weights])
    own = in_rows([w[None] for w in weights], big, small)[0]
    other = lax.ppermute(own, "section", [(0, 1), (1, 0)])
    first_rows = lax.all_gather(jnp.where(is_first, own, other), "dp", axis=0, tiled=False)
    last_rows = lax.all_gather(jnp.where(is_first, other, own), "dp", axis=0, tiled=False)
    return (
        unpack_layer(first_rows, weights, dims, big, small),
        unpack_layer(last_rows, weights, dims, big, small),
    )


def shards(
    inputs,
    cotangent,
    packed_weight,
    bias_pair,
    output_weight,
    output_bias,
    expand_weight,
    expand_bias,
    contract_weight,
    contract_bias,
    gain_first,
    shift_first,
    gain_second,
    shift_second,
):
    dims = (0, 1, 1, 0, 0, 0, 1, 0, 0, 0, 0, 0)
    section_index = lax.axis_index("section")
    is_first = section_index == 0
    weights_zero, weights_last = gather_all(
        (
            packed_weight[0],
            bias_pair[0],
            output_weight[0],
            output_bias[0],
            expand_weight[0],
            expand_bias[0],
            contract_weight[0],
            contract_bias[0],
            gain_first[0],
            shift_first[0],
            gain_second[0],
            shift_second[0],
        ),
        dims,
        is_first,
    )
    stream = lax.dynamic_index_in_dim(inputs, section_index, axis=0, keepdims=False)
    out_grad = lax.dynamic_index_in_dim(cotangent, section_index, axis=0, keepdims=False)
    grad_rows = out_grad.reshape(-1, out_grad.shape[-1]).astype(jnp.bfloat16)
    middle, kept_zero, grad_full = layer_forward(stream, weights_zero, grad_rows)
    final, kept_last, _ = layer_forward(middle, weights_last)
    other_middle = lax.ppermute(middle, "section", [(1, 0)])
    other_final = lax.ppermute(final, "section", [(0, 1)])
    middle_grad, grads_last = layer_backward(out_grad, kept_last, weights_last, grad_full)
    input_grad, grads_zero = layer_backward(middle_grad, kept_zero, weights_zero)
    other_grad = lax.ppermute(
        jnp.where(is_first, middle_grad, input_grad), "section", [(0, 1), (1, 0)]
    )
    reduced = sum_at_end(grads_zero, grads_last, dims)
    section_outputs = jnp.where(
        is_first, jnp.stack([middle, other_middle]), jnp.stack([other_final, final])
    )[None]
    section_grads = jnp.where(
        is_first,
        jnp.stack([input_grad, other_grad]),
        jnp.stack([other_grad, middle_grad]),
    )[None]
    return (section_outputs, section_grads) + tuple(reduced)


def solution(mesh):
    in_specs = (
        P(None, "dp", None, "tensor"),
        P(None, "dp", None, "tensor"),
        P("section", "dp", None, "tensor"),
        P("section", None, ("tensor", "dp")),
        P("section", "tensor", "dp"),
        P("section", ("tensor", "dp")),
        P("section", "dp", "tensor"),
        P("section", ("tensor", "dp")),
        P("section", "tensor", "dp"),
        P("section", ("tensor", "dp")),
        P("section", ("tensor", "dp")),
        P("section", ("tensor", "dp")),
        P("section", ("tensor", "dp")),
        P("section", ("tensor", "dp")),
    )
    out_specs = (
        P("section", None, "dp", None, "tensor"),
        P("section", None, "dp", None, "tensor"),
        P("section", "dp", None, "tensor"),
        P("section", None, ("tensor", "dp")),
        P("section", "tensor", "dp"),
        P("section", ("tensor", "dp")),
        P("section", "dp", "tensor"),
        P("section", ("tensor", "dp")),
        P("section", "tensor", "dp"),
        P("section", ("tensor", "dp")),
        P("section", ("tensor", "dp")),
        P("section", ("tensor", "dp")),
        P("section", ("tensor", "dp")),
        P("section", ("tensor", "dp")),
    )
    return jax.shard_map(shards, mesh=mesh, in_specs=in_specs, out_specs=out_specs, check_vma=False)
```

```python
import math

import jax
import jax.numpy as jnp
from jax import lax
from jax.sharding import PartitionSpec as P

HEAD_DIM = 64


epsilon = 1e-05
gelu_coef = math.sqrt(2.0 / math.pi)
masked_value = -1e30


def sent_to_all(array, axis):
    copies = jnp.broadcast_to(array, (lax.axis_size(axis), *array.shape))
    return lax.all_to_all(copies, axis, split_axis=0, concat_axis=0, tiled=True)


def taken_together(array, axis):
    return sent_to_all(array, axis).sum(axis=0)


def in_one(arrays, axis):
    ends = [0]
    for a in arrays:
        ends.append(ends[-1] + a.size)
    subtotal = taken_together(jnp.concatenate([a.ravel() for a in arrays]), axis)
    return tuple((subtotal[b:e].reshape(a.shape) for a, b, e in zip(arrays, ends, ends[1:])))


def joined_along(parts, dim):
    parts = jnp.moveaxis(parts, 0, dim)
    shape = parts.shape
    return parts.reshape(*shape[:dim], shape[dim] * shape[dim + 1], *shape[dim + 2 :])


def collect(array, axis, dim):
    parts = sent_to_all(array, axis)
    return joined_along(parts, dim)


def in_blocks(array, dim, peers):
    before, after = (array.shape[:dim], array.shape[dim + 1 :])
    return jnp.moveaxis(array.reshape(*before, peers, -1, *after), dim, 0)


def summed_on_arrival(parts, axis):
    arrived = lax.all_to_all(parts, axis, split_axis=0, concat_axis=0, tiled=True)
    return arrived.astype(jnp.float32).sum(axis=0)


def side_by_side(arrays, axis, dim, along):
    both = jnp.concatenate(arrays, axis=along)
    result, at, gathered = (lax.psum_scatter(both, axis, scatter_dimension=dim, tiled=True), 0, [])
    for a in arrays:
        gathered.append(lax.slice_in_dim(result, at, at + a.shape[along], axis=along))
        at += a.shape[along]
    return tuple(gathered)


def in_one_piece(arrays, axis, dim, along):
    both = jnp.concatenate(arrays, axis=along)
    result, at, gathered = (lax.all_gather(both, axis, axis=dim, tiled=True), 0, [])
    for a in arrays:
        gathered.append(lax.slice_in_dim(result, at, at + a.shape[along], axis=along))
        at += a.shape[along]
    return tuple(gathered)


def from_behind(array, axis, by):
    peers = lax.axis_size(axis)
    pairs = [(i, i + by) for i in range(peers) if 0 <= i + by < peers]
    return lax.ppermute(array, axis, pairs)


def gelu_tanh(values):
    return (
        0.5 * values * (1.0 + jnp.tanh(gelu_coef * (values + 0.044715 * values * values * values)))
    )


def norm_forward(stream, gain, offset, extra=None):
    width_all = stream.shape[1] * lax.axis_size("tensor")
    totals, squares = in_one((jnp.sum(stream, axis=1), jnp.sum(stream * stream, axis=1)), "tensor")
    mean_row = (totals / width_all)[:, None]
    var_row = (squares / width_all)[:, None] - mean_row * mean_row
    inv_scale = lax.rsqrt(var_row + epsilon)
    normal_part = (stream - mean_row) * inv_scale
    normed = (normal_part * gain + offset).astype(jnp.bfloat16)
    if extra is None:
        return (collect(normed, "tensor", 1), normal_part, inv_scale, None)
    both = collect(jnp.stack([normed, extra]), "tensor", 2)
    return (both[0], normal_part, inv_scale, both[1])


def norm_backward(partial_term, normal_part, inv_scale, gain):
    width_all = partial_term.shape[0] * partial_term.shape[2]
    d_normed = summed_on_arrival(partial_term.astype(jnp.bfloat16), "tensor")
    gain_grad = jnp.sum(d_normed * normal_part, axis=0)
    offset_grad = jnp.sum(d_normed, axis=0)
    scaled = d_normed * gain
    first_sum, second_sum = in_one(
        (jnp.sum(scaled, axis=1), jnp.sum(scaled * normal_part, axis=1)), "tensor"
    )
    stream_grad = inv_scale * (
        scaled - first_sum[:, None] / width_all - normal_part * second_sum[:, None] / width_all
    )
    return (stream_grad, gain_grad, offset_grad)


def blocked_product(spec, rows, weight, dim):
    peers = lax.axis_size("tensor")
    shape = weight.shape
    blocked = weight.reshape(*shape[:dim], peers, shape[dim] // peers, *shape[dim + 1 :])
    return jnp.einsum(spec, rows, blocked, preferred_element_type=jnp.float32)


def branch_sum(partial_term):
    return summed_on_arrival(partial_term.astype(jnp.bfloat16), "tensor")


def branch_grad(stream_grad):
    return collect(stream_grad.astype(jnp.bfloat16), "tensor", 1)


def causal_scores(queries, keys_in):
    length = queries.shape[0]
    scale_factor = queries.shape[2] ** (-0.5)
    scores = (
        jnp.einsum("qhe,khe->hqk", queries, keys_in, preferred_element_type=jnp.float32)
        * scale_factor
    )
    causal = lax.broadcasted_iota(jnp.int32, (length, length), 0) >= lax.broadcasted_iota(
        jnp.int32, (length, length), 1
    )
    return (jnp.where(causal[None], scores, masked_value), scale_factor)


def attend(operands):
    queries, keys_in, values_in = operands
    masked, scale_factor = causal_scores(queries, keys_in)
    highest = jnp.max(masked, axis=2, keepdims=True)
    logsum = highest + jnp.log(jnp.sum(jnp.exp(masked - highest), axis=2, keepdims=True))
    weights_low = jnp.exp(masked - logsum).astype(jnp.bfloat16)
    mixture = jnp.einsum("hqk,khe->qhe", weights_low, values_in, preferred_element_type=jnp.float32)
    return (mixture.astype(jnp.bfloat16), logsum[:, :, 0])


def attend_back(operands):
    queries, keys_in, values_in, logsum, mixed_grad = operands
    masked, scale_factor = causal_scores(queries, keys_in)
    probs_full = jnp.exp(masked - logsum[:, :, None])
    probs_grad = jnp.einsum(
        "qhe,khe->hqk", mixed_grad, values_in, preferred_element_type=jnp.float32
    )
    row_dot = jnp.sum(probs_full * probs_grad, axis=2, keepdims=True)
    score_grad = (probs_full * (probs_grad - row_dot)).astype(jnp.bfloat16)
    query_grad = (
        jnp.einsum("hqk,khe->qhe", score_grad, keys_in, preferred_element_type=jnp.float32)
        * scale_factor
    )
    key_grad = (
        jnp.einsum("hqk,qhe->khe", score_grad, queries, preferred_element_type=jnp.float32)
        * scale_factor
    )
    value_grad = jnp.einsum(
        "hqk,qhe->khe",
        probs_full.astype(jnp.bfloat16),
        mixed_grad,
        preferred_element_type=jnp.float32,
    )
    return (
        query_grad.astype(jnp.bfloat16),
        key_grad.astype(jnp.bfloat16),
        value_grad.astype(jnp.bfloat16),
    )


def attention_forward(normed_one, packed_weight, bias_pair, shape_heads, rows_count, width_part):
    packed = jnp.einsum(
        "nd,dcf->ncf", normed_one, packed_weight, preferred_element_type=jnp.float32
    )
    queries = (packed[:, 0] + bias_pair[0]).astype(jnp.bfloat16)
    keys_in = packed[:, 1].astype(jnp.bfloat16)
    values_in = (packed[:, 2] + bias_pair[1]).astype(jnp.bfloat16)
    mixture, logsum = lax.map(
        attend,
        (
            queries.reshape(shape_heads),
            keys_in.reshape(shape_heads),
            values_in.reshape(shape_heads),
        ),
    )
    return (queries, keys_in, values_in, logsum, mixture.reshape(rows_count, width_part))


def attention_backward(branch_one, kept_part, output_weight, shape_heads, rows_count, width_part):
    queries, keys_in, values_in, logsum, mixed_rows, normed_one = kept_part
    output_weight_grad = jnp.einsum(
        "nf,nd->fd", mixed_rows, branch_one, preferred_element_type=jnp.float32
    )
    mixed_grad = jnp.einsum(
        "nd,fd->nf", branch_one, output_weight, preferred_element_type=jnp.float32
    ).astype(jnp.bfloat16)
    query_grad, key_grad, value_grad = lax.map(
        attend_back,
        (
            queries.reshape(shape_heads),
            keys_in.reshape(shape_heads),
            values_in.reshape(shape_heads),
            logsum,
            mixed_grad.reshape(shape_heads),
        ),
    )
    query_rows = query_grad.reshape(rows_count, width_part)
    key_rows = key_grad.reshape(rows_count, width_part)
    value_rows = value_grad.reshape(rows_count, width_part)
    packed_grad = jnp.stack([query_rows, key_rows, value_rows], axis=1)
    bias_pair_grad = jnp.stack(
        [
            jnp.sum(query_rows.astype(jnp.float32), axis=0),
            jnp.sum(value_rows.astype(jnp.float32), axis=0),
        ]
    )
    packed_weight_grad = jnp.einsum(
        "nd,ncf->dcf", normed_one, packed_grad, preferred_element_type=jnp.float32
    )
    return (packed_grad, packed_weight_grad, bias_pair_grad, output_weight_grad)


def layer_forward(stream, weights, extra=None):
    (
        packed_weight,
        bias_pair,
        output_weight,
        output_bias,
        expand_weight,
        expand_bias,
        contract_weight,
        contract_bias,
        gain_first,
        shift_first,
        gain_second,
        shift_second,
    ) = weights
    seq_count, length, width_part = stream.shape
    rows_count = seq_count * length
    shape_heads = (seq_count, length, width_part // HEAD_DIM, HEAD_DIM)
    stream_rows = stream.reshape(rows_count, width_part)
    normed_one, normal_one, inv_one, extra_full = norm_forward(
        stream_rows, gain_first, shift_first, extra
    )
    queries, keys_in, values_in, logsum, mixed_rows = attention_forward(
        normed_one, packed_weight, bias_pair, shape_heads, rows_count, width_part
    )
    residual = (
        stream_rows
        + branch_sum(blocked_product("nf,ftd->tnd", mixed_rows, output_weight, 1))
        + output_bias
    )
    normed_two, normal_two, inv_two, _ = norm_forward(residual, gain_second, shift_second)
    hidden_pre = (
        jnp.dot(normed_two, expand_weight, preferred_element_type=jnp.float32) + expand_bias
    )
    hidden = gelu_tanh(hidden_pre).astype(jnp.bfloat16)
    result = (
        residual
        + branch_sum(blocked_product("nf,ftd->tnd", hidden, contract_weight, 1))
        + contract_bias
    )
    kept_values = (
        normed_one,
        normal_one,
        inv_one,
        queries,
        keys_in,
        values_in,
        logsum,
        mixed_rows,
        normed_two,
        normal_two,
        inv_two,
        hidden_pre,
        hidden,
    )
    return (result.reshape(stream.shape), kept_values, extra_full)


def layer_backward(out_grad, kept_values, weights, branch_two=None):
    (
        packed_weight,
        bias_pair,
        output_weight,
        output_bias,
        expand_weight,
        expand_bias,
        contract_weight,
        contract_bias,
        gain_first,
        shift_first,
        gain_second,
        shift_second,
    ) = weights
    (
        normed_one,
        normal_one,
        inv_one,
        queries,
        keys_in,
        values_in,
        logsum,
        mixed_rows,
        normed_two,
        normal_two,
        inv_two,
        hidden_pre,
        hidden,
    ) = kept_values
    seq_count, length, width_part = out_grad.shape
    rows_count = seq_count * length
    shape_heads = (seq_count, length, width_part // HEAD_DIM, HEAD_DIM)
    grad_rows = out_grad.reshape(rows_count, width_part)
    contract_bias_grad = jnp.sum(grad_rows, axis=0)
    if branch_two is None:
        branch_two = branch_grad(grad_rows)
    contract_weight_grad = jnp.einsum(
        "nf,nd->fd", hidden, branch_two, preferred_element_type=jnp.float32
    )
    hidden_grad = jnp.einsum(
        "nd,fd->nf", branch_two, contract_weight, preferred_element_type=jnp.float32
    )
    pre_grad = jax.vjp(gelu_tanh, hidden_pre)[1](hidden_grad)[0].astype(jnp.bfloat16)
    expand_bias_grad = jnp.sum(pre_grad.astype(jnp.float32), axis=0)
    expand_weight_grad = jnp.einsum(
        "nd,nf->df", normed_two, pre_grad, preferred_element_type=jnp.float32
    )
    second_grad, gain_second_grad, shift_second_grad = norm_backward(
        blocked_product("nf,tdf->tnd", pre_grad, expand_weight, 0),
        normal_two,
        inv_two,
        gain_second,
    )
    residual_grad = grad_rows + second_grad
    output_bias_grad = jnp.sum(residual_grad, axis=0)
    branch_one = branch_grad(residual_grad)
    packed_grad, packed_weight_grad, bias_pair_grad, output_weight_grad = attention_backward(
        branch_one,
        (queries, keys_in, values_in, logsum, mixed_rows, normed_one),
        output_weight,
        shape_heads,
        rows_count,
        width_part,
    )
    first_grad, gain_first_grad, shift_first_grad = norm_backward(
        blocked_product("ncf,tdcf->tnd", packed_grad, packed_weight, 0),
        normal_one,
        inv_one,
        gain_first,
    )
    input_grad = (residual_grad + first_grad).reshape(out_grad.shape)
    return (
        input_grad,
        (
            packed_weight_grad,
            bias_pair_grad,
            output_weight_grad,
            output_bias_grad,
            expand_weight_grad,
            expand_bias_grad,
            contract_weight_grad,
            contract_bias_grad,
            gain_first_grad,
            shift_first_grad,
            gain_second_grad,
            shift_second_grad,
        ),
    )


def as_blocks(array, dim, peers):
    before, after = (array.shape[:dim], array.shape[dim + 1 :])
    split = array.reshape(*before, peers, array.shape[dim] // peers, *after)
    return jnp.moveaxis(split, dim, 0).reshape(peers, -1)


def from_blocks(flat, shape, dim, peers):
    block_shape = (*shape[:dim], shape[dim] // peers, *shape[dim + 1 :])
    return flat.reshape(block_shape)


def split_by_size(arrays):
    big = [i for i, a in enumerate(arrays) if a[0].size % 128 == 0]
    small = [i for i, a in enumerate(arrays) if a[0].size % 128 != 0]
    return (big, small)


def in_rows(blocks, big, small):
    count = blocks[0].shape[0]
    rest = jnp.concatenate([blocks[i].reshape(count, -1) for i in small], axis=1)
    spare = -rest.shape[1] % 2048
    rest = jnp.concatenate([rest, jnp.zeros((count, spare), rest.dtype)], axis=1)
    rows = [blocks[i].reshape(count, -1, 128) for i in big] + [rest.reshape(count, -1, 128)]
    return jnp.concatenate(rows, axis=1)


def out_of_rows(rows, shapes, big, small):
    count = rows.shape[0]
    parts, at = ({}, 0)
    for i in big:
        height = math.prod(shapes[i]) // 128
        parts[i] = rows[:, at : at + height].reshape(count, *shapes[i])
        at += height
    rest = rows[:, at:].reshape(count, -1)
    at = 0
    for i in small:
        width = math.prod(shapes[i])
        parts[i] = rest[:, at : at + width].reshape(count, *shapes[i])
        at += width
    return [parts[i] for i in range(len(shapes))]


def sum_at_end(grads_zero, grads_last, dims):
    peers = lax.axis_size("dp")
    blocks = [
        jnp.concatenate(
            [as_blocks(g0.astype(jnp.bfloat16), d, peers), as_blocks(g1.astype(jnp.bfloat16), d, peers)]
        )
        for g0, g1, d in zip(grads_zero, grads_last, dims)
    ]
    big, small = split_by_size(blocks)
    rows = in_rows(blocks, big, small)
    total = lax.psum_scatter(
        rows.reshape(-1, 128), ("section", "dp"), scatter_dimension=0, tiled=True
    )
    shapes = [block.shape[1:] for block in blocks]
    parts = out_of_rows(total[None], shapes, big, small)
    return tuple(
        from_blocks(part[0].astype(jnp.float32), g.shape, d, peers)[None]
        for part, g, d in zip(parts, grads_zero, dims)
    )


def unpack_layer(gathered_rows, weights, dims, big, small):
    parts = out_of_rows(gathered_rows, [w.shape for w in weights], big, small)
    gathered = []
    for part, d in zip(parts, dims):
        part = jnp.moveaxis(part, 0, d)
        shape = part.shape
        gathered.append(part.reshape(*shape[:d], shape[d] * shape[d + 1], *shape[d + 2 :]))
    return tuple(gathered)


def gather_all(weights, dims, is_first):
    big, small = split_by_size([w[None] for w in weights])
    own = in_rows([w[None] for w in weights], big, small)[0]
    other = lax.ppermute(own, "section", [(0, 1), (1, 0)])
    first_rows = lax.all_gather(jnp.where(is_first, own, other), "dp", axis=0, tiled=False)
    last_rows = lax.all_gather(jnp.where(is_first, other, own), "dp", axis=0, tiled=False)
    return (
        unpack_layer(first_rows, weights, dims, big, small),
        unpack_layer(last_rows, weights, dims, big, small),
    )


def shards(
    inputs,
    cotangent,
    packed_weight,
    bias_pair,
    output_weight,
    output_bias,
    expand_weight,
    expand_bias,
    contract_weight,
    contract_bias,
    gain_first,
    shift_first,
    gain_second,
    shift_second,
):
    dims = (0, 1, 1, 0, 0, 0, 1, 0, 0, 0, 0, 0)
    section_index = lax.axis_index("section")
    is_first = section_index == 0
    weights_zero, weights_last = gather_all(
        (
            packed_weight[0],
            bias_pair[0],
            output_weight[0],
            output_bias[0],
            expand_weight[0],
            expand_bias[0],
            contract_weight[0],
            contract_bias[0],
            gain_first[0],
            shift_first[0],
            gain_second[0],
            shift_second[0],
        ),
        dims,
        is_first,
    )
    stream = lax.dynamic_index_in_dim(inputs, section_index, axis=0, keepdims=False)
    out_grad = lax.dynamic_index_in_dim(cotangent, section_index, axis=0, keepdims=False)
    grad_rows = out_grad.reshape(-1, out_grad.shape[-1]).astype(jnp.bfloat16)
    middle, kept_zero, grad_full = layer_forward(stream, weights_zero, grad_rows)
    final, kept_last, _ = layer_forward(middle, weights_last)
    other_middle = lax.ppermute(middle, "section", [(1, 0)])
    other_final = lax.ppermute(final, "section", [(0, 1)])
    middle_grad, grads_last = layer_backward(out_grad, kept_last, weights_last, grad_full)
    other_middle_grad = lax.ppermute(middle_grad, "section", [(0, 1)])
    input_grad, grads_zero = layer_backward(middle_grad, kept_zero, weights_zero)
    other_input_grad = lax.ppermute(input_grad, "section", [(1, 0)])
    reduced = sum_at_end(grads_zero, grads_last, dims)
    section_outputs = jnp.where(
        is_first, jnp.stack([middle, other_middle]), jnp.stack([other_final, final])
    )[None]
    section_grads = jnp.where(
        is_first,
        jnp.stack([input_grad, other_input_grad]),
        jnp.stack([other_middle_grad, middle_grad]),
    )[None]
    return (section_outputs, section_grads) + tuple(reduced)


def solution(mesh):
    in_specs = (
        P(None, "dp", None, "tensor"),
        P(None, "dp", None, "tensor"),
        P("section", "dp", None, "tensor"),
        P("section", None, ("tensor", "dp")),
        P("section", "tensor", "dp"),
        P("section", ("tensor", "dp")),
        P("section", "dp", "tensor"),
        P("section", ("tensor", "dp")),
        P("section", "tensor", "dp"),
        P("section", ("tensor", "dp")),
        P("section", ("tensor", "dp")),
        P("section", ("tensor", "dp")),
        P("section", ("tensor", "dp")),
        P("section", ("tensor", "dp")),
    )
    out_specs = (
        P("section", None, "dp", None, "tensor"),
        P("section", None, "dp", None, "tensor"),
        P("section", "dp", None, "tensor"),
        P("section", None, ("tensor", "dp")),
        P("section", "tensor", "dp"),
        P("section", ("tensor", "dp")),
        P("section", "dp", "tensor"),
        P("section", ("tensor", "dp")),
        P("section", "tensor", "dp"),
        P("section", ("tensor", "dp")),
        P("section", ("tensor", "dp")),
        P("section", ("tensor", "dp")),
        P("section", ("tensor", "dp")),
        P("section", ("tensor", "dp")),
    )
    return jax.shard_map(shards, mesh=mesh, in_specs=in_specs, out_specs=out_specs, check_vma=False)
```

```python
import math

import jax
import jax.numpy as jnp
from jax import lax
from jax.sharding import PartitionSpec as P

HEAD_DIM = 64


epsilon = 1e-05
gelu_coef = math.sqrt(2.0 / math.pi)
masked_value = -1e30


def sent_to_all(array, axis):
    copies = jnp.broadcast_to(array, (lax.axis_size(axis), *array.shape))
    return lax.all_to_all(copies, axis, split_axis=0, concat_axis=0, tiled=True)


def taken_together(array, axis):
    return sent_to_all(array, axis).sum(axis=0)


def in_one(arrays, axis):
    ends = [0]
    for a in arrays:
        ends.append(ends[-1] + a.size)
    subtotal = taken_together(jnp.concatenate([a.ravel() for a in arrays]), axis)
    return tuple((subtotal[b:e].reshape(a.shape) for a, b, e in zip(arrays, ends, ends[1:])))


def joined_along(parts, dim):
    parts = jnp.moveaxis(parts, 0, dim)
    shape = parts.shape
    return parts.reshape(*shape[:dim], shape[dim] * shape[dim + 1], *shape[dim + 2 :])


def collect(array, axis, dim):
    parts = sent_to_all(array, axis)
    return joined_along(parts, dim)


def in_blocks(array, dim, peers):
    before, after = (array.shape[:dim], array.shape[dim + 1 :])
    return jnp.moveaxis(array.reshape(*before, peers, -1, *after), dim, 0)


def summed_on_arrival(array, axis, dim):
    parts = in_blocks(array, dim, lax.axis_size(axis))
    arrived = lax.all_to_all(parts, axis, split_axis=0, concat_axis=0, tiled=True)
    return arrived.astype(jnp.float32).sum(axis=0)


def side_by_side(arrays, axis, dim, along):
    both = jnp.concatenate(arrays, axis=along)
    result, at, gathered = (lax.psum_scatter(both, axis, scatter_dimension=dim, tiled=True), 0, [])
    for a in arrays:
        gathered.append(lax.slice_in_dim(result, at, at + a.shape[along], axis=along))
        at += a.shape[along]
    return tuple(gathered)


def in_one_piece(arrays, axis, dim, along):
    both = jnp.concatenate(arrays, axis=along)
    result, at, gathered = (lax.all_gather(both, axis, axis=dim, tiled=True), 0, [])
    for a in arrays:
        gathered.append(lax.slice_in_dim(result, at, at + a.shape[along], axis=along))
        at += a.shape[along]
    return tuple(gathered)


def from_behind(array, axis, by):
    peers = lax.axis_size(axis)
    pairs = [(i, i + by) for i in range(peers) if 0 <= i + by < peers]
    return lax.ppermute(array, axis, pairs)


def gelu_tanh(values):
    return (
        0.5 * values * (1.0 + jnp.tanh(gelu_coef * (values + 0.044715 * values * values * values)))
    )


def norm_forward(stream, gain, offset, extra=None):
    width_all = stream.shape[1] * lax.axis_size("tensor")
    totals, squares = in_one((jnp.sum(stream, axis=1), jnp.sum(stream * stream, axis=1)), "tensor")
    mean_row = (totals / width_all)[:, None]
    var_row = (squares / width_all)[:, None] - mean_row * mean_row
    inv_scale = lax.rsqrt(var_row + epsilon)
    normal_part = (stream - mean_row) * inv_scale
    normed = (normal_part * gain + offset).astype(jnp.bfloat16)
    if extra is None:
        return (collect(normed, "tensor", 1), normal_part, inv_scale, None)
    both = collect(jnp.stack([normed, extra]), "tensor", 2)
    return (both[0], normal_part, inv_scale, both[1])


def norm_backward(partial_term, normal_part, inv_scale, gain):
    width_all = partial_term.shape[1]
    d_normed = summed_on_arrival(partial_term.astype(jnp.bfloat16), "tensor", 1)
    gain_grad = jnp.sum(d_normed * normal_part, axis=0)
    offset_grad = jnp.sum(d_normed, axis=0)
    scaled = d_normed * gain
    first_sum, second_sum = in_one(
        (jnp.sum(scaled, axis=1), jnp.sum(scaled * normal_part, axis=1)), "tensor"
    )
    stream_grad = inv_scale * (
        scaled - first_sum[:, None] / width_all - normal_part * second_sum[:, None] / width_all
    )
    return (stream_grad, gain_grad, offset_grad)


def branch_sum(partial_term):
    return summed_on_arrival(partial_term.astype(jnp.bfloat16), "tensor", 1)


def branch_grad(stream_grad):
    return collect(stream_grad.astype(jnp.bfloat16), "tensor", 1)


def causal_scores(queries, keys_in):
    length = queries.shape[0]
    scale_factor = queries.shape[2] ** (-0.5)
    scores = (
        jnp.einsum("qhe,khe->hqk", queries, keys_in, preferred_element_type=jnp.float32)
        * scale_factor
    )
    causal = lax.broadcasted_iota(jnp.int32, (length, length), 0) >= lax.broadcasted_iota(
        jnp.int32, (length, length), 1
    )
    return (jnp.where(causal[None], scores, masked_value), scale_factor)


def attend(operands):
    queries, keys_in, values_in = operands
    masked, scale_factor = causal_scores(queries, keys_in)
    highest = jnp.max(masked, axis=2, keepdims=True)
    logsum = highest + jnp.log(jnp.sum(jnp.exp(masked - highest), axis=2, keepdims=True))
    weights_low = jnp.exp(masked - logsum).astype(jnp.bfloat16)
    mixture = jnp.einsum("hqk,khe->qhe", weights_low, values_in, preferred_element_type=jnp.float32)
    return (mixture.astype(jnp.bfloat16), logsum[:, :, 0])


def attend_back(operands):
    queries, keys_in, values_in, logsum, mixed_grad = operands
    masked, scale_factor = causal_scores(queries, keys_in)
    probs_full = jnp.exp(masked - logsum[:, :, None])
    probs_grad = jnp.einsum(
        "qhe,khe->hqk", mixed_grad, values_in, preferred_element_type=jnp.float32
    )
    row_dot = jnp.sum(probs_full * probs_grad, axis=2, keepdims=True)
    score_grad = (probs_full * (probs_grad - row_dot)).astype(jnp.bfloat16)
    query_grad = (
        jnp.einsum("hqk,khe->qhe", score_grad, keys_in, preferred_element_type=jnp.float32)
        * scale_factor
    )
    key_grad = (
        jnp.einsum("hqk,qhe->khe", score_grad, queries, preferred_element_type=jnp.float32)
        * scale_factor
    )
    value_grad = jnp.einsum(
        "hqk,qhe->khe",
        probs_full.astype(jnp.bfloat16),
        mixed_grad,
        preferred_element_type=jnp.float32,
    )
    return (
        query_grad.astype(jnp.bfloat16),
        key_grad.astype(jnp.bfloat16),
        value_grad.astype(jnp.bfloat16),
    )


def attention_forward(normed_one, packed_weight, bias_pair, shape_heads, rows_count, width_part):
    packed = jnp.einsum(
        "nd,dcf->ncf", normed_one, packed_weight, preferred_element_type=jnp.float32
    )
    queries = (packed[:, 0] + bias_pair[0]).astype(jnp.bfloat16)
    keys_in = packed[:, 1].astype(jnp.bfloat16)
    values_in = (packed[:, 2] + bias_pair[1]).astype(jnp.bfloat16)
    mixture, logsum = lax.map(
        attend,
        (
            queries.reshape(shape_heads),
            keys_in.reshape(shape_heads),
            values_in.reshape(shape_heads),
        ),
    )
    return (queries, keys_in, values_in, logsum, mixture.reshape(rows_count, width_part))


def attention_backward(branch_one, kept_part, output_weight, shape_heads, rows_count, width_part):
    queries, keys_in, values_in, logsum, mixed_rows, normed_one = kept_part
    output_weight_grad = jnp.einsum(
        "nf,nd->fd", mixed_rows, branch_one, preferred_element_type=jnp.float32
    )
    mixed_grad = jnp.einsum(
        "nd,fd->nf", branch_one, output_weight, preferred_element_type=jnp.float32
    ).astype(jnp.bfloat16)
    query_grad, key_grad, value_grad = lax.map(
        attend_back,
        (
            queries.reshape(shape_heads),
            keys_in.reshape(shape_heads),
            values_in.reshape(shape_heads),
            logsum,
            mixed_grad.reshape(shape_heads),
        ),
    )
    query_rows = query_grad.reshape(rows_count, width_part)
    key_rows = key_grad.reshape(rows_count, width_part)
    value_rows = value_grad.reshape(rows_count, width_part)
    packed_grad = jnp.stack([query_rows, key_rows, value_rows], axis=1)
    bias_pair_grad = jnp.stack(
        [
            jnp.sum(query_rows.astype(jnp.float32), axis=0),
            jnp.sum(value_rows.astype(jnp.float32), axis=0),
        ]
    )
    packed_weight_grad = jnp.einsum(
        "nd,ncf->dcf", normed_one, packed_grad, preferred_element_type=jnp.float32
    )
    return (packed_grad, packed_weight_grad, bias_pair_grad, output_weight_grad)


def layer_forward(stream, weights, extra=None):
    (
        packed_weight,
        bias_pair,
        output_weight,
        output_bias,
        expand_weight,
        expand_bias,
        contract_weight,
        contract_bias,
        gain_first,
        shift_first,
        gain_second,
        shift_second,
    ) = weights
    seq_count, length, width_part = stream.shape
    rows_count = seq_count * length
    shape_heads = (seq_count, length, width_part // HEAD_DIM, HEAD_DIM)
    stream_rows = stream.reshape(rows_count, width_part)
    normed_one, normal_one, inv_one, extra_full = norm_forward(
        stream_rows, gain_first, shift_first, extra
    )
    queries, keys_in, values_in, logsum, mixed_rows = attention_forward(
        normed_one, packed_weight, bias_pair, shape_heads, rows_count, width_part
    )
    residual = (
        stream_rows
        + branch_sum(jnp.dot(mixed_rows, output_weight, preferred_element_type=jnp.float32))
        + output_bias
    )
    normed_two, normal_two, inv_two, _ = norm_forward(residual, gain_second, shift_second)
    hidden_pre = (
        jnp.dot(normed_two, expand_weight, preferred_element_type=jnp.float32) + expand_bias
    )
    hidden = gelu_tanh(hidden_pre).astype(jnp.bfloat16)
    result = (
        residual
        + branch_sum(jnp.dot(hidden, contract_weight, preferred_element_type=jnp.float32))
        + contract_bias
    )
    kept_values = (
        normed_one,
        normal_one,
        inv_one,
        queries,
        keys_in,
        values_in,
        logsum,
        mixed_rows,
        normed_two,
        normal_two,
        inv_two,
        hidden_pre,
        hidden,
    )
    return (result.reshape(stream.shape), kept_values, extra_full)


def layer_backward(out_grad, kept_values, weights, branch_two=None):
    (
        packed_weight,
        bias_pair,
        output_weight,
        output_bias,
        expand_weight,
        expand_bias,
        contract_weight,
        contract_bias,
        gain_first,
        shift_first,
        gain_second,
        shift_second,
    ) = weights
    (
        normed_one,
        normal_one,
        inv_one,
        queries,
        keys_in,
        values_in,
        logsum,
        mixed_rows,
        normed_two,
        normal_two,
        inv_two,
        hidden_pre,
        hidden,
    ) = kept_values
    seq_count, length, width_part = out_grad.shape
    rows_count = seq_count * length
    shape_heads = (seq_count, length, width_part // HEAD_DIM, HEAD_DIM)
    grad_rows = out_grad.reshape(rows_count, width_part)
    contract_bias_grad = jnp.sum(grad_rows, axis=0)
    if branch_two is None:
        branch_two = branch_grad(grad_rows)
    contract_weight_grad = jnp.einsum(
        "nf,nd->fd", hidden, branch_two, preferred_element_type=jnp.float32
    )
    hidden_grad = jnp.einsum(
        "nd,fd->nf", branch_two, contract_weight, preferred_element_type=jnp.float32
    )
    pre_grad = jax.vjp(gelu_tanh, hidden_pre)[1](hidden_grad)[0].astype(jnp.bfloat16)
    expand_bias_grad = jnp.sum(pre_grad.astype(jnp.float32), axis=0)
    expand_weight_grad = jnp.einsum(
        "nd,nf->df", normed_two, pre_grad, preferred_element_type=jnp.float32
    )
    second_grad, gain_second_grad, shift_second_grad = norm_backward(
        jnp.einsum("nf,df->nd", pre_grad, expand_weight, preferred_element_type=jnp.float32),
        normal_two,
        inv_two,
        gain_second,
    )
    residual_grad = grad_rows + second_grad
    output_bias_grad = jnp.sum(residual_grad, axis=0)
    branch_one = branch_grad(residual_grad)
    packed_grad, packed_weight_grad, bias_pair_grad, output_weight_grad = attention_backward(
        branch_one,
        (queries, keys_in, values_in, logsum, mixed_rows, normed_one),
        output_weight,
        shape_heads,
        rows_count,
        width_part,
    )
    first_grad, gain_first_grad, shift_first_grad = norm_backward(
        jnp.einsum("ncf,dcf->nd", packed_grad, packed_weight, preferred_element_type=jnp.float32),
        normal_one,
        inv_one,
        gain_first,
    )
    input_grad = (residual_grad + first_grad).reshape(out_grad.shape)
    return (
        input_grad,
        (
            packed_weight_grad,
            bias_pair_grad,
            output_weight_grad,
            output_bias_grad,
            expand_weight_grad,
            expand_bias_grad,
            contract_weight_grad,
            contract_bias_grad,
            gain_first_grad,
            shift_first_grad,
            gain_second_grad,
            shift_second_grad,
        ),
    )


def as_blocks(array, dim, peers):
    before, after = (array.shape[:dim], array.shape[dim + 1 :])
    split = array.reshape(*before, peers, array.shape[dim] // peers, *after)
    return jnp.moveaxis(split, dim, 0).reshape(peers, -1)


def from_blocks(flat, shape, dim, peers):
    block_shape = (*shape[:dim], shape[dim] // peers, *shape[dim + 1 :])
    return flat.reshape(block_shape)


def split_by_size(arrays):
    big = [i for i, a in enumerate(arrays) if a[0].size % 128 == 0]
    small = [i for i, a in enumerate(arrays) if a[0].size % 128 != 0]
    return (big, small)


def in_rows(blocks, big, small):
    count = blocks[0].shape[0]
    rest = jnp.concatenate([blocks[i].reshape(count, -1) for i in small], axis=1)
    spare = -rest.shape[1] % 2048
    rest = jnp.concatenate([rest, jnp.zeros((count, spare), rest.dtype)], axis=1)
    rows = [blocks[i].reshape(count, -1, 128) for i in big] + [rest.reshape(count, -1, 128)]
    return jnp.concatenate(rows, axis=1)


def out_of_rows(rows, shapes, big, small):
    count = rows.shape[0]
    parts, at = ({}, 0)
    for i in big:
        height = math.prod(shapes[i]) // 128
        parts[i] = rows[:, at : at + height].reshape(count, *shapes[i])
        at += height
    rest = rows[:, at:].reshape(count, -1)
    at = 0
    for i in small:
        width = math.prod(shapes[i])
        parts[i] = rest[:, at : at + width].reshape(count, *shapes[i])
        at += width
    return [parts[i] for i in range(len(shapes))]


def sum_at_end(grads_zero, grads_last, dims):
    peers = lax.axis_size("dp")
    blocks = [
        jnp.concatenate(
            [as_blocks(g0.astype(jnp.bfloat16), d, peers), as_blocks(g1.astype(jnp.bfloat16), d, peers)]
        )
        for g0, g1, d in zip(grads_zero, grads_last, dims)
    ]
    big, small = split_by_size(blocks)
    rows = in_rows(blocks, big, small)
    total = lax.psum_scatter(
        rows.reshape(-1, 128), ("section", "dp"), scatter_dimension=0, tiled=True
    )
    shapes = [block.shape[1:] for block in blocks]
    parts = out_of_rows(total[None], shapes, big, small)
    return tuple(
        from_blocks(part[0].astype(jnp.float32), g.shape, d, peers)[None]
        for part, g, d in zip(parts, grads_zero, dims)
    )


def unpack_layer(gathered_rows, weights, dims, big, small):
    parts = out_of_rows(gathered_rows, [w.shape for w in weights], big, small)
    gathered = []
    for part, d in zip(parts, dims):
        part = jnp.moveaxis(part, 0, d)
        shape = part.shape
        gathered.append(part.reshape(*shape[:d], shape[d] * shape[d + 1], *shape[d + 2 :]))
    return tuple(gathered)


def gather_all(weights, dims, is_first):
    big, small = split_by_size([w[None] for w in weights])
    own = in_rows([w[None] for w in weights], big, small)[0]
    other = lax.ppermute(own, "section", [(0, 1), (1, 0)])
    first_rows = lax.all_gather(jnp.where(is_first, own, other), "dp", axis=0, tiled=False)
    last_rows = lax.all_gather(jnp.where(is_first, other, own), "dp", axis=0, tiled=False)
    return (
        unpack_layer(first_rows, weights, dims, big, small),
        unpack_layer(last_rows, weights, dims, big, small),
    )


def shards(
    inputs,
    cotangent,
    packed_weight,
    bias_pair,
    output_weight,
    output_bias,
    expand_weight,
    expand_bias,
    contract_weight,
    contract_bias,
    gain_first,
    shift_first,
    gain_second,
    shift_second,
):
    dims = (0, 1, 1, 0, 0, 0, 1, 0, 0, 0, 0, 0)
    section_index = lax.axis_index("section")
    is_first = section_index == 0
    weights_zero, weights_last = gather_all(
        (
            packed_weight[0],
            bias_pair[0],
            output_weight[0],
            output_bias[0],
            expand_weight[0],
            expand_bias[0],
            contract_weight[0],
            contract_bias[0],
            gain_first[0],
            shift_first[0],
            gain_second[0],
            shift_second[0],
        ),
        dims,
        is_first,
    )
    stream = lax.dynamic_index_in_dim(inputs, section_index, axis=0, keepdims=False)
    out_grad = lax.dynamic_index_in_dim(cotangent, section_index, axis=0, keepdims=False)
    grad_rows = out_grad.reshape(-1, out_grad.shape[-1]).astype(jnp.bfloat16)
    middle, kept_zero, grad_full = layer_forward(stream, weights_zero, grad_rows)
    final, kept_last, _ = layer_forward(middle, weights_last)
    other_middle = lax.ppermute(middle, "section", [(1, 0)])
    other_final = lax.ppermute(final, "section", [(0, 1)])
    middle_grad, grads_last = layer_backward(out_grad, kept_last, weights_last, grad_full)
    other_middle_grad = lax.ppermute(middle_grad, "section", [(0, 1)])
    middle_grad, other_middle, other_final = lax.optimization_barrier(
        (middle_grad, other_middle, other_final)
    )
    input_grad, grads_zero = layer_backward(middle_grad, kept_zero, weights_zero)
    other_input_grad = lax.ppermute(input_grad, "section", [(1, 0)])
    reduced = sum_at_end(grads_zero, grads_last, dims)
    section_outputs = jnp.where(
        is_first, jnp.stack([middle, other_middle]), jnp.stack([other_final, final])
    )[None]
    section_grads = jnp.where(
        is_first,
        jnp.stack([input_grad, other_input_grad]),
        jnp.stack([other_middle_grad, middle_grad]),
    )[None]
    return (section_outputs, section_grads) + tuple(reduced)


def solution(mesh):
    in_specs = (
        P(None, "dp", None, "tensor"),
        P(None, "dp", None, "tensor"),
        P("section", "dp", None, "tensor"),
        P("section", None, ("tensor", "dp")),
        P("section", "tensor", "dp"),
        P("section", ("tensor", "dp")),
        P("section", "dp", "tensor"),
        P("section", ("tensor", "dp")),
        P("section", "tensor", "dp"),
        P("section", ("tensor", "dp")),
        P("section", ("tensor", "dp")),
        P("section", ("tensor", "dp")),
        P("section", ("tensor", "dp")),
        P("section", ("tensor", "dp")),
    )
    out_specs = (
        P("section", None, "dp", None, "tensor"),
        P("section", None, "dp", None, "tensor"),
        P("section", "dp", None, "tensor"),
        P("section", None, ("tensor", "dp")),
        P("section", "tensor", "dp"),
        P("section", ("tensor", "dp")),
        P("section", "dp", "tensor"),
        P("section", ("tensor", "dp")),
        P("section", "tensor", "dp"),
        P("section", ("tensor", "dp")),
        P("section", ("tensor", "dp")),
        P("section", ("tensor", "dp")),
        P("section", ("tensor", "dp")),
        P("section", ("tensor", "dp")),
    )
    return jax.shard_map(shards, mesh=mesh, in_specs=in_specs, out_specs=out_specs, check_vma=False)
```

```python
import math

import jax
import jax.numpy as jnp
from jax import lax
from jax.sharding import PartitionSpec as P

HEAD_DIM = 64


epsilon = 1e-05
gelu_coef = math.sqrt(2.0 / math.pi)
masked_value = -1e30


def sent_to_all(array, axis):
    copies = jnp.broadcast_to(array, (lax.axis_size(axis), *array.shape))
    return lax.all_to_all(copies, axis, split_axis=0, concat_axis=0, tiled=True)


def taken_together(array, axis):
    return sent_to_all(array, axis).sum(axis=0)


def in_one(arrays, axis):
    ends = [0]
    for a in arrays:
        ends.append(ends[-1] + a.size)
    subtotal = taken_together(jnp.concatenate([a.ravel() for a in arrays]), axis)
    return tuple((subtotal[b:e].reshape(a.shape) for a, b, e in zip(arrays, ends, ends[1:])))


def joined_along(parts, dim):
    parts = jnp.moveaxis(parts, 0, dim)
    shape = parts.shape
    return parts.reshape(*shape[:dim], shape[dim] * shape[dim + 1], *shape[dim + 2 :])


def collect(array, axis, dim):
    parts = sent_to_all(array, axis)
    return joined_along(parts, dim)


def in_blocks(array, dim, peers):
    before, after = (array.shape[:dim], array.shape[dim + 1 :])
    return jnp.moveaxis(array.reshape(*before, peers, -1, *after), dim, 0)


def summed_on_arrival(array, axis, dim):
    parts = in_blocks(array, dim, lax.axis_size(axis))
    arrived = lax.all_to_all(parts, axis, split_axis=0, concat_axis=0, tiled=True)
    return arrived.astype(jnp.float32).sum(axis=0)


def side_by_side(arrays, axis, dim, along):
    both = jnp.concatenate(arrays, axis=along)
    result, at, gathered = (lax.psum_scatter(both, axis, scatter_dimension=dim, tiled=True), 0, [])
    for a in arrays:
        gathered.append(lax.slice_in_dim(result, at, at + a.shape[along], axis=along))
        at += a.shape[along]
    return tuple(gathered)


def in_one_piece(arrays, axis, dim, along):
    both = jnp.concatenate(arrays, axis=along)
    result, at, gathered = (lax.all_gather(both, axis, axis=dim, tiled=True), 0, [])
    for a in arrays:
        gathered.append(lax.slice_in_dim(result, at, at + a.shape[along], axis=along))
        at += a.shape[along]
    return tuple(gathered)


def from_behind(array, axis, by):
    peers = lax.axis_size(axis)
    pairs = [(i, i + by) for i in range(peers) if 0 <= i + by < peers]
    return lax.ppermute(array, axis, pairs)


def gelu_tanh(values):
    return (
        0.5 * values * (1.0 + jnp.tanh(gelu_coef * (values + 0.044715 * values * values * values)))
    )


def norm_forward(stream, gain, offset, extra=None):
    width_all = stream.shape[1] * lax.axis_size("tensor")
    totals, squares = in_one((jnp.sum(stream, axis=1), jnp.sum(stream * stream, axis=1)), "tensor")
    mean_row = (totals / width_all)[:, None]
    var_row = (squares / width_all)[:, None] - mean_row * mean_row
    inv_scale = lax.rsqrt(var_row + epsilon)
    normal_part = (stream - mean_row) * inv_scale
    normed = (normal_part * gain + offset).astype(jnp.bfloat16)
    if extra is None:
        return (collect(normed, "tensor", 1), normal_part, inv_scale, None)
    both = collect(jnp.stack([normed, extra]), "tensor", 2)
    return (both[0], normal_part, inv_scale, both[1])


def norm_backward(partial_term, normal_part, inv_scale, gain):
    width_all = partial_term.shape[1]
    d_normed = summed_on_arrival(partial_term.astype(jnp.bfloat16), "tensor", 1)
    gain_grad = jnp.sum(d_normed * normal_part, axis=0)
    offset_grad = jnp.sum(d_normed, axis=0)
    scaled = d_normed * gain
    first_sum, second_sum = in_one(
        (jnp.sum(scaled, axis=1), jnp.sum(scaled * normal_part, axis=1)), "tensor"
    )
    stream_grad = inv_scale * (
        scaled - first_sum[:, None] / width_all - normal_part * second_sum[:, None] / width_all
    )
    return (stream_grad, gain_grad, offset_grad)


def branch_sum(partial_term):
    return summed_on_arrival(partial_term.astype(jnp.bfloat16), "tensor", 1)


def branch_grad(stream_grad):
    return collect(stream_grad.astype(jnp.bfloat16), "tensor", 1)


def causal_scores(queries, keys_in):
    length = queries.shape[0]
    scale_factor = queries.shape[2] ** (-0.5)
    scores = (
        jnp.einsum("qhe,khe->hqk", queries, keys_in, preferred_element_type=jnp.float32)
        * scale_factor
    )
    causal = lax.broadcasted_iota(jnp.int32, (length, length), 0) >= lax.broadcasted_iota(
        jnp.int32, (length, length), 1
    )
    return (jnp.where(causal[None], scores, masked_value), scale_factor)


def attend(operands):
    queries, keys_in, values_in = operands
    masked, scale_factor = causal_scores(queries, keys_in)
    highest = jnp.max(masked, axis=2, keepdims=True)
    logsum = highest + jnp.log(jnp.sum(jnp.exp(masked - highest), axis=2, keepdims=True))
    weights_low = jnp.exp(masked - logsum).astype(jnp.bfloat16)
    mixture = jnp.einsum("hqk,khe->qhe", weights_low, values_in, preferred_element_type=jnp.float32)
    return (mixture.astype(jnp.bfloat16), logsum[:, :, 0])


def attend_back(operands):
    queries, keys_in, values_in, logsum, mixed_grad = operands
    masked, scale_factor = causal_scores(queries, keys_in)
    probs_full = jnp.exp(masked - logsum[:, :, None])
    probs_grad = jnp.einsum(
        "qhe,khe->hqk", mixed_grad, values_in, preferred_element_type=jnp.float32
    )
    row_dot = jnp.sum(probs_full * probs_grad, axis=2, keepdims=True)
    score_grad = (probs_full * (probs_grad - row_dot)).astype(jnp.bfloat16)
    query_grad = (
        jnp.einsum("hqk,khe->qhe", score_grad, keys_in, preferred_element_type=jnp.float32)
        * scale_factor
    )
    key_grad = (
        jnp.einsum("hqk,qhe->khe", score_grad, queries, preferred_element_type=jnp.float32)
        * scale_factor
    )
    value_grad = jnp.einsum(
        "hqk,qhe->khe",
        probs_full.astype(jnp.bfloat16),
        mixed_grad,
        preferred_element_type=jnp.float32,
    )
    return (
        query_grad.astype(jnp.bfloat16),
        key_grad.astype(jnp.bfloat16),
        value_grad.astype(jnp.bfloat16),
    )


def attention_forward(normed_one, packed_weight, bias_pair, shape_heads, rows_count, width_part):
    packed = jnp.einsum(
        "nd,dcf->ncf", normed_one, packed_weight, preferred_element_type=jnp.float32
    )
    queries = (packed[:, 0] + bias_pair[0]).astype(jnp.bfloat16)
    keys_in = packed[:, 1].astype(jnp.bfloat16)
    values_in = (packed[:, 2] + bias_pair[1]).astype(jnp.bfloat16)
    mixture, logsum = lax.map(
        attend,
        (
            queries.reshape(shape_heads),
            keys_in.reshape(shape_heads),
            values_in.reshape(shape_heads),
        ),
    )
    return (queries, keys_in, values_in, logsum, mixture.reshape(rows_count, width_part))


def attention_backward(branch_one, kept_part, output_weight, shape_heads, rows_count, width_part):
    queries, keys_in, values_in, logsum, mixed_rows, normed_one = kept_part
    output_weight_grad = jnp.einsum(
        "nf,nd->fd", mixed_rows, branch_one, preferred_element_type=jnp.float32
    )
    mixed_grad = jnp.einsum(
        "nd,fd->nf", branch_one, output_weight, preferred_element_type=jnp.float32
    ).astype(jnp.bfloat16)
    query_grad, key_grad, value_grad = lax.map(
        attend_back,
        (
            queries.reshape(shape_heads),
            keys_in.reshape(shape_heads),
            values_in.reshape(shape_heads),
            logsum,
            mixed_grad.reshape(shape_heads),
        ),
    )
    query_rows = query_grad.reshape(rows_count, width_part)
    key_rows = key_grad.reshape(rows_count, width_part)
    value_rows = value_grad.reshape(rows_count, width_part)
    packed_grad = jnp.stack([query_rows, key_rows, value_rows], axis=1)
    bias_pair_grad = jnp.stack(
        [
            jnp.sum(query_rows.astype(jnp.float32), axis=0),
            jnp.sum(value_rows.astype(jnp.float32), axis=0),
        ]
    )
    packed_weight_grad = jnp.einsum(
        "nd,ncf->dcf", normed_one, packed_grad, preferred_element_type=jnp.float32
    )
    return (packed_grad, packed_weight_grad, bias_pair_grad, output_weight_grad)


def layer_forward(stream, weights, extra=None):
    (
        packed_weight,
        bias_pair,
        output_weight,
        output_bias,
        expand_weight,
        expand_bias,
        contract_weight,
        contract_bias,
        gain_first,
        shift_first,
        gain_second,
        shift_second,
    ) = weights
    seq_count, length, width_part = stream.shape
    rows_count = seq_count * length
    shape_heads = (seq_count, length, width_part // HEAD_DIM, HEAD_DIM)
    stream_rows = stream.reshape(rows_count, width_part)
    normed_one, normal_one, inv_one, extra_full = norm_forward(
        stream_rows, gain_first, shift_first, extra
    )
    queries, keys_in, values_in, logsum, mixed_rows = attention_forward(
        normed_one, packed_weight, bias_pair, shape_heads, rows_count, width_part
    )
    residual = (
        stream_rows
        + branch_sum(jnp.dot(mixed_rows, output_weight, preferred_element_type=jnp.float32))
        + output_bias
    )
    normed_two, normal_two, inv_two, _ = norm_forward(residual, gain_second, shift_second)
    hidden_pre = (
        jnp.dot(normed_two, expand_weight, preferred_element_type=jnp.float32) + expand_bias
    )
    hidden = gelu_tanh(hidden_pre).astype(jnp.bfloat16)
    result = (
        residual
        + branch_sum(jnp.dot(hidden, contract_weight, preferred_element_type=jnp.float32))
        + contract_bias
    )
    kept_values = (
        normed_one,
        normal_one,
        inv_one,
        queries,
        keys_in,
        values_in,
        logsum,
        mixed_rows,
        normed_two,
        normal_two,
        inv_two,
        hidden_pre,
        hidden,
    )
    return (result.reshape(stream.shape), kept_values, extra_full)


def layer_backward(out_grad, kept_values, weights, branch_two=None):
    (
        packed_weight,
        bias_pair,
        output_weight,
        output_bias,
        expand_weight,
        expand_bias,
        contract_weight,
        contract_bias,
        gain_first,
        shift_first,
        gain_second,
        shift_second,
    ) = weights
    (
        normed_one,
        normal_one,
        inv_one,
        queries,
        keys_in,
        values_in,
        logsum,
        mixed_rows,
        normed_two,
        normal_two,
        inv_two,
        hidden_pre,
        hidden,
    ) = kept_values
    seq_count, length, width_part = out_grad.shape
    rows_count = seq_count * length
    shape_heads = (seq_count, length, width_part // HEAD_DIM, HEAD_DIM)
    grad_rows = out_grad.reshape(rows_count, width_part)
    contract_bias_grad = jnp.sum(grad_rows, axis=0)
    if branch_two is None:
        branch_two = branch_grad(grad_rows)
    contract_weight_grad = jnp.einsum(
        "nf,nd->fd", hidden, branch_two, preferred_element_type=jnp.float32
    )
    hidden_grad = jnp.einsum(
        "nd,fd->nf", branch_two, contract_weight, preferred_element_type=jnp.float32
    )
    pre_grad = jax.vjp(gelu_tanh, hidden_pre)[1](hidden_grad)[0].astype(jnp.bfloat16)
    expand_bias_grad = jnp.sum(pre_grad.astype(jnp.float32), axis=0)
    expand_weight_grad = jnp.einsum(
        "nd,nf->df", normed_two, pre_grad, preferred_element_type=jnp.float32
    )
    second_grad, gain_second_grad, shift_second_grad = norm_backward(
        jnp.einsum("nf,df->nd", pre_grad, expand_weight, preferred_element_type=jnp.float32),
        normal_two,
        inv_two,
        gain_second,
    )
    residual_grad = grad_rows + second_grad
    output_bias_grad = jnp.sum(residual_grad, axis=0)
    branch_one = branch_grad(residual_grad)
    packed_grad, packed_weight_grad, bias_pair_grad, output_weight_grad = attention_backward(
        branch_one,
        (queries, keys_in, values_in, logsum, mixed_rows, normed_one),
        output_weight,
        shape_heads,
        rows_count,
        width_part,
    )
    first_grad, gain_first_grad, shift_first_grad = norm_backward(
        jnp.einsum("ncf,dcf->nd", packed_grad, packed_weight, preferred_element_type=jnp.float32),
        normal_one,
        inv_one,
        gain_first,
    )
    input_grad = (residual_grad + first_grad).reshape(out_grad.shape)
    return (
        input_grad,
        (
            packed_weight_grad,
            bias_pair_grad,
            output_weight_grad,
            output_bias_grad,
            expand_weight_grad,
            expand_bias_grad,
            contract_weight_grad,
            contract_bias_grad,
            gain_first_grad,
            shift_first_grad,
            gain_second_grad,
            shift_second_grad,
        ),
    )


def as_blocks(array, dim, peers):
    before, after = (array.shape[:dim], array.shape[dim + 1 :])
    split = array.reshape(*before, peers, array.shape[dim] // peers, *after)
    return jnp.moveaxis(split, dim, 0).reshape(peers, -1)


def from_blocks(flat, shape, dim, peers):
    block_shape = (*shape[:dim], shape[dim] // peers, *shape[dim + 1 :])
    return flat.reshape(block_shape)


def split_by_size(arrays):
    big = [i for i, a in enumerate(arrays) if a[0].size % 128 == 0]
    small = [i for i, a in enumerate(arrays) if a[0].size % 128 != 0]
    return (big, small)


def in_rows(blocks, big, small):
    count = blocks[0].shape[0]
    rest = jnp.concatenate([blocks[i].reshape(count, -1) for i in small], axis=1)
    spare = -rest.shape[1] % 2048
    rest = jnp.concatenate([rest, jnp.zeros((count, spare), rest.dtype)], axis=1)
    rows = [blocks[i].reshape(count, -1, 128) for i in big] + [rest.reshape(count, -1, 128)]
    return jnp.concatenate(rows, axis=1)


def out_of_rows(rows, shapes, big, small):
    count = rows.shape[0]
    parts, at = ({}, 0)
    for i in big:
        height = math.prod(shapes[i]) // 128
        parts[i] = rows[:, at : at + height].reshape(count, *shapes[i])
        at += height
    rest = rows[:, at:].reshape(count, -1)
    at = 0
    for i in small:
        width = math.prod(shapes[i])
        parts[i] = rest[:, at : at + width].reshape(count, *shapes[i])
        at += width
    return [parts[i] for i in range(len(shapes))]


def sum_at_end(grads_zero, grads_last, dims):
    peers = lax.axis_size("dp")
    blocks = [
        jnp.concatenate(
            [as_blocks(g0.astype(jnp.bfloat16), d, peers), as_blocks(g1.astype(jnp.bfloat16), d, peers)]
        )
        for g0, g1, d in zip(grads_zero, grads_last, dims)
    ]
    big, small = split_by_size(blocks)
    rows = in_rows(blocks, big, small)
    total = lax.psum_scatter(
        rows.reshape(-1, 128), ("section", "dp"), scatter_dimension=0, tiled=True
    )
    shapes = [block.shape[1:] for block in blocks]
    parts = out_of_rows(total[None], shapes, big, small)
    return tuple(
        from_blocks(part[0].astype(jnp.float32), g.shape, d, peers)[None]
        for part, g, d in zip(parts, grads_zero, dims)
    )


def unpack_layer(gathered_rows, weights, dims, big, small):
    parts = out_of_rows(gathered_rows, [w.shape for w in weights], big, small)
    gathered = []
    for part, d in zip(parts, dims):
        part = jnp.moveaxis(part, 0, d)
        shape = part.shape
        gathered.append(part.reshape(*shape[:d], shape[d] * shape[d + 1], *shape[d + 2 :]))
    return tuple(gathered)


def gather_all(weights, dims, is_first):
    big, small = split_by_size([w[None] for w in weights])
    own = in_rows([w[None] for w in weights], big, small)[0]
    other = lax.ppermute(own, "section", [(0, 1), (1, 0)])
    first_rows = lax.all_gather(jnp.where(is_first, own, other), "dp", axis=0, tiled=False)
    last_rows = lax.all_gather(jnp.where(is_first, other, own), "dp", axis=0, tiled=False)
    return (
        unpack_layer(first_rows, weights, dims, big, small),
        unpack_layer(last_rows, weights, dims, big, small),
    )


def shards(
    inputs,
    cotangent,
    packed_weight,
    bias_pair,
    output_weight,
    output_bias,
    expand_weight,
    expand_bias,
    contract_weight,
    contract_bias,
    gain_first,
    shift_first,
    gain_second,
    shift_second,
):
    dims = (0, 1, 1, 0, 0, 0, 1, 0, 0, 0, 0, 0)
    section_index = lax.axis_index("section")
    is_first = section_index == 0
    weights_zero, weights_last = gather_all(
        (
            packed_weight[0],
            bias_pair[0],
            output_weight[0],
            output_bias[0],
            expand_weight[0],
            expand_bias[0],
            contract_weight[0],
            contract_bias[0],
            gain_first[0],
            shift_first[0],
            gain_second[0],
            shift_second[0],
        ),
        dims,
        is_first,
    )
    stream = lax.dynamic_index_in_dim(inputs, section_index, axis=0, keepdims=False)
    out_grad = lax.dynamic_index_in_dim(cotangent, section_index, axis=0, keepdims=False)
    grad_rows = out_grad.reshape(-1, out_grad.shape[-1]).astype(jnp.bfloat16)
    middle, kept_zero, grad_full = layer_forward(stream, weights_zero, grad_rows)
    final, kept_last, _ = layer_forward(middle, weights_last)
    other_out = lax.ppermute(jnp.where(is_first, final, middle), "section", [(0, 1), (1, 0)])
    middle_grad, grads_last = layer_backward(out_grad, kept_last, weights_last, grad_full)
    other_middle_grad = lax.ppermute(middle_grad, "section", [(0, 1)])
    input_grad, grads_zero = layer_backward(middle_grad, kept_zero, weights_zero)
    other_input_grad = lax.ppermute(input_grad, "section", [(1, 0)])
    reduced = sum_at_end(grads_zero, grads_last, dims)
    section_outputs = jnp.where(
        is_first, jnp.stack([middle, other_out]), jnp.stack([other_out, final])
    )[None]
    section_grads = jnp.where(
        is_first,
        jnp.stack([input_grad, other_input_grad]),
        jnp.stack([other_middle_grad, middle_grad]),
    )[None]
    return (section_outputs, section_grads) + tuple(reduced)


def solution(mesh):
    in_specs = (
        P(None, "dp", None, "tensor"),
        P(None, "dp", None, "tensor"),
        P("section", "dp", None, "tensor"),
        P("section", None, ("tensor", "dp")),
        P("section", "tensor", "dp"),
        P("section", ("tensor", "dp")),
        P("section", "dp", "tensor"),
        P("section", ("tensor", "dp")),
        P("section", "tensor", "dp"),
        P("section", ("tensor", "dp")),
        P("section", ("tensor", "dp")),
        P("section", ("tensor", "dp")),
        P("section", ("tensor", "dp")),
        P("section", ("tensor", "dp")),
    )
    out_specs = (
        P("section", None, "dp", None, "tensor"),
        P("section", None, "dp", None, "tensor"),
        P("section", "dp", None, "tensor"),
        P("section", None, ("tensor", "dp")),
        P("section", "tensor", "dp"),
        P("section", ("tensor", "dp")),
        P("section", "dp", "tensor"),
        P("section", ("tensor", "dp")),
        P("section", "tensor", "dp"),
        P("section", ("tensor", "dp")),
        P("section", ("tensor", "dp")),
        P("section", ("tensor", "dp")),
        P("section", ("tensor", "dp")),
        P("section", ("tensor", "dp")),
    )
    return jax.shard_map(shards, mesh=mesh, in_specs=in_specs, out_specs=out_specs, check_vma=False)
```
